128 devices in a mesh: grp: 16 (over x, y), chan: 8 (over z, core).
Axes of the slice: x: 4, y: 4, z: 4, core: 2. Of those that a mesh axis runs over, the one named last changes fastest.
Arguments:
- spectra: bfloat16 [2048, 2, 2, 8192], P(('grp', 'chan')), may hold values from -45 to 45
- pair_blocks: int32 [16, 8, 18, 2], P('grp', 'chan'), may hold values from 0 to 63
- owners: int32 [16, 8, 18, 1], P('grp', 'chan'), may hold values from 0 to 15; in each aligned block of 18 rows (0 to 17, 18 to 35, ..., all dimensions but the last counted through in order) at most 3 rows name the same one
Outputs:
- stacks: float32 [16, 8, 48, 4, 1024], P('grp', 'chan')
The draws below stay inside these ranges and needn't reach their ends.
Inputs may be any that keep to these rules, and one draw needn't show every extreme that they name: `owners`: at most 3 of one device's 18 pair blocks name the same owner.
All inputs are finite; a program needn't handle non-finite values.
Results may differ from the reference program's by a relative error of at most 0.011.
Values may be sent and summed in bfloat16 or wider, within the bound.
A program may use at most 128 MiB of HBM per device.

```python
import math
import jax
import jax.numpy as jnp
import numpy as np
from jax import lax

F = 8192
LAGS = 1024
BLK = 2
NB_SRC = 18
MOST = 3
WINDOWS = 2
CHANNELS = 2048
GCH = 128
GBLK = 64
N_GRP = 16
N_CHAN = 8


def draw_spectra(key, part):
    keys = jax.random.split(key, 3)
    shape = (CHANNELS, WINDOWS, 2, F)
    base = jnp.clip(jax.random.normal(keys[0], shape, jnp.float32), -4.0, 4.0)
    rows = 10.0 ** jax.random.uniform(keys[1], (CHANNELS, WINDOWS, 1, 1), jnp.float32, -0.5, 0.5)
    spread = jnp.exp(jax.random.uniform(keys[2], (CHANNELS, WINDOWS, 1, F), jnp.float32, -1.0, 1.0))
    return (base * rows * spread).astype(jnp.bfloat16)


def set_ends(array, rng, least, largest):
    index_at = [jax.random.randint(jax.random.fold_in(rng, axis), (), 0, length) for axis, length in enumerate(array.shape)]
    widest = array.shape.index(max(array.shape))
    next_to = index_at[:widest] + [(index_at[widest] + 1) % array.shape[widest]] + index_at[widest + 1:]
    return array.at[tuple(index_at)].set(least).at[tuple(next_to)].set(largest)


def routed_block(key, own, number, rows, number_of, top, bound, slope):
    ranking = jax.random.permutation(key, number_of)
    crowded, usual = load_shares(number_of, rows * top, bound, slope, True), load_shares(number_of, rows * top, bound, slope, False)
    places = jnp.arange(number_of)

    def named(tallies, turn):
        used = int((tallies > 0).sum())
        fixed = max(1, used // 4)
        moved = fixed + (places - fixed + turn * (used - fixed)) % max(1, number_of - fixed)
        return jnp.zeros((number_of,), jnp.int32).at[ranking[jnp.where(places < fixed, places, moved)]].set(jnp.asarray(tallies, jnp.int32))

    tallies = jnp.where(number % 4 == 0, named(crowded, number // 4), named(usual, number - number // 4 - 1))
    mixed = jax.random.permutation(jax.random.fold_in(own, 3), number_of)
    giver, receiver = mixed[0:number_of // 2 * 2:2], mixed[1:number_of // 2 * 2:2]
    room = jnp.minimum(tallies[giver] - 1, bound - tallies[receiver]) // 2
    room = jnp.where((giver == ranking[0]) | (receiver == ranking[0]) | (tallies[receiver] == 0), 0, jnp.maximum(room, 0))
    moved = jax.random.randint(jax.random.fold_in(own, 4), (number_of // 2,), 0, 1 << 20) % (room + 1)
    tallies = tallies.at[giver].add(-moved).at[receiver].add(moved)
    labels = jnp.searchsorted(jnp.cumsum(tallies), jnp.arange(rows * top), side="right").astype(jnp.int32)
    table = labels.reshape(top, rows).T
    table = table[jax.random.permutation(jax.random.fold_in(own, 1), rows)]
    turn = jax.random.randint(jax.random.fold_in(own, 2), (rows, 1), 0, top)
    return jnp.take_along_axis(table, (jnp.arange(top)[None, :] + turn) % top, axis=1)


def load_shares(number_of, total, reach, lean, full):
    portions = [(1 << 20) // math.isqrt(standing ** lean) + 1 for standing in range(1, number_of + 1)]
    largest = reach if full else min(reach, max(-(-total // number_of), total * portions[0] // sum(portions)))
    least = 1 if total - largest >= number_of - 1 else 0
    holding, rest = [largest] + [least] * (number_of - 1), total - largest - least * (number_of - 1)
    while rest > 0:
        free = [i for i in range(1, number_of) if holding[i] < largest] or [i for i in range(1, number_of) if holding[i] < reach]
        pool, budget = sum([portions[i] for i in free]), rest
        for i in free:
            addition = min(reach - holding[i], max(1, budget * portions[i] // pool), rest)
            holding[i] = holding[i] + addition
            rest = rest - addition
    return np.array(holding)


def setup_inputs(seed: int = 0) -> dict:
    arg_keys = jax.random.split(jax.random.key(seed), 4)
    spectra = draw_spectra(jax.random.fold_in(arg_keys[3], 71), 0)
    pair_blocks = set_ends(jax.random.randint(arg_keys[1], (N_GRP, N_CHAN, NB_SRC, 2), 0, GBLK), jax.random.fold_in(arg_keys[1], 1), 0, GBLK - 1).astype(jnp.int32)
    owners_keys = jax.random.split(jax.random.fold_in(arg_keys[2], 1), N_GRP * N_CHAN * NB_SRC // NB_SRC)
    owners_turns = jax.random.permutation(jax.random.fold_in(arg_keys[2], 3), N_GRP * N_CHAN * NB_SRC // NB_SRC)
    owners = jax.vmap(lambda own, number: routed_block(jax.random.fold_in(arg_keys[2], 2), own, number, NB_SRC, N_GRP, 1, MOST, 2))(owners_keys, owners_turns).reshape((N_GRP, N_CHAN, NB_SRC, 1))
    return dict(spectra=spectra, pair_blocks=pair_blocks, owners=owners)


def lag_table(start, count):
    bins = start + jnp.arange(count, dtype=jnp.int32)
    lag_index = jnp.arange(LAGS, dtype=jnp.int32) - LAGS // 2
    phase = bins[:, None] * lag_index[None, :] % (2 * F)
    angle = phase.astype(jnp.float32) * (jnp.pi / F)
    weight = jnp.where(bins == 0, 1.0, 2.0).astype(jnp.float32) / jnp.sqrt(jnp.float32(F))
    cos_part = (jnp.cos(angle) * weight[:, None]).astype(jnp.bfloat16)
    sin_part = (-jnp.sin(angle) * weight[:, None]).astype(jnp.bfloat16)
    return (cos_part, sin_part)

def whiten(spectra):
    values = spectra.astype(jnp.float32)
    power = values[:, :, 0] ** 2 + values[:, :, 1] ** 2
    level = lax.optimization_barrier(jnp.mean(power, axis=-1, keepdims=True)) + 1e-05
    scale = lax.rsqrt(power + 0.1 * level)
    return (values * scale[:, :, None, :]).astype(jnp.bfloat16)

def cross_pairs(left, right):
    real_left = left[..., :, None, :, 0, :]
    imag_left = left[..., :, None, :, 1, :]
    real_right = right[..., None, :, :, 0, :]
    imag_right = right[..., None, :, :, 1, :]
    real_part = real_left * real_right + imag_left * imag_right
    imag_part = imag_left * real_right - real_left * imag_right
    both = jnp.stack([real_part, imag_part], axis=-2)
    return both.astype(jnp.bfloat16)

def order_ranks(owner_list):
    same = owner_list[..., :, None] == owner_list[..., None, :]
    count = owner_list.shape[-1]
    earlier = jnp.arange(count)[None, :] < jnp.arange(count)[:, None]
    return lax.optimization_barrier(jnp.sum(jnp.logical_and(same, earlier), axis=-1)).astype(jnp.int32)

def reference(spectra, pair_blocks, owners):
    white = whiten(spectra)
    cos_table, sin_table = lag_table(jnp.int32(0), F)
    groups = jnp.arange(N_GRP, dtype=jnp.int32)

    def one_group(group):
        panel = lax.dynamic_slice_in_dim(white, group * GCH, GCH, 0)
        blocks = pair_blocks[group]
        offsets = jnp.arange(BLK, dtype=jnp.int32)
        left_idx = (blocks[:, :, 0][:, :, None] * BLK + offsets).astype(jnp.int32)
        right_idx = (blocks[:, :, 1][:, :, None] * BLK + offsets).astype(jnp.int32)
        left = panel[left_idx].astype(jnp.float32)
        right = panel[right_idx].astype(jnp.float32)
        cross = cross_pairs(left, right)
        stacked = (lax.optimization_barrier(jnp.sum(cross.astype(jnp.float32), axis=-3)) / WINDOWS).astype(jnp.bfloat16)
        rows = stacked.reshape(-1, 2, F)
        corr = jnp.dot(rows[:, 0], cos_table, preferred_element_type=jnp.float32)
        corr = corr + jnp.dot(rows[:, 1], sin_table, preferred_element_type=jnp.float32)
        return corr.reshape(N_CHAN, NB_SRC, BLK * BLK, LAGS)
    values = lax.map(one_group, groups)
    owner_list = owners[..., 0].astype(jnp.int32)
    ranks = order_ranks(owner_list)
    slot_ids = (groups[:, None, None] * MOST + ranks).astype(jnp.int32)
    chan_ids = jnp.broadcast_to(jnp.arange(N_CHAN, dtype=jnp.int32)[None, :, None], owner_list.shape)
    stacks = jnp.zeros((N_GRP, N_CHAN, N_GRP * MOST, BLK * BLK, LAGS), jnp.float32)
    return stacks.at[owner_list, chan_ids, slot_ids].set(values)
```

```python
import jax
import jax.numpy as jnp
from jax import lax
from jax.sharding import PartitionSpec as P

F = 8192
LAGS = 1024
BLK = 2
NB_SRC = 18
MOST = 3
WINDOWS = 2
FINE = 128


def phase_angle(bins, lag_index):
    phase = bins[:, None] * lag_index[None, :] % (2 * F)
    return phase.astype(jnp.float32) * (jnp.pi / F)


def table_slice(start, count):
    lag_index = jnp.arange(LAGS, dtype=jnp.int32) - LAGS // 2
    coarse = phase_angle(start + FINE * jnp.arange(count // FINE, dtype=jnp.int32), lag_index)
    fine = phase_angle(jnp.arange(FINE, dtype=jnp.int32), lag_index)
    cos_a, sin_a = jnp.cos(coarse)[:, None, :], jnp.sin(coarse)[:, None, :]
    cos_b, sin_b = jnp.cos(fine)[None, :, :], jnp.sin(fine)[None, :, :]
    cos_ab = (cos_a * cos_b - sin_a * sin_b).reshape(count, LAGS)
    sin_ab = (sin_a * cos_b + cos_a * sin_b).reshape(count, LAGS)
    bins = start + jnp.arange(count, dtype=jnp.int32)
    weight = (jnp.where(bins == 0, 1.0, 2.0).astype(jnp.float32) / jnp.sqrt(jnp.float32(F)))[:, None]
    cos_part = (cos_ab * weight).astype(jnp.bfloat16)
    sin_part = (-sin_ab * weight).astype(jnp.bfloat16)
    return cos_part, sin_part


def whiten(spectra):
    values = spectra.astype(jnp.float32)
    power = values[:, :, 0] ** 2 + values[:, :, 1] ** 2
    level = jnp.mean(power, axis=-1, keepdims=True) + 1e-05
    scale = lax.rsqrt(power + 0.1 * level)
    return (values * scale[:, :, None, :]).astype(jnp.bfloat16)


def cross_pairs(left, right):
    real_left = left[..., :, None, :, 0, :]
    imag_left = left[..., :, None, :, 1, :]
    real_right = right[..., None, :, :, 0, :]
    imag_right = right[..., None, :, :, 1, :]
    real_part = real_left * real_right + imag_left * imag_right
    imag_part = imag_left * real_right - real_left * imag_right
    both = jnp.stack([real_part, imag_part], axis=-2)
    return both.astype(jnp.bfloat16)


def local(spectra, pair_blocks, owners):
    groups_count = lax.axis_size("grp")
    chan_count = lax.axis_size("chan")
    slot_count = groups_count * MOST
    pairs = BLK * BLK
    part = F // chan_count
    me = lax.axis_index("chan")

    white = whiten(spectra)
    channels = white.shape[0]
    chunks = white.reshape(channels, WINDOWS, 2, chan_count, part).transpose(3, 0, 1, 2, 4)
    panel = lax.all_to_all(chunks, "chan", split_axis=0, concat_axis=0, tiled=True)
    panel = panel.reshape(chan_count * channels, WINDOWS, 2, part)

    all_blocks = lax.all_gather(pair_blocks[0, 0], "chan", axis=0, tiled=False)
    all_blocks = all_blocks.reshape(chan_count * NB_SRC, 2)
    offsets = jnp.arange(BLK, dtype=jnp.int32)
    left_idx = all_blocks[:, 0][:, None] * BLK + offsets
    right_idx = all_blocks[:, 1][:, None] * BLK + offsets
    left = jnp.take(panel, left_idx, axis=0).astype(jnp.float32)
    right = jnp.take(panel, right_idx, axis=0).astype(jnp.float32)
    cross = cross_pairs(left, right)
    stacked = (jnp.sum(cross.astype(jnp.float32), axis=-3) / WINDOWS).astype(jnp.bfloat16)
    rows = stacked.reshape(-1, 2, part)

    cos_part, sin_part = table_slice(me * part, part)
    partial = jnp.dot(rows[:, 0], cos_part, preferred_element_type=jnp.float32)
    partial = partial + jnp.dot(rows[:, 1], sin_part, preferred_element_type=jnp.float32)
    partial = partial.reshape(chan_count, NB_SRC * pairs, LAGS)
    corr = lax.psum_scatter(partial, "chan", scatter_dimension=0, tiled=True)
    corr = corr.reshape(NB_SRC, pairs * LAGS)

    owner_list = owners[0, 0, :, 0]
    same = owner_list[:, None] == owner_list[None, :]
    earlier = jnp.arange(NB_SRC)[None, :] < jnp.arange(NB_SRC)[:, None]
    order_rank = jnp.sum(jnp.logical_and(same, earlier), axis=1)
    slot_ids = owner_list * MOST + order_rank
    chooser = slot_ids[None, :] == jnp.arange(slot_count, dtype=jnp.int32)[:, None]
    source = jnp.argmax(chooser, axis=1)
    filled = jnp.any(chooser, axis=1)
    placed = jnp.where(filled[:, None], jnp.take(corr, source, axis=0), 0.0)
    placed = placed.reshape(groups_count, MOST, pairs, LAGS)
    received = lax.all_to_all(placed, "grp", split_axis=0, concat_axis=0, tiled=True)
    return received.reshape(1, 1, slot_count, pairs, LAGS)


def solution(mesh):
    return jax.shard_map(
        local,
        mesh=mesh,
        in_specs=(
            P(("grp", "chan"), None, None, None),
            P("grp", "chan", None, None),
            P("grp", "chan", None, None),
        ),
        out_specs=P("grp", "chan", None, None, None),
        check_vma=False,
    )
```

```python
import jax
import jax.numpy as jnp
from jax import lax
from jax.experimental import pallas as pl
from jax.experimental.pallas import tpu as pltpu
from jax.sharding import PartitionSpec as P

F = 8192
LAGS = 1024
BLK = 2
NB_SRC = 18
MOST = 3
WINDOWS = 2
FINE = 128


def phase_angle(bins, lag_index):
    phase = bins[:, None] * lag_index[None, :] % (2 * F)
    return phase.astype(jnp.float32) * (jnp.pi / F)


def table_slice(start, count):
    lag_index = jnp.arange(LAGS, dtype=jnp.int32) - LAGS // 2
    coarse = phase_angle(start + FINE * jnp.arange(count // FINE, dtype=jnp.int32), lag_index)
    fine = phase_angle(jnp.arange(FINE, dtype=jnp.int32), lag_index)
    cos_a, sin_a = jnp.cos(coarse)[:, None, :], jnp.sin(coarse)[:, None, :]
    cos_b, sin_b = jnp.cos(fine)[None, :, :], jnp.sin(fine)[None, :, :]
    cos_ab = (cos_a * cos_b - sin_a * sin_b).reshape(count, LAGS)
    sin_ab = (sin_a * cos_b + cos_a * sin_b).reshape(count, LAGS)
    bins = start + jnp.arange(count, dtype=jnp.int32)
    weight = (jnp.where(bins == 0, 1.0, 2.0).astype(jnp.float32) / jnp.sqrt(jnp.float32(F)))[:, None]
    cos_part = (cos_ab * weight).astype(jnp.bfloat16)
    sin_part = (-sin_ab * weight).astype(jnp.bfloat16)
    return cos_part, sin_part


def whiten(spectra):
    values = spectra.astype(jnp.float32)
    power = values[:, :, 0] ** 2 + values[:, :, 1] ** 2
    level = jnp.mean(power, axis=-1, keepdims=True) + 1e-05
    scale = lax.rsqrt(power + 0.1 * level)
    return (values * scale[:, :, None, :]).astype(jnp.bfloat16)


def pair_kernel(left_hot, right_hot, panel, cos_ref, sin_ref, out_ref, left_rows, right_rows):
    part = cos_ref.shape[0]
    kinds = BLK * WINDOWS * 2
    for kind in range(kinds):
        cols = panel[:, kind * part:(kind + 1) * part]
        left_rows[kind] = jnp.dot(left_hot[...], cols, preferred_element_type=jnp.float32)
        right_rows[kind] = jnp.dot(right_hot[...], cols, preferred_element_type=jnp.float32)

    def one_pair(pq, carry):
        p = pq // BLK
        q = pq % BLK
        real_sum = None
        imag_sum = None
        for window in range(WINDOWS):
            ra = left_rows[(p * WINDOWS + window) * 2]
            ia = left_rows[(p * WINDOWS + window) * 2 + 1]
            rb = right_rows[(q * WINDOWS + window) * 2]
            ib = right_rows[(q * WINDOWS + window) * 2 + 1]
            real = (ra * rb + ia * ib).astype(jnp.bfloat16).astype(jnp.float32)
            imag = (ia * rb - ra * ib).astype(jnp.bfloat16).astype(jnp.float32)
            real_sum = real if real_sum is None else real_sum + real
            imag_sum = imag if imag_sum is None else imag_sum + imag
        real_stack = (real_sum / WINDOWS).astype(jnp.bfloat16)
        imag_stack = (imag_sum / WINDOWS).astype(jnp.bfloat16)
        total = jnp.dot(real_stack, cos_ref[...], preferred_element_type=jnp.float32)
        total = total + jnp.dot(imag_stack, sin_ref[...], preferred_element_type=jnp.float32)
        listed = out_ref.shape[2]
        for chan in range(out_ref.shape[0]):
            out_ref[chan, pq] = total[chan * listed:(chan + 1) * listed]
        return carry

    lax.fori_loop(0, BLK * BLK, one_pair, 0)


def pair_correlations(left_hot, right_hot, panel, cos_part, sin_part, chan_count):
    count = left_hot.shape[0]
    part = cos_part.shape[0]
    kinds = BLK * WINDOWS * 2
    vmem = pl.BlockSpec(memory_space=pltpu.VMEM)
    flops = 2 * count * panel.shape[0] * panel.shape[1] * 2 + 2 * 2 * BLK * BLK * count * part * LAGS
    return pl.pallas_call(
        pair_kernel,
        out_shape=jax.ShapeDtypeStruct((chan_count, BLK * BLK, count // chan_count, LAGS), jnp.float32),
        in_specs=[vmem] * 5,
        out_specs=vmem,
        scratch_shapes=[
            pltpu.VMEM((kinds, count, part), jnp.float32),
            pltpu.VMEM((kinds, count, part), jnp.float32),
        ],
        compiler_params=pltpu.CompilerParams(vmem_limit_bytes=56 * 1024 * 1024),
        cost_estimate=pl.CostEstimate(
            flops=flops,
            transcendentals=0,
            bytes_accessed=panel.size * 2 + 4 * part * LAGS + BLK * BLK * count * LAGS * 4,
        ),
    )(left_hot, right_hot, panel, cos_part, sin_part)


def local(spectra, pair_blocks, owners):
    groups_count = lax.axis_size("grp")
    chan_count = lax.axis_size("chan")
    slot_count = groups_count * MOST
    pairs = BLK * BLK
    part = F // chan_count
    me = lax.axis_index("chan")

    white = whiten(spectra)
    channels = white.shape[0]
    chunks = white.reshape(channels, WINDOWS, 2, chan_count, part).transpose(3, 0, 1, 2, 4)
    chunks = chunks.reshape(chan_count, channels * WINDOWS * 2, part)
    listed = pair_blocks[0, 0].reshape(-1).astype(jnp.bfloat16)
    extra = jnp.zeros((part,), jnp.bfloat16).at[: listed.shape[0]].set(listed)
    extra = jnp.broadcast_to(extra[None, None, :], (chan_count, 1, part))
    sent = jnp.concatenate([chunks, extra], axis=1)
    got = lax.all_to_all(sent, "chan", split_axis=0, concat_axis=0, tiled=True)
    rows_per = channels * WINDOWS * 2
    blocks_count = chan_count * channels // BLK
    panel = got[:, :rows_per].reshape(blocks_count, BLK * WINDOWS * 2 * part)
    all_blocks = got[:, rows_per, : NB_SRC * 2].astype(jnp.float32).astype(jnp.int32)
    all_blocks = all_blocks.reshape(chan_count * NB_SRC, 2)
    block_ids = jnp.arange(blocks_count, dtype=jnp.int32)[None, :]
    left_hot = (all_blocks[:, 0][:, None] == block_ids).astype(jnp.bfloat16)
    right_hot = (all_blocks[:, 1][:, None] == block_ids).astype(jnp.bfloat16)

    cos_part, sin_part = table_slice(me * part, part)
    partial = pair_correlations(left_hot, right_hot, panel, cos_part, sin_part, chan_count)
    partial = partial.reshape(chan_count, pairs * NB_SRC, LAGS)
    corr = lax.psum_scatter(partial, "chan", scatter_dimension=0, tiled=True)
    corr = corr.reshape(pairs, NB_SRC, LAGS).transpose(1, 0, 2).reshape(NB_SRC, pairs * LAGS)

    owner_list = owners[0, 0, :, 0]
    same = owner_list[:, None] == owner_list[None, :]
    earlier = jnp.arange(NB_SRC)[None, :] < jnp.arange(NB_SRC)[:, None]
    order_rank = jnp.sum(jnp.logical_and(same, earlier), axis=1)
    slot_ids = owner_list * MOST + order_rank
    chooser = slot_ids[None, :] == jnp.arange(slot_count, dtype=jnp.int32)[:, None]
    source = jnp.argmax(chooser, axis=1)
    filled = jnp.any(chooser, axis=1)
    placed = jnp.where(filled[:, None], jnp.take(corr, source, axis=0), 0.0)
    placed = placed.reshape(groups_count, MOST, pairs, LAGS)
    received = lax.all_to_all(placed, "grp", split_axis=0, concat_axis=0, tiled=True)
    return received.reshape(1, 1, slot_count, pairs, LAGS)


def solution(mesh):
    return jax.shard_map(
        local,
        mesh=mesh,
        in_specs=(
            P(("grp", "chan"), None, None, None),
            P("grp", "chan", None, None),
            P("grp", "chan", None, None),
        ),
        out_specs=P("grp", "chan", None, None, None),
        check_vma=False,
    )
```

```python
import jax
import jax.numpy as jnp
from jax import lax
from jax.experimental import pallas as pl
from jax.experimental.pallas import tpu as pltpu
from jax.sharding import PartitionSpec as P

F = 8192
LAGS = 1024
BLK = 2
NB_SRC = 18
MOST = 3
WINDOWS = 2
FINE = 128
ROW_CHUNK = 144


def phase_angle(bins, lag_index):
    phase = bins[:, None] * lag_index[None, :] % (2 * F)
    return phase.astype(jnp.float32) * (jnp.pi / F)


def table_slice(start, count):
    lag_index = jnp.arange(LAGS, dtype=jnp.int32) - LAGS // 2
    coarse = phase_angle(start + FINE * jnp.arange(count // FINE, dtype=jnp.int32), lag_index)
    fine = phase_angle(jnp.arange(FINE, dtype=jnp.int32), lag_index)
    cos_a, sin_a = jnp.cos(coarse)[:, None, :], jnp.sin(coarse)[:, None, :]
    cos_b, sin_b = jnp.cos(fine)[None, :, :], jnp.sin(fine)[None, :, :]
    cos_ab = (cos_a * cos_b - sin_a * sin_b).reshape(count, LAGS)
    sin_ab = (sin_a * cos_b + cos_a * sin_b).reshape(count, LAGS)
    bins = start + jnp.arange(count, dtype=jnp.int32)
    weight = (jnp.where(bins == 0, 1.0, 2.0).astype(jnp.float32) / jnp.sqrt(jnp.float32(F)))[:, None]
    cos_part = (cos_ab * weight).astype(jnp.bfloat16)
    sin_part = (-sin_ab * weight).astype(jnp.bfloat16)
    return cos_part, sin_part


def whiten(spectra):
    values = spectra.astype(jnp.float32)
    power = values[:, :, 0] ** 2 + values[:, :, 1] ** 2
    level = jnp.mean(power, axis=-1, keepdims=True) + 1e-05
    scale = lax.rsqrt(power + 0.1 * level)
    return (values * scale[:, :, None, :]).astype(jnp.bfloat16)


def pair_kernel(left_hot, right_hot, panel, cos_ref, sin_ref, out_ref):
    part = cos_ref.shape[0]
    chunk = ROW_CHUNK

    def rows_of(hot, window, kind):
        col = (window * 2 + kind) * part
        return jnp.dot(hot, panel[:, col:col + part], preferred_element_type=jnp.float32)

    def one_chunk(step, carry):
        at = pl.multiple_of(step * chunk, chunk)
        left = left_hot[pl.ds(at, chunk), :]
        right = right_hot[pl.ds(at, chunk), :]
        real_sum = None
        imag_sum = None
        for window in range(WINDOWS):
            ra = rows_of(left, window, 0)
            ia = rows_of(left, window, 1)
            rb = rows_of(right, window, 0)
            ib = rows_of(right, window, 1)
            real = (ra * rb + ia * ib).astype(jnp.bfloat16).astype(jnp.float32)
            imag = (ia * rb - ra * ib).astype(jnp.bfloat16).astype(jnp.float32)
            real_sum = real if real_sum is None else real_sum + real
            imag_sum = imag if imag_sum is None else imag_sum + imag
        real_stack = (real_sum / WINDOWS).astype(jnp.bfloat16)
        imag_stack = (imag_sum / WINDOWS).astype(jnp.bfloat16)
        total = jnp.dot(real_stack, cos_ref[...], preferred_element_type=jnp.float32)
        total = total + jnp.dot(imag_stack, sin_ref[...], preferred_element_type=jnp.float32)
        out_ref[pl.ds(at, chunk), :] = total.astype(out_ref.dtype)
        return carry

    lax.fori_loop(0, out_ref.shape[0] // chunk, one_chunk, 0)


def pair_correlations(left_hot, right_hot, panel, cos_part, sin_part):
    rows = left_hot.shape[0]
    part = cos_part.shape[0]
    vmem = pl.BlockSpec(memory_space=pltpu.VMEM)
    flops = 2 * 2 * rows * panel.shape[0] * panel.shape[1] + 2 * 2 * rows * part * LAGS
    return pl.pallas_call(
        pair_kernel,
        out_shape=jax.ShapeDtypeStruct((rows, LAGS), jnp.bfloat16),
        in_specs=[vmem] * 5,
        out_specs=vmem,
        compiler_params=pltpu.CompilerParams(vmem_limit_bytes=56 * 1024 * 1024),
        cost_estimate=pl.CostEstimate(
            flops=flops,
            transcendentals=0,
            bytes_accessed=panel.size * 2 + 4 * part * LAGS + rows * LAGS * 2,
        ),
    )(left_hot, right_hot, panel, cos_part, sin_part)


def local(spectra, pair_blocks, owners):
    groups_count = lax.axis_size("grp")
    chan_count = lax.axis_size("chan")
    slot_count = groups_count * MOST
    pairs = BLK * BLK
    part = F // chan_count
    me = lax.axis_index("chan")

    white = whiten(spectra)
    channels = white.shape[0]
    chunks = white.reshape(channels, WINDOWS, 2, chan_count, part).transpose(3, 0, 1, 2, 4)
    chunks = chunks.reshape(chan_count, channels * WINDOWS * 2, part)
    listed = pair_blocks[0, 0].reshape(-1).astype(jnp.bfloat16)
    extra = jnp.zeros((part,), jnp.bfloat16).at[: listed.shape[0]].set(listed)
    extra = jnp.broadcast_to(extra[None, None, :], (chan_count, 1, part))
    sent = jnp.concatenate([chunks, extra], axis=1)
    got = lax.all_to_all(sent, "chan", split_axis=0, concat_axis=0, tiled=True)
    rows_per = channels * WINDOWS * 2
    group_channels = chan_count * channels
    panel = got[:, :rows_per].reshape(group_channels, WINDOWS * 2 * part)
    all_blocks = got[:, rows_per, : NB_SRC * 2].astype(jnp.float32).astype(jnp.int32)
    all_blocks = all_blocks.reshape(chan_count * NB_SRC, 1, 2)
    offsets = jnp.arange(BLK, dtype=jnp.int32)
    left_ch = (all_blocks[:, :, 0] * BLK + offsets[None, :])[:, :, None] + jnp.zeros((1, 1, BLK), jnp.int32)
    right_ch = (all_blocks[:, :, 1] * BLK + offsets[None, :])[:, None, :] + jnp.zeros((1, BLK, 1), jnp.int32)
    channel_ids = jnp.arange(group_channels, dtype=jnp.int32)[None, :]
    left_hot = (left_ch.reshape(-1, 1) == channel_ids).astype(jnp.bfloat16)
    right_hot = (right_ch.reshape(-1, 1) == channel_ids).astype(jnp.bfloat16)

    cos_part, sin_part = table_slice(me * part, part)
    partial = pair_correlations(left_hot, right_hot, panel, cos_part, sin_part)
    partial = partial.reshape(chan_count, NB_SRC * pairs, LAGS)
    corr = lax.psum_scatter(partial, "chan", scatter_dimension=0, tiled=True)
    corr = corr.reshape(NB_SRC, pairs * LAGS).astype(jnp.float32)

    owner_list = owners[0, 0, :, 0]
    same = owner_list[:, None] == owner_list[None, :]
    earlier = jnp.arange(NB_SRC)[None, :] < jnp.arange(NB_SRC)[:, None]
    order_rank = jnp.sum(jnp.logical_and(same, earlier), axis=1)
    slot_ids = owner_list * MOST + order_rank
    chooser = slot_ids[None, :] == jnp.arange(slot_count, dtype=jnp.int32)[:, None]
    source = jnp.argmax(chooser, axis=1)
    filled = jnp.any(chooser, axis=1)
    placed = jnp.where(filled[:, None], jnp.take(corr, source, axis=0), 0.0)
    placed = placed.reshape(groups_count, MOST, pairs, LAGS)
    received = lax.all_to_all(placed, "grp", split_axis=0, concat_axis=0, tiled=True)
    return received.reshape(1, 1, slot_count, pairs, LAGS)


def solution(mesh):
    return jax.shard_map(
        local,
        mesh=mesh,
        in_specs=(
            P(("grp", "chan"), None, None, None),
            P("grp", "chan", None, None),
            P("grp", "chan", None, None),
        ),
        out_specs=P("grp", "chan", None, None, None),
        check_vma=False,
    )
```

```python
import functools

import jax
import jax.numpy as jnp
from jax import lax
from jax.experimental import pallas as pl
from jax.experimental.pallas import tpu as pltpu
from jax.sharding import PartitionSpec as P

F = 8192
LAGS = 1024
BLK = 2
NB_SRC = 18
MOST = 3
WINDOWS = 2
FINE = 128
ROW_CHUNK = 144


def phase_angle(bins, lag_index):
    phase = bins[:, None] * lag_index[None, :] % (2 * F)
    return phase.astype(jnp.float32) * (jnp.pi / F)


def table_slice(start, count):
    lag_index = jnp.arange(LAGS, dtype=jnp.int32) - LAGS // 2
    coarse = phase_angle(start + FINE * jnp.arange(count // FINE, dtype=jnp.int32), lag_index)
    fine = phase_angle(jnp.arange(FINE, dtype=jnp.int32), lag_index)
    cos_a, sin_a = jnp.cos(coarse)[:, None, :], jnp.sin(coarse)[:, None, :]
    cos_b, sin_b = jnp.cos(fine)[None, :, :], jnp.sin(fine)[None, :, :]
    cos_ab = (cos_a * cos_b - sin_a * sin_b).reshape(count, LAGS)
    sin_ab = (sin_a * cos_b + cos_a * sin_b).reshape(count, LAGS)
    bins = start + jnp.arange(count, dtype=jnp.int32)
    weight = (jnp.where(bins == 0, 1.0, 2.0).astype(jnp.float32) / jnp.sqrt(jnp.float32(F)))[:, None]
    cos_part = (cos_ab * weight).astype(jnp.bfloat16)
    sin_part = (-sin_ab * weight).astype(jnp.bfloat16)
    return cos_part, sin_part


def whiten(spectra):
    values = spectra.astype(jnp.float32)
    power = values[:, :, 0] ** 2 + values[:, :, 1] ** 2
    level = jnp.mean(power, axis=-1, keepdims=True) + 1e-05
    scale = lax.rsqrt(power + 0.1 * level)
    return (values * scale[:, :, None, :]).astype(jnp.bfloat16)


def pair_kernel(left_hot, right_hot, panel, cos_ref, sin_ref, out_ref):
    part = cos_ref.shape[0]
    chunk = ROW_CHUNK

    def rows_of(hot, window, kind):
        col = (window * 2 + kind) * part
        return jnp.dot(hot, panel[:, col:col + part], preferred_element_type=jnp.float32)

    def one_chunk(step, carry):
        at = pl.multiple_of(step * chunk, chunk)
        left = left_hot[pl.ds(at, chunk), :]
        right = right_hot[pl.ds(at, chunk), :]
        real_sum = None
        imag_sum = None
        for window in range(WINDOWS):
            ra = rows_of(left, window, 0)
            ia = rows_of(left, window, 1)
            rb = rows_of(right, window, 0)
            ib = rows_of(right, window, 1)
            real = (ra * rb + ia * ib).astype(jnp.bfloat16).astype(jnp.float32)
            imag = (ia * rb - ra * ib).astype(jnp.bfloat16).astype(jnp.float32)
            real_sum = real if real_sum is None else real_sum + real
            imag_sum = imag if imag_sum is None else imag_sum + imag
        real_stack = (real_sum / WINDOWS).astype(jnp.bfloat16)
        imag_stack = (imag_sum / WINDOWS).astype(jnp.bfloat16)
        total = jnp.dot(real_stack, cos_ref[...], preferred_element_type=jnp.float32)
        total = total + jnp.dot(imag_stack, sin_ref[...], preferred_element_type=jnp.float32)
        out_ref[pl.ds(at, chunk), :] = total.astype(out_ref.dtype)
        return carry

    lax.fori_loop(0, out_ref.shape[0] // chunk, one_chunk, 0)


def pair_correlations(left_hot, right_hot, panel, cos_part, sin_part):
    rows = left_hot.shape[0]
    part = cos_part.shape[0]
    vmem = pl.BlockSpec(memory_space=pltpu.VMEM)
    flops = 2 * 2 * rows * panel.shape[0] * panel.shape[1] + 2 * 2 * rows * part * LAGS
    return pl.pallas_call(
        pair_kernel,
        out_shape=jax.ShapeDtypeStruct((rows, LAGS), jnp.float32),
        in_specs=[vmem] * 5,
        out_specs=vmem,
        compiler_params=pltpu.CompilerParams(vmem_limit_bytes=56 * 1024 * 1024),
        cost_estimate=pl.CostEstimate(
            flops=flops,
            transcendentals=0,
            bytes_accessed=panel.size * 2 + 4 * part * LAGS + rows * LAGS * 4,
        ),
    )(left_hot, right_hot, panel, cos_part, sin_part)


def exchange_kernel(axis, other_axis, axis_first, collective, x_ref, out_ref, local_sem, send_sem, recv_sem):
    n = x_ref.shape[0]
    me = lax.axis_index(axis)
    other = lax.axis_index(other_axis)

    def device(j):
        return (j, other) if axis_first else (other, j)

    barrier = pltpu.get_barrier_semaphore()
    for step in range(1, n):
        pl.semaphore_signal(barrier, inc=1, device_id=device(lax.rem(me + step, n)),
                            device_id_type=pl.DeviceIdType.MESH)
    pl.semaphore_wait(barrier, n - 1)

    own = pltpu.make_async_copy(x_ref.at[me], out_ref.at[me], local_sem)
    own.start()
    copies = []
    for step in range(1, n):
        target = lax.rem(me + step, n)
        copy = pltpu.make_async_remote_copy(
            src_ref=x_ref.at[target],
            dst_ref=out_ref.at[me],
            send_sem=send_sem.at[step],
            recv_sem=recv_sem.at[step],
            device_id=device(target),
            device_id_type=pl.DeviceIdType.MESH,
        )
        copy.start()
        copies.append(copy)
    own.wait()
    for step in range(1, n):
        source = lax.rem(me + n - step, n)
        copies[step - 1].wait_send()
        incoming = pltpu.make_async_remote_copy(
            src_ref=x_ref.at[source],
            dst_ref=out_ref.at[source],
            send_sem=send_sem.at[step],
            recv_sem=recv_sem.at[step],
            device_id=device(source),
            device_id_type=pl.DeviceIdType.MESH,
        )
        incoming.wait_recv()


def exchange(x, axis, other_axis, axis_first, collective):
    n = x.shape[0]
    anywhere = pl.BlockSpec(memory_space=pl.ANY)
    return pl.pallas_call(
        functools.partial(exchange_kernel, axis, other_axis, axis_first, collective),
        out_shape=jax.ShapeDtypeStruct(x.shape, x.dtype),
        in_specs=[anywhere],
        out_specs=anywhere,
        scratch_shapes=[
            pltpu.SemaphoreType.DMA(()),
            pltpu.SemaphoreType.DMA((n,)),
            pltpu.SemaphoreType.DMA((n,)),
        ],
        compiler_params=pltpu.CompilerParams(collective_id=collective, has_side_effects=True),
    )(x)


def local(spectra, pair_blocks, owners):
    groups_count = lax.axis_size("grp")
    chan_count = lax.axis_size("chan")
    slot_count = groups_count * MOST
    pairs = BLK * BLK
    part = F // chan_count
    me = lax.axis_index("chan")

    white = whiten(spectra)
    channels = white.shape[0]
    chunks = white.reshape(channels, WINDOWS, 2, chan_count, part).transpose(3, 0, 1, 2, 4)
    chunks = chunks.reshape(chan_count, channels * WINDOWS * 2, part)
    listed = pair_blocks[0, 0].reshape(-1).astype(jnp.bfloat16)
    extra = jnp.zeros((part,), jnp.bfloat16).at[: listed.shape[0]].set(listed)
    extra = jnp.broadcast_to(extra[None, None, :], (chan_count, 1, part))
    sent = jnp.concatenate([chunks, extra], axis=1)
    got = lax.all_to_all(sent, "chan", split_axis=0, concat_axis=0, tiled=True)
    rows_per = channels * WINDOWS * 2
    group_channels = chan_count * channels
    panel = got[:, :rows_per].reshape(group_channels, WINDOWS * 2 * part)
    all_blocks = got[:, rows_per, : NB_SRC * 2].astype(jnp.float32).astype(jnp.int32)
    all_blocks = all_blocks.reshape(chan_count * NB_SRC, 1, 2)
    offsets = jnp.arange(BLK, dtype=jnp.int32)
    left_ch = (all_blocks[:, :, 0] * BLK + offsets[None, :])[:, :, None] + jnp.zeros((1, 1, BLK), jnp.int32)
    right_ch = (all_blocks[:, :, 1] * BLK + offsets[None, :])[:, None, :] + jnp.zeros((1, BLK, 1), jnp.int32)
    channel_ids = jnp.arange(group_channels, dtype=jnp.int32)[None, :]
    left_hot = (left_ch.reshape(-1, 1) == channel_ids).astype(jnp.bfloat16)
    right_hot = (right_ch.reshape(-1, 1) == channel_ids).astype(jnp.bfloat16)

    cos_part, sin_part = table_slice(me * part, part)
    partial = pair_correlations(left_hot, right_hot, panel, cos_part, sin_part)
    partial = partial.reshape(chan_count, NB_SRC * pairs, LAGS)
    gathered = exchange(partial, "chan", "grp", False, 0)
    corr = jnp.sum(gathered, axis=0).reshape(NB_SRC, pairs * LAGS)

    owner_list = owners[0, 0, :, 0]
    same = owner_list[:, None] == owner_list[None, :]
    earlier = jnp.arange(NB_SRC)[None, :] < jnp.arange(NB_SRC)[:, None]
    order_rank = jnp.sum(jnp.logical_and(same, earlier), axis=1)
    slot_ids = owner_list * MOST + order_rank
    chooser = slot_ids[None, :] == jnp.arange(slot_count, dtype=jnp.int32)[:, None]
    source = jnp.argmax(chooser, axis=1)
    filled = jnp.any(chooser, axis=1)
    placed = jnp.where(filled[:, None], jnp.take(corr, source, axis=0), 0.0)
    placed = placed.reshape(groups_count, MOST, pairs, LAGS)
    received = exchange(placed, "grp", "chan", True, 1)
    return received.reshape(1, 1, slot_count, pairs, LAGS)


def solution(mesh):
    return jax.shard_map(
        local,
        mesh=mesh,
        in_specs=(
            P(("grp", "chan"), None, None, None),
            P("grp", "chan", None, None),
            P("grp", "chan", None, None),
        ),
        out_specs=P("grp", "chan", None, None, None),
        check_vma=False,
    )
```

```python
import functools

import jax
import jax.numpy as jnp
from jax import lax
from jax.experimental import pallas as pl
from jax.experimental.pallas import tpu as pltpu
from jax.sharding import PartitionSpec as P

F = 8192
LAGS = 1024
BLK = 2
NB_SRC = 18
MOST = 3
WINDOWS = 2
FINE = 128
ROW_CHUNK = 144
CORES = 2


def phase_angle(bins, lag_index):
    phase = bins[:, None] * lag_index[None, :] % (2 * F)
    return phase.astype(jnp.float32) * (jnp.pi / F)


def table_slice(start, count):
    lag_index = jnp.arange(LAGS, dtype=jnp.int32) - LAGS // 2
    coarse = phase_angle(start + FINE * jnp.arange(count // FINE, dtype=jnp.int32), lag_index)
    fine = phase_angle(jnp.arange(FINE, dtype=jnp.int32), lag_index)
    cos_a, sin_a = jnp.cos(coarse)[:, None, :], jnp.sin(coarse)[:, None, :]
    cos_b, sin_b = jnp.cos(fine)[None, :, :], jnp.sin(fine)[None, :, :]
    cos_ab = (cos_a * cos_b - sin_a * sin_b).reshape(count, LAGS)
    sin_ab = (sin_a * cos_b + cos_a * sin_b).reshape(count, LAGS)
    bins = start + jnp.arange(count, dtype=jnp.int32)
    weight = (jnp.where(bins == 0, 1.0, 2.0).astype(jnp.float32) / jnp.sqrt(jnp.float32(F)))[:, None]
    cos_part = (cos_ab * weight).astype(jnp.bfloat16)
    sin_part = (-sin_ab * weight).astype(jnp.bfloat16)
    return cos_part, sin_part


def whiten(spectra):
    values = spectra.astype(jnp.float32)
    power = values[:, :, 0] ** 2 + values[:, :, 1] ** 2
    level = jnp.mean(power, axis=-1, keepdims=True) + 1e-05
    scale = lax.rsqrt(power + 0.1 * level)
    return (values * scale[:, :, None, :]).astype(jnp.bfloat16)


def pair_kernel(left_hot, right_hot, panel, cos_ref, sin_ref, out_ref):
    part = cos_ref.shape[0]
    chunk = ROW_CHUNK

    def rows_of(hot, window, kind):
        col = (window * 2 + kind) * part
        return jnp.dot(hot, panel[:, col:col + part], preferred_element_type=jnp.float32)

    def one_chunk(step, carry):
        at = pl.multiple_of(step * chunk, chunk)
        left = left_hot[pl.ds(at, chunk), :]
        right = right_hot[pl.ds(at, chunk), :]
        real_sum = None
        imag_sum = None
        for window in range(WINDOWS):
            ra = rows_of(left, window, 0)
            ia = rows_of(left, window, 1)
            rb = rows_of(right, window, 0)
            ib = rows_of(right, window, 1)
            real = (ra * rb + ia * ib).astype(jnp.bfloat16).astype(jnp.float32)
            imag = (ia * rb - ra * ib).astype(jnp.bfloat16).astype(jnp.float32)
            real_sum = real if real_sum is None else real_sum + real
            imag_sum = imag if imag_sum is None else imag_sum + imag
        real_stack = (real_sum / WINDOWS).astype(jnp.bfloat16)
        imag_stack = (imag_sum / WINDOWS).astype(jnp.bfloat16)
        total = jnp.dot(real_stack, cos_ref[...], preferred_element_type=jnp.float32)
        total = total + jnp.dot(imag_stack, sin_ref[...], preferred_element_type=jnp.float32)
        out_ref[pl.ds(at, chunk), :] = total.astype(out_ref.dtype)
        return carry

    lax.fori_loop(0, out_ref.shape[0] // chunk, one_chunk, 0)


def pair_correlations(left_hot, right_hot, panel, cos_part, sin_part):
    rows = left_hot.shape[0]
    part = cos_part.shape[0]
    vmem = pl.BlockSpec(memory_space=pltpu.VMEM)
    flops = 2 * 2 * rows * panel.shape[0] * panel.shape[1] + 2 * 2 * rows * part * LAGS
    return pl.pallas_call(
        pair_kernel,
        out_shape=jax.ShapeDtypeStruct((rows, LAGS), jnp.float32),
        in_specs=[vmem] * 5,
        out_specs=vmem,
        compiler_params=pltpu.CompilerParams(vmem_limit_bytes=56 * 1024 * 1024),
        cost_estimate=pl.CostEstimate(
            flops=flops,
            transcendentals=0,
            bytes_accessed=panel.size * 2 + 4 * part * LAGS + rows * LAGS * 4,
        ),
    )(left_hot, right_hot, panel, cos_part, sin_part)


def exchange_kernel(axis, other_axis, axis_first, stride, x_ref, out_ref, local_sem, send_sem, recv_sem):
    n = x_ref.shape[0]
    index = lax.axis_index(axis)
    me = lax.rem(index // stride, n)
    base = index - me * stride
    other = lax.axis_index(other_axis)

    def device(j):
        coord = base + stride * j
        return (coord, other) if axis_first else (other, coord)

    barrier = pltpu.get_barrier_semaphore()
    for step in range(1, n):
        pl.semaphore_signal(barrier, inc=1, device_id=device(lax.rem(me + step, n)),
                            device_id_type=pl.DeviceIdType.MESH)
    pl.semaphore_wait(barrier, n - 1)

    own = pltpu.make_async_copy(x_ref.at[me], out_ref.at[me], local_sem)
    own.start()
    copies = []
    for step in range(1, n):
        target = lax.rem(me + step, n)
        copy = pltpu.make_async_remote_copy(
            src_ref=x_ref.at[target],
            dst_ref=out_ref.at[me],
            send_sem=send_sem.at[step],
            recv_sem=recv_sem.at[step],
            device_id=device(target),
            device_id_type=pl.DeviceIdType.MESH,
        )
        copy.start()
        copies.append(copy)
    own.wait()
    for step in range(1, n):
        source = lax.rem(me + n - step, n)
        copies[step - 1].wait_send()
        incoming = pltpu.make_async_remote_copy(
            src_ref=x_ref.at[source],
            dst_ref=out_ref.at[source],
            send_sem=send_sem.at[step],
            recv_sem=recv_sem.at[step],
            device_id=device(source),
            device_id_type=pl.DeviceIdType.MESH,
        )
        incoming.wait_recv()


def exchange(x, axis, other_axis, axis_first, stride, collective):
    n = x.shape[0]
    anywhere = pl.BlockSpec(memory_space=pl.ANY)
    return pl.pallas_call(
        functools.partial(exchange_kernel, axis, other_axis, axis_first, stride),
        out_shape=jax.ShapeDtypeStruct(x.shape, x.dtype),
        in_specs=[anywhere],
        out_specs=anywhere,
        scratch_shapes=[
            pltpu.SemaphoreType.DMA(()),
            pltpu.SemaphoreType.DMA((n,)),
            pltpu.SemaphoreType.DMA((n,)),
        ],
        compiler_params=pltpu.CompilerParams(collective_id=collective, has_side_effects=True),
    )(x)


def local(spectra, pair_blocks, owners):
    groups_count = lax.axis_size("grp")
    chan_count = lax.axis_size("chan")
    slot_count = groups_count * MOST
    pairs = BLK * BLK
    part = F // chan_count
    me = lax.axis_index("chan")

    white = whiten(spectra)
    channels = white.shape[0]
    chunks = white.reshape(channels, WINDOWS, 2, chan_count, part).transpose(3, 0, 1, 2, 4)
    chunks = chunks.reshape(chan_count, channels * WINDOWS * 2, part)
    listed = pair_blocks[0, 0].reshape(-1).astype(jnp.bfloat16)
    extra = jnp.zeros((part,), jnp.bfloat16).at[: listed.shape[0]].set(listed)
    extra = jnp.broadcast_to(extra[None, None, :], (chan_count, 1, part))
    sent = jnp.concatenate([chunks, extra], axis=1)
    got = lax.all_to_all(sent, "chan", split_axis=0, concat_axis=0, tiled=True)
    rows_per = channels * WINDOWS * 2
    group_channels = chan_count * channels
    panel = got[:, :rows_per].reshape(group_channels, WINDOWS * 2 * part)
    all_blocks = got[:, rows_per, : NB_SRC * 2].astype(jnp.float32).astype(jnp.int32)
    all_blocks = all_blocks.reshape(chan_count // CORES, CORES, NB_SRC, 2).transpose(1, 0, 2, 3)
    all_blocks = all_blocks.reshape(chan_count * NB_SRC, 1, 2)
    offsets = jnp.arange(BLK, dtype=jnp.int32)
    left_ch = (all_blocks[:, :, 0] * BLK + offsets[None, :])[:, :, None] + jnp.zeros((1, 1, BLK), jnp.int32)
    right_ch = (all_blocks[:, :, 1] * BLK + offsets[None, :])[:, None, :] + jnp.zeros((1, BLK, 1), jnp.int32)
    channel_ids = jnp.arange(group_channels, dtype=jnp.int32)[None, :]
    left_hot = (left_ch.reshape(-1, 1) == channel_ids).astype(jnp.bfloat16)
    right_hot = (right_ch.reshape(-1, 1) == channel_ids).astype(jnp.bfloat16)

    cos_part, sin_part = table_slice(me * part, part)
    partial = pair_correlations(left_hot, right_hot, panel, cos_part, sin_part)
    partial = partial.reshape(CORES, chan_count // CORES * NB_SRC * pairs, LAGS)
    on_chip = exchange(partial, "chan", "grp", False, 1, 0)
    chip_sum = (on_chip[0] + on_chip[1]).reshape(chan_count // CORES, NB_SRC * pairs, LAGS)
    across = exchange(chip_sum, "chan", "grp", False, CORES, 1)
    corr = jnp.sum(across, axis=0).reshape(NB_SRC, pairs * LAGS)

    owner_list = owners[0, 0, :, 0]
    same = owner_list[:, None] == owner_list[None, :]
    earlier = jnp.arange(NB_SRC)[None, :] < jnp.arange(NB_SRC)[:, None]
    order_rank = jnp.sum(jnp.logical_and(same, earlier), axis=1)
    slot_ids = owner_list * MOST + order_rank
    chooser = slot_ids[None, :] == jnp.arange(slot_count, dtype=jnp.int32)[:, None]
    source = jnp.argmax(chooser, axis=1)
    filled = jnp.any(chooser, axis=1)
    placed = jnp.where(filled[:, None], jnp.take(corr, source, axis=0), 0.0)
    placed = placed.reshape(groups_count, MOST, pairs, LAGS).astype(jnp.bfloat16)
    received = exchange(placed, "grp", "chan", True, 1, 2).astype(jnp.float32)
    return received.reshape(1, 1, slot_count, pairs, LAGS)


def solution(mesh):
    return jax.shard_map(
        local,
        mesh=mesh,
        in_specs=(
            P(("grp", "chan"), None, None, None),
            P("grp", "chan", None, None),
            P("grp", "chan", None, None),
        ),
        out_specs=P("grp", "chan", None, None, None),
        check_vma=False,
    )
```

```python
import functools

import jax
import jax.numpy as jnp
from jax import lax
from jax.experimental import pallas as pl
from jax.experimental.pallas import tpu as pltpu
from jax.sharding import PartitionSpec as P

F = 8192
LAGS = 1024
BLK = 2
NB_SRC = 18
MOST = 3
WINDOWS = 2
FINE = 128
ROW_CHUNK = 144
CORES = 2
PARTNER_PIECES = 8
CHIP_PIECES = 4


def phase_angle(bins, lag_index):
    phase = bins[:, None] * lag_index[None, :] % (2 * F)
    return phase.astype(jnp.float32) * (jnp.pi / F)


def table_slice(start, count):
    lag_index = jnp.arange(LAGS, dtype=jnp.int32) - LAGS // 2
    coarse = phase_angle(start + FINE * jnp.arange(count // FINE, dtype=jnp.int32), lag_index)
    fine = phase_angle(jnp.arange(FINE, dtype=jnp.int32), lag_index)
    cos_a, sin_a = jnp.cos(coarse)[:, None, :], jnp.sin(coarse)[:, None, :]
    cos_b, sin_b = jnp.cos(fine)[None, :, :], jnp.sin(fine)[None, :, :]
    cos_ab = (cos_a * cos_b - sin_a * sin_b).reshape(count, LAGS)
    sin_ab = (sin_a * cos_b + cos_a * sin_b).reshape(count, LAGS)
    bins = start + jnp.arange(count, dtype=jnp.int32)
    weight = (jnp.where(bins == 0, 1.0, 2.0).astype(jnp.float32) / jnp.sqrt(jnp.float32(F)))[:, None]
    cos_part = (cos_ab * weight).astype(jnp.bfloat16)
    sin_part = (-sin_ab * weight).astype(jnp.bfloat16)
    return cos_part, sin_part


def whiten(spectra):
    values = spectra.astype(jnp.float32)
    power = values[:, :, 0] ** 2 + values[:, :, 1] ** 2
    level = jnp.mean(power, axis=-1, keepdims=True) + 1e-05
    scale = lax.rsqrt(power + 0.1 * level)
    return (values * scale[:, :, None, :]).astype(jnp.bfloat16)


def pair_kernel(left_hot, right_hot, panel, cos_ref, sin_ref, out_ref):
    part = cos_ref.shape[0]
    chunk = ROW_CHUNK

    def rows_of(hot, window, kind):
        col = (window * 2 + kind) * part
        return jnp.dot(hot, panel[:, col:col + part], preferred_element_type=jnp.float32)

    def one_chunk(step, carry):
        at = pl.multiple_of(step * chunk, chunk)
        left = left_hot[pl.ds(at, chunk), :]
        right = right_hot[pl.ds(at, chunk), :]
        real_sum = None
        imag_sum = None
        for window in range(WINDOWS):
            ra = rows_of(left, window, 0)
            ia = rows_of(left, window, 1)
            rb = rows_of(right, window, 0)
            ib = rows_of(right, window, 1)
            real = (ra * rb + ia * ib).astype(jnp.bfloat16).astype(jnp.float32)
            imag = (ia * rb - ra * ib).astype(jnp.bfloat16).astype(jnp.float32)
            real_sum = real if real_sum is None else real_sum + real
            imag_sum = imag if imag_sum is None else imag_sum + imag
        real_stack = (real_sum / WINDOWS).astype(jnp.bfloat16)
        imag_stack = (imag_sum / WINDOWS).astype(jnp.bfloat16)
        total = jnp.dot(real_stack, cos_ref[...], preferred_element_type=jnp.float32)
        total = total + jnp.dot(imag_stack, sin_ref[...], preferred_element_type=jnp.float32)
        out_ref[pl.ds(at, chunk), :] = total.astype(out_ref.dtype)
        return carry

    lax.fori_loop(0, out_ref.shape[0] // chunk, one_chunk, 0)


def pair_correlations(left_hot, right_hot, panel, cos_part, sin_part):
    rows = left_hot.shape[0]
    part = cos_part.shape[0]
    vmem = pl.BlockSpec(memory_space=pltpu.VMEM)
    flops = 2 * 2 * rows * panel.shape[0] * panel.shape[1] + 2 * 2 * rows * part * LAGS
    return pl.pallas_call(
        pair_kernel,
        out_shape=jax.ShapeDtypeStruct((rows, LAGS), jnp.float32),
        in_specs=[vmem] * 5,
        out_specs=vmem,
        compiler_params=pltpu.CompilerParams(vmem_limit_bytes=56 * 1024 * 1024),
        cost_estimate=pl.CostEstimate(
            flops=flops,
            transcendentals=0,
            bytes_accessed=panel.size * 2 + 4 * part * LAGS + rows * LAGS * 4,
        ),
    )(left_hot, right_hot, panel, cos_part, sin_part)


def exchange_kernel(axis, other_axis, axis_first, stride, x_ref, out_ref, local_sem, send_sem, recv_sem):
    n = x_ref.shape[0]
    index = lax.axis_index(axis)
    me = lax.rem(index // stride, n)
    base = index - me * stride
    other = lax.axis_index(other_axis)

    def device(j):
        coord = base + stride * j
        return (coord, other) if axis_first else (other, coord)

    barrier = pltpu.get_barrier_semaphore()
    for step in range(1, n):
        pl.semaphore_signal(barrier, inc=1, device_id=device(lax.rem(me + step, n)),
                            device_id_type=pl.DeviceIdType.MESH)
    pl.semaphore_wait(barrier, n - 1)

    pieces = x_ref.shape[1]
    own = pltpu.make_async_copy(x_ref.at[me], out_ref.at[me], local_sem)
    own.start()
    copies = []
    for step in range(1, n):
        target = lax.rem(me + step, n)
        for piece in range(pieces):
            copy = pltpu.make_async_remote_copy(
                src_ref=x_ref.at[target, piece],
                dst_ref=out_ref.at[me, piece],
                send_sem=send_sem.at[step, piece],
                recv_sem=recv_sem.at[step, piece],
                device_id=device(target),
                device_id_type=pl.DeviceIdType.MESH,
            )
            copy.start()
            copies.append(copy)
    own.wait()
    for step in range(1, n):
        source = lax.rem(me + n - step, n)
        for piece in range(pieces):
            copies[(step - 1) * pieces + piece].wait_send()
            incoming = pltpu.make_async_remote_copy(
                src_ref=x_ref.at[source, piece],
                dst_ref=out_ref.at[source, piece],
                send_sem=send_sem.at[step, piece],
                recv_sem=recv_sem.at[step, piece],
                device_id=device(source),
                device_id_type=pl.DeviceIdType.MESH,
            )
            incoming.wait_recv()


def exchange(x, axis, other_axis, axis_first, stride, collective):
    n = x.shape[0]
    anywhere = pl.BlockSpec(memory_space=pl.ANY)
    return pl.pallas_call(
        functools.partial(exchange_kernel, axis, other_axis, axis_first, stride),
        out_shape=jax.ShapeDtypeStruct(x.shape, x.dtype),
        in_specs=[anywhere],
        out_specs=anywhere,
        scratch_shapes=[
            pltpu.SemaphoreType.DMA(()),
            pltpu.SemaphoreType.DMA((n, x.shape[1])),
            pltpu.SemaphoreType.DMA((n, x.shape[1])),
        ],
        compiler_params=pltpu.CompilerParams(collective_id=collective, has_side_effects=True),
    )(x)


def local(spectra, pair_blocks, owners):
    groups_count = lax.axis_size("grp")
    chan_count = lax.axis_size("chan")
    slot_count = groups_count * MOST
    pairs = BLK * BLK
    part = F // chan_count
    me = lax.axis_index("chan")

    white = whiten(spectra)
    channels = white.shape[0]
    chunks = white.reshape(channels, WINDOWS, 2, chan_count, part).transpose(3, 0, 1, 2, 4)
    chunks = chunks.reshape(chan_count, channels * WINDOWS * 2, part)
    listed = pair_blocks[0, 0].reshape(-1).astype(jnp.bfloat16)
    extra = jnp.zeros((part,), jnp.bfloat16).at[: listed.shape[0]].set(listed)
    extra = jnp.broadcast_to(extra[None, None, :], (chan_count, 1, part))
    sent = jnp.concatenate([chunks, extra], axis=1)
    got = lax.all_to_all(sent, "chan", split_axis=0, concat_axis=0, tiled=True)
    rows_per = channels * WINDOWS * 2
    group_channels = chan_count * channels
    panel = got[:, :rows_per].reshape(group_channels, WINDOWS * 2 * part)
    all_blocks = got[:, rows_per, : NB_SRC * 2].astype(jnp.float32).astype(jnp.int32)
    all_blocks = all_blocks.reshape(chan_count // CORES, CORES, NB_SRC, 2).transpose(1, 0, 2, 3)
    all_blocks = all_blocks.reshape(chan_count * NB_SRC, 1, 2)
    offsets = jnp.arange(BLK, dtype=jnp.int32)
    left_ch = (all_blocks[:, :, 0] * BLK + offsets[None, :])[:, :, None] + jnp.zeros((1, 1, BLK), jnp.int32)
    right_ch = (all_blocks[:, :, 1] * BLK + offsets[None, :])[:, None, :] + jnp.zeros((1, BLK, 1), jnp.int32)
    channel_ids = jnp.arange(group_channels, dtype=jnp.int32)[None, :]
    left_hot = (left_ch.reshape(-1, 1) == channel_ids).astype(jnp.bfloat16)
    right_hot = (right_ch.reshape(-1, 1) == channel_ids).astype(jnp.bfloat16)

    cos_part, sin_part = table_slice(me * part, part)
    partial = pair_correlations(left_hot, right_hot, panel, cos_part, sin_part)
    partial = partial.reshape(CORES, PARTNER_PIECES, -1, LAGS)
    on_chip = exchange(partial, "chan", "grp", False, 1, 0)
    chip_sum = (on_chip[0] + on_chip[1]).reshape(chan_count // CORES, CHIP_PIECES, -1, LAGS)
    across = exchange(chip_sum, "chan", "grp", False, CORES, 1)
    corr = jnp.sum(across, axis=0).reshape(NB_SRC, pairs * LAGS)

    owner_list = owners[0, 0, :, 0]
    same = owner_list[:, None] == owner_list[None, :]
    earlier = jnp.arange(NB_SRC)[None, :] < jnp.arange(NB_SRC)[:, None]
    order_rank = jnp.sum(jnp.logical_and(same, earlier), axis=1)
    slot_ids = owner_list * MOST + order_rank
    chooser = slot_ids[None, :] == jnp.arange(slot_count, dtype=jnp.int32)[:, None]
    source = jnp.argmax(chooser, axis=1)
    filled = jnp.any(chooser, axis=1)
    placed = jnp.where(filled[:, None], jnp.take(corr, source, axis=0), 0.0)
    placed = placed.reshape(groups_count, 1, MOST, pairs, LAGS).astype(jnp.bfloat16)
    received = exchange(placed, "grp", "chan", True, 1, 2).astype(jnp.float32)
    return received.reshape(1, 1, slot_count, pairs, LAGS)


def solution(mesh):
    return jax.shard_map(
        local,
        mesh=mesh,
        in_specs=(
            P(("grp", "chan"), None, None, None),
            P("grp", "chan", None, None),
            P("grp", "chan", None, None),
        ),
        out_specs=P("grp", "chan", None, None, None),
        check_vma=False,
    )
```

```python
import functools

import jax
import jax.numpy as jnp
from jax import lax
from jax.experimental import pallas as pl
from jax.experimental.pallas import tpu as pltpu
from jax.sharding import PartitionSpec as P

F = 8192
LAGS = 1024
BLK = 2
NB_SRC = 18
MOST = 3
WINDOWS = 2
FINE = 128
ROW_CHUNK = 144


def phase_angle(bins, lag_index):
    phase = bins[:, None] * lag_index[None, :] % (2 * F)
    return phase.astype(jnp.float32) * (jnp.pi / F)


def table_slice(start, count):
    lag_index = jnp.arange(LAGS, dtype=jnp.int32) - LAGS // 2
    coarse = phase_angle(start + FINE * jnp.arange(count // FINE, dtype=jnp.int32), lag_index)
    fine = phase_angle(jnp.arange(FINE, dtype=jnp.int32), lag_index)
    cos_a, sin_a = jnp.cos(coarse)[:, None, :], jnp.sin(coarse)[:, None, :]
    cos_b, sin_b = jnp.cos(fine)[None, :, :], jnp.sin(fine)[None, :, :]
    cos_ab = (cos_a * cos_b - sin_a * sin_b).reshape(count, LAGS)
    sin_ab = (sin_a * cos_b + cos_a * sin_b).reshape(count, LAGS)
    bins = start + jnp.arange(count, dtype=jnp.int32)
    weight = (jnp.where(bins == 0, 1.0, 2.0).astype(jnp.float32) / jnp.sqrt(jnp.float32(F)))[:, None]
    cos_part = (cos_ab * weight).astype(jnp.bfloat16)
    sin_part = (-sin_ab * weight).astype(jnp.bfloat16)
    return cos_part, sin_part


def whiten(spectra):
    values = spectra.astype(jnp.float32)
    power = values[:, :, 0] ** 2 + values[:, :, 1] ** 2
    level = jnp.mean(power, axis=-1, keepdims=True) + 1e-05
    scale = lax.rsqrt(power + 0.1 * level)
    return (values * scale[:, :, None, :]).astype(jnp.bfloat16)


def pair_kernel(left_hot, right_hot, panel, cos_ref, sin_ref, out_ref):
    part = cos_ref.shape[0]
    chunk = ROW_CHUNK

    def rows_of(hot, window, kind):
        col = (window * 2 + kind) * part
        return jnp.dot(hot, panel[:, col:col + part], preferred_element_type=jnp.float32)

    def one_chunk(step, carry):
        at = pl.multiple_of(step * chunk, chunk)
        left = left_hot[pl.ds(at, chunk), :]
        right = right_hot[pl.ds(at, chunk), :]
        real_sum = None
        imag_sum = None
        for window in range(WINDOWS):
            ra = rows_of(left, window, 0)
            ia = rows_of(left, window, 1)
            rb = rows_of(right, window, 0)
            ib = rows_of(right, window, 1)
            real = (ra * rb + ia * ib).astype(jnp.bfloat16).astype(jnp.float32)
            imag = (ia * rb - ra * ib).astype(jnp.bfloat16).astype(jnp.float32)
            real_sum = real if real_sum is None else real_sum + real
            imag_sum = imag if imag_sum is None else imag_sum + imag
        real_stack = (real_sum / WINDOWS).astype(jnp.bfloat16)
        imag_stack = (imag_sum / WINDOWS).astype(jnp.bfloat16)
        total = jnp.dot(real_stack, cos_ref[...], preferred_element_type=jnp.float32)
        total = total + jnp.dot(imag_stack, sin_ref[...], preferred_element_type=jnp.float32)
        out_ref[pl.ds(at, chunk), :] = total.astype(out_ref.dtype)
        return carry

    lax.fori_loop(0, out_ref.shape[0] // chunk, one_chunk, 0)


def pair_correlations(left_hot, right_hot, panel, cos_part, sin_part):
    rows = left_hot.shape[0]
    part = cos_part.shape[0]
    vmem = pl.BlockSpec(memory_space=pltpu.VMEM)
    flops = 2 * 2 * rows * panel.shape[0] * panel.shape[1] + 2 * 2 * rows * part * LAGS
    return pl.pallas_call(
        pair_kernel,
        out_shape=jax.ShapeDtypeStruct((rows, LAGS), jnp.float32),
        in_specs=[vmem] * 5,
        out_specs=vmem,
        compiler_params=pltpu.CompilerParams(vmem_limit_bytes=56 * 1024 * 1024),
        cost_estimate=pl.CostEstimate(
            flops=flops,
            transcendentals=0,
            bytes_accessed=panel.size * 2 + 4 * part * LAGS + rows * LAGS * 4,
        ),
    )(left_hot, right_hot, panel, cos_part, sin_part)


def exchange_kernel(axis, other_axis, axis_first, stride, x_ref, out_ref, local_sem, send_sem, recv_sem):
    n = x_ref.shape[0]
    index = lax.axis_index(axis)
    me = lax.rem(index // stride, n)
    base = index - me * stride
    other = lax.axis_index(other_axis)

    def device(j):
        coord = base + stride * j
        return (coord, other) if axis_first else (other, coord)

    barrier = pltpu.get_barrier_semaphore()
    for step in range(1, n):
        pl.semaphore_signal(barrier, inc=1, device_id=device(lax.rem(me + step, n)),
                            device_id_type=pl.DeviceIdType.MESH)
    pl.semaphore_wait(barrier, n - 1)

    pieces = x_ref.shape[1]
    own = pltpu.make_async_copy(x_ref.at[me], out_ref.at[me], local_sem)
    own.start()
    copies = []
    for step in range(1, n):
        target = lax.rem(me + step, n)
        for piece in range(pieces):
            copy = pltpu.make_async_remote_copy(
                src_ref=x_ref.at[target, piece],
                dst_ref=out_ref.at[me, piece],
                send_sem=send_sem.at[step, piece],
                recv_sem=recv_sem.at[step, piece],
                device_id=device(target),
                device_id_type=pl.DeviceIdType.MESH,
            )
            copy.start()
            copies.append(copy)
    own.wait()
    for step in range(1, n):
        source = lax.rem(me + n - step, n)
        for piece in range(pieces):
            copies[(step - 1) * pieces + piece].wait_send()
            incoming = pltpu.make_async_remote_copy(
                src_ref=x_ref.at[source, piece],
                dst_ref=out_ref.at[source, piece],
                send_sem=send_sem.at[step, piece],
                recv_sem=recv_sem.at[step, piece],
                device_id=device(source),
                device_id_type=pl.DeviceIdType.MESH,
            )
            incoming.wait_recv()


def exchange(x, axis, other_axis, axis_first, stride, collective):
    n = x.shape[0]
    vmem = pl.BlockSpec(memory_space=pltpu.VMEM)
    return pl.pallas_call(
        functools.partial(exchange_kernel, axis, other_axis, axis_first, stride),
        out_shape=jax.ShapeDtypeStruct(x.shape, x.dtype),
        in_specs=[vmem],
        out_specs=vmem,
        scratch_shapes=[
            pltpu.SemaphoreType.DMA(()),
            pltpu.SemaphoreType.DMA((n, x.shape[1])),
            pltpu.SemaphoreType.DMA((n, x.shape[1])),
        ],
        compiler_params=pltpu.CompilerParams(collective_id=collective, has_side_effects=True),
    )(x)


def local(spectra, pair_blocks, owners):
    groups_count = lax.axis_size("grp")
    chan_count = lax.axis_size("chan")
    slot_count = groups_count * MOST
    pairs = BLK * BLK
    part = F // chan_count
    me = lax.axis_index("chan")

    white = whiten(spectra)
    channels = white.shape[0]
    chunks = white.reshape(channels, WINDOWS, 2, chan_count, part).transpose(3, 0, 1, 2, 4)
    chunks = chunks.reshape(chan_count, channels * WINDOWS * 2, part)
    listed = pair_blocks[0, 0].reshape(-1).astype(jnp.bfloat16)
    extra = jnp.zeros((part,), jnp.bfloat16).at[: listed.shape[0]].set(listed)
    extra = jnp.broadcast_to(extra[None, None, :], (chan_count, 1, part))
    sent = jnp.concatenate([chunks, extra], axis=1)
    got = lax.all_to_all(sent, "chan", split_axis=0, concat_axis=0, tiled=True)
    rows_per = channels * WINDOWS * 2
    group_channels = chan_count * channels
    panel = got[:, :rows_per].reshape(group_channels, WINDOWS * 2 * part)
    all_blocks = got[:, rows_per, : NB_SRC * 2].astype(jnp.float32).astype(jnp.int32)
    all_blocks = all_blocks.reshape(chan_count * NB_SRC, 1, 2)
    offsets = jnp.arange(BLK, dtype=jnp.int32)
    left_ch = (all_blocks[:, :, 0] * BLK + offsets[None, :])[:, :, None] + jnp.zeros((1, 1, BLK), jnp.int32)
    right_ch = (all_blocks[:, :, 1] * BLK + offsets[None, :])[:, None, :] + jnp.zeros((1, BLK, 1), jnp.int32)
    channel_ids = jnp.arange(group_channels, dtype=jnp.int32)[None, :]
    left_hot = (left_ch.reshape(-1, 1) == channel_ids).astype(jnp.bfloat16)
    right_hot = (right_ch.reshape(-1, 1) == channel_ids).astype(jnp.bfloat16)

    cos_part, sin_part = table_slice(me * part, part)
    partial = pair_correlations(left_hot, right_hot, panel, cos_part, sin_part)
    partial = partial.reshape(chan_count, 1, NB_SRC * pairs, LAGS)
    gathered = exchange(partial, "chan", "grp", False, 1, 0)
    corr = jnp.sum(gathered, axis=0).reshape(NB_SRC, pairs * LAGS)

    owner_list = owners[0, 0, :, 0]
    same = owner_list[:, None] == owner_list[None, :]
    earlier = jnp.arange(NB_SRC)[None, :] < jnp.arange(NB_SRC)[:, None]
    order_rank = jnp.sum(jnp.logical_and(same, earlier), axis=1)
    slot_ids = owner_list * MOST + order_rank
    chooser = slot_ids[None, :] == jnp.arange(slot_count, dtype=jnp.int32)[:, None]
    source = jnp.argmax(chooser, axis=1)
    filled = jnp.any(chooser, axis=1)
    placed = jnp.where(filled[:, None], jnp.take(corr, source, axis=0), 0.0)
    placed = placed.reshape(groups_count, 1, MOST, pairs, LAGS).astype(jnp.bfloat16)
    received = exchange(placed, "grp", "chan", True, 1, 1).astype(jnp.float32)
    return received.reshape(1, 1, slot_count, pairs, LAGS)


def solution(mesh):
    return jax.shard_map(
        local,
        mesh=mesh,
        in_specs=(
            P(("grp", "chan"), None, None, None),
            P("grp", "chan", None, None),
            P("grp", "chan", None, None),
        ),
        out_specs=P("grp", "chan", None, None, None),
        check_vma=False,
    )
```

```python
import functools

import jax
import jax.numpy as jnp
from jax import lax
from jax.experimental import pallas as pl
from jax.experimental.pallas import tpu as pltpu
from jax.sharding import PartitionSpec as P

F = 8192
LAGS = 1024
BLK = 2
NB_SRC = 18
MOST = 3
WINDOWS = 2
FINE = 128


def phase_angle(bins, lag_index):
    phase = bins[:, None] * lag_index[None, :] % (2 * F)
    return phase.astype(jnp.float32) * (jnp.pi / F)


def table_slice(start, count):
    lag_index = jnp.arange(LAGS, dtype=jnp.int32) - LAGS // 2
    coarse = phase_angle(start + FINE * jnp.arange(count // FINE, dtype=jnp.int32), lag_index)
    fine = phase_angle(jnp.arange(FINE, dtype=jnp.int32), lag_index)
    cos_a, sin_a = jnp.cos(coarse)[:, None, :], jnp.sin(coarse)[:, None, :]
    cos_b, sin_b = jnp.cos(fine)[None, :, :], jnp.sin(fine)[None, :, :]
    cos_ab = (cos_a * cos_b - sin_a * sin_b).reshape(count, LAGS)
    sin_ab = (sin_a * cos_b + cos_a * sin_b).reshape(count, LAGS)
    bins = start + jnp.arange(count, dtype=jnp.int32)
    weight = (jnp.where(bins == 0, 1.0, 2.0).astype(jnp.float32) / jnp.sqrt(jnp.float32(F)))[:, None]
    cos_part = (cos_ab * weight).astype(jnp.bfloat16)
    sin_part = (-sin_ab * weight).astype(jnp.bfloat16)
    return cos_part, sin_part


def whiten(spectra):
    values = spectra.astype(jnp.float32)
    power = values[:, :, 0] ** 2 + values[:, :, 1] ** 2
    level = jnp.mean(power, axis=-1, keepdims=True) + 1e-05
    scale = lax.rsqrt(power + 0.1 * level)
    return (values * scale[:, :, None, :]).astype(jnp.bfloat16)


def pair_rows(left_hot, right_hot, panel, cos_ref, sin_ref, target):
    part = cos_ref.shape[0]
    left = left_hot[target]
    right = right_hot[target]

    def rows_of(hot, window, kind):
        col = (window * 2 + kind) * part
        return jnp.dot(hot, panel[:, col:col + part], preferred_element_type=jnp.float32)

    real_sum = None
    imag_sum = None
    for window in range(WINDOWS):
        ra = rows_of(left, window, 0)
        ia = rows_of(left, window, 1)
        rb = rows_of(right, window, 0)
        ib = rows_of(right, window, 1)
        real = (ra * rb + ia * ib).astype(jnp.bfloat16).astype(jnp.float32)
        imag = (ia * rb - ra * ib).astype(jnp.bfloat16).astype(jnp.float32)
        real_sum = real if real_sum is None else real_sum + real
        imag_sum = imag if imag_sum is None else imag_sum + imag
    real_stack = (real_sum / WINDOWS).astype(jnp.bfloat16)
    imag_stack = (imag_sum / WINDOWS).astype(jnp.bfloat16)
    total = jnp.dot(real_stack, cos_ref[...], preferred_element_type=jnp.float32)
    return total + jnp.dot(imag_stack, sin_ref[...], preferred_element_type=jnp.float32)


def pair_exchange_kernel(left_hot, right_hot, panel, cos_ref, sin_ref, out_ref, slots, local_sem, send_sem, recv_sem):
    n = out_ref.shape[0]
    me = lax.axis_index("chan")
    group = lax.axis_index("grp")

    barrier = pltpu.get_barrier_semaphore()
    for step in range(1, n):
        pl.semaphore_signal(barrier, inc=1, device_id=(group, lax.rem(me + step, n)),
                            device_id_type=pl.DeviceIdType.MESH)
    pl.semaphore_wait(barrier, n - 1)

    def fill(target):
        slots[target] = pair_rows(left_hot, right_hot, panel, cos_ref, sin_ref, target)

    def send(step):
        target = lax.rem(me + step, n)
        return pltpu.make_async_remote_copy(
            src_ref=slots.at[target],
            dst_ref=out_ref.at[me],
            send_sem=send_sem.at[step],
            recv_sem=recv_sem.at[step],
            device_id=(group, target),
            device_id_type=pl.DeviceIdType.MESH,
        )

    def one_step(step, carry):
        fill(lax.rem(me + step, n))

        @pl.when(step > 1)
        def _():
            send(step - 1).start()

        return carry

    lax.fori_loop(1, n, one_step, 0)
    fill(me)
    send(n - 1).start()
    own = pltpu.make_async_copy(slots.at[me], out_ref.at[me], local_sem)
    own.start()
    own.wait()

    def finish(step, carry):
        send(step).wait_send()
        source = lax.rem(me + n - step, n)
        pltpu.make_async_remote_copy(
            src_ref=slots.at[source],
            dst_ref=out_ref.at[source],
            send_sem=send_sem.at[step],
            recv_sem=recv_sem.at[step],
            device_id=(group, source),
            device_id_type=pl.DeviceIdType.MESH,
        ).wait_recv()
        return carry

    lax.fori_loop(1, n, finish, 0)


def pair_exchange(left_hot, right_hot, panel, cos_part, sin_part, chan_count, collective):
    rows = left_hot.shape[0]
    count = rows // chan_count
    left_hot = left_hot.reshape(chan_count, count, -1)
    right_hot = right_hot.reshape(chan_count, count, -1)
    part = cos_part.shape[0]
    vmem = pl.BlockSpec(memory_space=pltpu.VMEM)
    flops = 2 * 2 * rows * panel.shape[0] * panel.shape[1] + 2 * 2 * rows * part * LAGS
    return pl.pallas_call(
        pair_exchange_kernel,
        out_shape=jax.ShapeDtypeStruct((chan_count, count, LAGS), jnp.float32),
        in_specs=[vmem] * 5,
        out_specs=pl.BlockSpec(memory_space=pl.ANY),
        scratch_shapes=[
            pltpu.VMEM((chan_count, count, LAGS), jnp.float32),
            pltpu.SemaphoreType.DMA(()),
            pltpu.SemaphoreType.DMA((chan_count,)),
            pltpu.SemaphoreType.DMA((chan_count,)),
        ],
        compiler_params=pltpu.CompilerParams(
            collective_id=collective, has_side_effects=True, vmem_limit_bytes=56 * 1024 * 1024
        ),
        cost_estimate=pl.CostEstimate(
            flops=flops,
            transcendentals=0,
            bytes_accessed=panel.size * 2 + 4 * part * LAGS + rows * LAGS * 4,
        ),
    )(left_hot, right_hot, panel, cos_part, sin_part)


def exchange_kernel(axis, other_axis, axis_first, stride, x_ref, out_ref, local_sem, send_sem, recv_sem):
    n = x_ref.shape[0]
    index = lax.axis_index(axis)
    me = lax.rem(index // stride, n)
    base = index - me * stride
    other = lax.axis_index(other_axis)

    def device(j):
        coord = base + stride * j
        return (coord, other) if axis_first else (other, coord)

    barrier = pltpu.get_barrier_semaphore()
    for step in range(1, n):
        pl.semaphore_signal(barrier, inc=1, device_id=device(lax.rem(me + step, n)),
                            device_id_type=pl.DeviceIdType.MESH)
    pl.semaphore_wait(barrier, n - 1)

    pieces = x_ref.shape[1]
    own = pltpu.make_async_copy(x_ref.at[me], out_ref.at[me], local_sem)
    own.start()
    copies = []
    for step in range(1, n):
        target = lax.rem(me + step, n)
        for piece in range(pieces):
            copy = pltpu.make_async_remote_copy(
                src_ref=x_ref.at[target, piece],
                dst_ref=out_ref.at[me, piece],
                send_sem=send_sem.at[step, piece],
                recv_sem=recv_sem.at[step, piece],
                device_id=device(target),
                device_id_type=pl.DeviceIdType.MESH,
            )
            copy.start()
            copies.append(copy)
    own.wait()
    for step in range(1, n):
        source = lax.rem(me + n - step, n)
        for piece in range(pieces):
            copies[(step - 1) * pieces + piece].wait_send()
            incoming = pltpu.make_async_remote_copy(
                src_ref=x_ref.at[source, piece],
                dst_ref=out_ref.at[source, piece],
                send_sem=send_sem.at[step, piece],
                recv_sem=recv_sem.at[step, piece],
                device_id=device(source),
                device_id_type=pl.DeviceIdType.MESH,
            )
            incoming.wait_recv()


def exchange(x, axis, other_axis, axis_first, stride, collective):
    n = x.shape[0]
    vmem = pl.BlockSpec(memory_space=pltpu.VMEM)
    return pl.pallas_call(
        functools.partial(exchange_kernel, axis, other_axis, axis_first, stride),
        out_shape=jax.ShapeDtypeStruct(x.shape, x.dtype),
        in_specs=[vmem],
        out_specs=vmem,
        scratch_shapes=[
            pltpu.SemaphoreType.DMA(()),
            pltpu.SemaphoreType.DMA((n, x.shape[1])),
            pltpu.SemaphoreType.DMA((n, x.shape[1])),
        ],
        compiler_params=pltpu.CompilerParams(collective_id=collective, has_side_effects=True),
    )(x)


def local(spectra, pair_blocks, owners):
    groups_count = lax.axis_size("grp")
    chan_count = lax.axis_size("chan")
    slot_count = groups_count * MOST
    pairs = BLK * BLK
    part = F // chan_count
    me = lax.axis_index("chan")

    white = whiten(spectra)
    channels = white.shape[0]
    chunks = white.reshape(channels, WINDOWS, 2, chan_count, part).transpose(3, 0, 1, 2, 4)
    chunks = chunks.reshape(chan_count, channels * WINDOWS * 2, part)
    listed = pair_blocks[0, 0].reshape(-1).astype(jnp.bfloat16)
    extra = jnp.zeros((part,), jnp.bfloat16).at[: listed.shape[0]].set(listed)
    extra = jnp.broadcast_to(extra[None, None, :], (chan_count, 1, part))
    sent = jnp.concatenate([chunks, extra], axis=1)
    got = lax.all_to_all(sent, "chan", split_axis=0, concat_axis=0, tiled=True)
    rows_per = channels * WINDOWS * 2
    group_channels = chan_count * channels
    panel = got[:, :rows_per].reshape(group_channels, WINDOWS * 2 * part)
    all_blocks = got[:, rows_per, : NB_SRC * 2].astype(jnp.float32).astype(jnp.int32)
    all_blocks = all_blocks.reshape(chan_count * NB_SRC, 1, 2)
    offsets = jnp.arange(BLK, dtype=jnp.int32)
    left_ch = (all_blocks[:, :, 0] * BLK + offsets[None, :])[:, :, None] + jnp.zeros((1, 1, BLK), jnp.int32)
    right_ch = (all_blocks[:, :, 1] * BLK + offsets[None, :])[:, None, :] + jnp.zeros((1, BLK, 1), jnp.int32)
    channel_ids = jnp.arange(group_channels, dtype=jnp.int32)[None, :]
    left_hot = (left_ch.reshape(-1, 1) == channel_ids).astype(jnp.bfloat16)
    right_hot = (right_ch.reshape(-1, 1) == channel_ids).astype(jnp.bfloat16)

    cos_part, sin_part = table_slice(me * part, part)
    gathered = pair_exchange(left_hot, right_hot, panel, cos_part, sin_part, chan_count, 0)
    corr = jnp.sum(gathered, axis=0).reshape(NB_SRC, pairs * LAGS)

    owner_list = owners[0, 0, :, 0]
    same = owner_list[:, None] == owner_list[None, :]
    earlier = jnp.arange(NB_SRC)[None, :] < jnp.arange(NB_SRC)[:, None]
    order_rank = jnp.sum(jnp.logical_and(same, earlier), axis=1)
    slot_ids = owner_list * MOST + order_rank
    chooser = slot_ids[None, :] == jnp.arange(slot_count, dtype=jnp.int32)[:, None]
    source = jnp.argmax(chooser, axis=1)
    filled = jnp.any(chooser, axis=1)
    placed = jnp.where(filled[:, None], jnp.take(corr, source, axis=0), 0.0)
    placed = placed.reshape(groups_count, 1, MOST, pairs, LAGS).astype(jnp.bfloat16)
    received = exchange(placed, "grp", "chan", True, 1, 1).astype(jnp.float32)
    return received.reshape(1, 1, slot_count, pairs, LAGS)


def solution(mesh):
    return jax.shard_map(
        local,
        mesh=mesh,
        in_specs=(
            P(("grp", "chan"), None, None, None),
            P("grp", "chan", None, None),
            P("grp", "chan", None, None),
        ),
        out_specs=P("grp", "chan", None, None, None),
        check_vma=False,
    )
```

```python
import functools

import jax
import jax.numpy as jnp
from jax import lax
from jax.experimental import pallas as pl
from jax.experimental.pallas import tpu as pltpu
from jax.sharding import PartitionSpec as P

F = 8192
LAGS = 1024
BLK = 2
NB_SRC = 18
MOST = 3
WINDOWS = 2
FINE = 128


def phase_angle(bins, lag_index):
    phase = bins[:, None] * lag_index[None, :] % (2 * F)
    return phase.astype(jnp.float32) * (jnp.pi / F)


def table_slice(start, count):
    lag_index = jnp.arange(LAGS, dtype=jnp.int32) - LAGS // 2
    coarse = phase_angle(start + FINE * jnp.arange(count // FINE, dtype=jnp.int32), lag_index)
    fine = phase_angle(jnp.arange(FINE, dtype=jnp.int32), lag_index)
    cos_a, sin_a = jnp.cos(coarse)[:, None, :], jnp.sin(coarse)[:, None, :]
    cos_b, sin_b = jnp.cos(fine)[None, :, :], jnp.sin(fine)[None, :, :]
    cos_ab = (cos_a * cos_b - sin_a * sin_b).reshape(count, LAGS)
    sin_ab = (sin_a * cos_b + cos_a * sin_b).reshape(count, LAGS)
    bins = start + jnp.arange(count, dtype=jnp.int32)
    weight = (jnp.where(bins == 0, 1.0, 2.0).astype(jnp.float32) / jnp.sqrt(jnp.float32(F)))[:, None]
    cos_part = (cos_ab * weight).astype(jnp.bfloat16)
    sin_part = (-sin_ab * weight).astype(jnp.bfloat16)
    return cos_part, sin_part


def whiten(spectra):
    values = spectra.astype(jnp.float32)
    power = values[:, :, 0] ** 2 + values[:, :, 1] ** 2
    level = jnp.mean(power, axis=-1, keepdims=True) + 1e-05
    scale = lax.rsqrt(power + 0.1 * level)
    return (values * scale[:, :, None, :]).astype(jnp.bfloat16)


def pair_rows(left_hot, right_hot, panel, cos_ref, sin_ref, target):
    part = cos_ref.shape[0]
    left = left_hot[target]
    right = right_hot[target]

    def rows_of(hot, window, kind):
        col = (window * 2 + kind) * part
        return jnp.dot(hot, panel[:, col:col + part], preferred_element_type=jnp.float32)

    real_sum = None
    imag_sum = None
    for window in range(WINDOWS):
        ra = rows_of(left, window, 0)
        ia = rows_of(left, window, 1)
        rb = rows_of(right, window, 0)
        ib = rows_of(right, window, 1)
        real = (ra * rb + ia * ib).astype(jnp.bfloat16).astype(jnp.float32)
        imag = (ia * rb - ra * ib).astype(jnp.bfloat16).astype(jnp.float32)
        real_sum = real if real_sum is None else real_sum + real
        imag_sum = imag if imag_sum is None else imag_sum + imag
    real_stack = (real_sum / WINDOWS).astype(jnp.bfloat16)
    imag_stack = (imag_sum / WINDOWS).astype(jnp.bfloat16)
    total = jnp.dot(real_stack, cos_ref[...], preferred_element_type=jnp.float32)
    return total + jnp.dot(imag_stack, sin_ref[...], preferred_element_type=jnp.float32)


def pair_exchange_kernel(left_hot, right_hot, panel, cos_ref, sin_ref, out_ref, slots, local_sem, send_sem, recv_sem):
    n = out_ref.shape[0]
    me = lax.axis_index("chan")
    group = lax.axis_index("grp")

    barrier = pltpu.get_barrier_semaphore()
    for step in range(1, n):
        pl.semaphore_signal(barrier, inc=1, device_id=(group, lax.rem(me + step, n)),
                            device_id_type=pl.DeviceIdType.MESH)
    pl.semaphore_wait(barrier, n - 1)

    def fill(target):
        slots[target] = pair_rows(left_hot, right_hot, panel, cos_ref, sin_ref, target).astype(slots.dtype)

    def send(step):
        target = lax.rem(me + step, n)
        return pltpu.make_async_remote_copy(
            src_ref=slots.at[target],
            dst_ref=out_ref.at[me],
            send_sem=send_sem.at[step],
            recv_sem=recv_sem.at[step],
            device_id=(group, target),
            device_id_type=pl.DeviceIdType.MESH,
        )

    def one_step(step, carry):
        fill(lax.rem(me + step, n))

        @pl.when(step > 1)
        def _():
            send(step - 1).start()

        return carry

    lax.fori_loop(1, n, one_step, 0)
    fill(me)
    send(n - 1).start()
    own = pltpu.make_async_copy(slots.at[me], out_ref.at[me], local_sem)
    own.start()
    own.wait()

    def finish(step, carry):
        send(step).wait_send()
        source = lax.rem(me + n - step, n)
        pltpu.make_async_remote_copy(
            src_ref=slots.at[source],
            dst_ref=out_ref.at[source],
            send_sem=send_sem.at[step],
            recv_sem=recv_sem.at[step],
            device_id=(group, source),
            device_id_type=pl.DeviceIdType.MESH,
        ).wait_recv()
        return carry

    lax.fori_loop(1, n, finish, 0)


def pair_exchange(left_hot, right_hot, panel, cos_part, sin_part, chan_count, collective):
    rows = left_hot.shape[0]
    count = rows // chan_count
    left_hot = left_hot.reshape(chan_count, count, -1)
    right_hot = right_hot.reshape(chan_count, count, -1)
    part = cos_part.shape[0]
    vmem = pl.BlockSpec(memory_space=pltpu.VMEM)
    flops = 2 * 2 * rows * panel.shape[0] * panel.shape[1] + 2 * 2 * rows * part * LAGS
    return pl.pallas_call(
        pair_exchange_kernel,
        out_shape=jax.ShapeDtypeStruct((chan_count, count, LAGS), jnp.bfloat16),
        in_specs=[vmem] * 5,
        out_specs=pl.BlockSpec(memory_space=pl.ANY),
        scratch_shapes=[
            pltpu.VMEM((chan_count, count, LAGS), jnp.bfloat16),
            pltpu.SemaphoreType.DMA(()),
            pltpu.SemaphoreType.DMA((chan_count,)),
            pltpu.SemaphoreType.DMA((chan_count,)),
        ],
        compiler_params=pltpu.CompilerParams(
            collective_id=collective, has_side_effects=True, vmem_limit_bytes=56 * 1024 * 1024
        ),
        cost_estimate=pl.CostEstimate(
            flops=flops,
            transcendentals=0,
            bytes_accessed=panel.size * 2 + 4 * part * LAGS + rows * LAGS * 2,
        ),
    )(left_hot, right_hot, panel, cos_part, sin_part)


def exchange_kernel(axis, other_axis, axis_first, stride, x_ref, out_ref, local_sem, send_sem, recv_sem):
    n = x_ref.shape[0]
    index = lax.axis_index(axis)
    me = lax.rem(index // stride, n)
    base = index - me * stride
    other = lax.axis_index(other_axis)

    def device(j):
        coord = base + stride * j
        return (coord, other) if axis_first else (other, coord)

    barrier = pltpu.get_barrier_semaphore()
    for step in range(1, n):
        pl.semaphore_signal(barrier, inc=1, device_id=device(lax.rem(me + step, n)),
                            device_id_type=pl.DeviceIdType.MESH)
    pl.semaphore_wait(barrier, n - 1)

    pieces = x_ref.shape[1]
    own = pltpu.make_async_copy(x_ref.at[me], out_ref.at[me], local_sem)
    own.start()
    copies = []
    for step in range(1, n):
        target = lax.rem(me + step, n)
        for piece in range(pieces):
            copy = pltpu.make_async_remote_copy(
                src_ref=x_ref.at[target, piece],
                dst_ref=out_ref.at[me, piece],
                send_sem=send_sem.at[step, piece],
                recv_sem=recv_sem.at[step, piece],
                device_id=device(target),
                device_id_type=pl.DeviceIdType.MESH,
            )
            copy.start()
            copies.append(copy)
    own.wait()
    for step in range(1, n):
        source = lax.rem(me + n - step, n)
        for piece in range(pieces):
            copies[(step - 1) * pieces + piece].wait_send()
            incoming = pltpu.make_async_remote_copy(
                src_ref=x_ref.at[source, piece],
                dst_ref=out_ref.at[source, piece],
                send_sem=send_sem.at[step, piece],
                recv_sem=recv_sem.at[step, piece],
                device_id=device(source),
                device_id_type=pl.DeviceIdType.MESH,
            )
            incoming.wait_recv()


def exchange(x, axis, other_axis, axis_first, stride, collective):
    n = x.shape[0]
    vmem = pl.BlockSpec(memory_space=pltpu.VMEM)
    return pl.pallas_call(
        functools.partial(exchange_kernel, axis, other_axis, axis_first, stride),
        out_shape=jax.ShapeDtypeStruct(x.shape, x.dtype),
        in_specs=[vmem],
        out_specs=vmem,
        scratch_shapes=[
            pltpu.SemaphoreType.DMA(()),
            pltpu.SemaphoreType.DMA((n, x.shape[1])),
            pltpu.SemaphoreType.DMA((n, x.shape[1])),
        ],
        compiler_params=pltpu.CompilerParams(collective_id=collective, has_side_effects=True),
    )(x)


def local(spectra, pair_blocks, owners):
    groups_count = lax.axis_size("grp")
    chan_count = lax.axis_size("chan")
    slot_count = groups_count * MOST
    pairs = BLK * BLK
    part = F // chan_count
    me = lax.axis_index("chan")

    white = whiten(spectra)
    channels = white.shape[0]
    chunks = white.reshape(channels, WINDOWS, 2, chan_count, part).transpose(3, 0, 1, 2, 4)
    chunks = chunks.reshape(chan_count, channels * WINDOWS * 2, part)
    listed = pair_blocks[0, 0].reshape(-1).astype(jnp.bfloat16)
    extra = jnp.zeros((part,), jnp.bfloat16).at[: listed.shape[0]].set(listed)
    extra = jnp.broadcast_to(extra[None, None, :], (chan_count, 1, part))
    sent = jnp.concatenate([chunks, extra], axis=1)
    got = lax.all_to_all(sent, "chan", split_axis=0, concat_axis=0, tiled=True)
    rows_per = channels * WINDOWS * 2
    group_channels = chan_count * channels
    panel = got[:, :rows_per].reshape(group_channels, WINDOWS * 2 * part)
    all_blocks = got[:, rows_per, : NB_SRC * 2].astype(jnp.float32).astype(jnp.int32)
    all_blocks = all_blocks.reshape(chan_count * NB_SRC, 1, 2)
    offsets = jnp.arange(BLK, dtype=jnp.int32)
    left_ch = (all_blocks[:, :, 0] * BLK + offsets[None, :])[:, :, None] + jnp.zeros((1, 1, BLK), jnp.int32)
    right_ch = (all_blocks[:, :, 1] * BLK + offsets[None, :])[:, None, :] + jnp.zeros((1, BLK, 1), jnp.int32)
    channel_ids = jnp.arange(group_channels, dtype=jnp.int32)[None, :]
    left_hot = (left_ch.reshape(-1, 1) == channel_ids).astype(jnp.bfloat16)
    right_hot = (right_ch.reshape(-1, 1) == channel_ids).astype(jnp.bfloat16)

    cos_part, sin_part = table_slice(me * part, part)
    gathered = pair_exchange(left_hot, right_hot, panel, cos_part, sin_part, chan_count, 0)
    corr = jnp.sum(gathered.astype(jnp.float32), axis=0).reshape(NB_SRC, pairs * LAGS)

    owner_list = owners[0, 0, :, 0]
    same = owner_list[:, None] == owner_list[None, :]
    earlier = jnp.arange(NB_SRC)[None, :] < jnp.arange(NB_SRC)[:, None]
    order_rank = jnp.sum(jnp.logical_and(same, earlier), axis=1)
    slot_ids = owner_list * MOST + order_rank
    chooser = slot_ids[None, :] == jnp.arange(slot_count, dtype=jnp.int32)[:, None]
    source = jnp.argmax(chooser, axis=1)
    filled = jnp.any(chooser, axis=1)
    placed = jnp.where(filled[:, None], jnp.take(corr, source, axis=0), 0.0)
    placed = placed.reshape(groups_count, 1, MOST, pairs, LAGS).astype(jnp.bfloat16)
    received = exchange(placed, "grp", "chan", True, 1, 1).astype(jnp.float32)
    return received.reshape(1, 1, slot_count, pairs, LAGS)


def solution(mesh):
    return jax.shard_map(
        local,
        mesh=mesh,
        in_specs=(
            P(("grp", "chan"), None, None, None),
            P("grp", "chan", None, None),
            P("grp", "chan", None, None),
        ),
        out_specs=P("grp", "chan", None, None, None),
        check_vma=False,
    )
```

```python
import functools

import jax
import jax.numpy as jnp
from jax import lax
from jax.experimental import pallas as pl
from jax.experimental.pallas import tpu as pltpu
from jax.sharding import PartitionSpec as P

F = 8192
LAGS = 1024
BLK = 2
NB_SRC = 18
MOST = 3
WINDOWS = 2
FINE = 128


def phase_angle(bins, lag_index):
    phase = bins[:, None] * lag_index[None, :] % (2 * F)
    return phase.astype(jnp.float32) * (jnp.pi / F)


def table_factors(start, count):
    lag_index = jnp.arange(LAGS, dtype=jnp.int32) - LAGS // 2
    coarse = phase_angle(start + FINE * jnp.arange(count // FINE, dtype=jnp.int32), lag_index)
    fine = phase_angle(jnp.arange(FINE, dtype=jnp.int32), lag_index)
    bins = start + jnp.arange(count, dtype=jnp.int32)
    weight = (jnp.where(bins == 0, 1.0, 2.0).astype(jnp.float32) / jnp.sqrt(jnp.float32(F)))[:, None]
    return jnp.cos(coarse), jnp.sin(coarse), jnp.cos(fine), jnp.sin(fine), weight


def fill_tables(cos_a, sin_a, cos_b, sin_b, weight, cos_out, sin_out):
    fine = cos_b.shape[0]
    for q in range(cos_a.shape[0]):
        ca = cos_a[q:q + 1, :]
        sa = sin_a[q:q + 1, :]
        cb = cos_b[...]
        sb = sin_b[...]
        w = weight[q * fine:(q + 1) * fine, :]
        cos_out[q * fine:(q + 1) * fine, :] = ((ca * cb - sa * sb) * w).astype(cos_out.dtype)
        sin_out[q * fine:(q + 1) * fine, :] = (-(sa * cb + ca * sb) * w).astype(sin_out.dtype)


def whiten(spectra):
    values = spectra.astype(jnp.float32)
    power = values[:, :, 0] ** 2 + values[:, :, 1] ** 2
    level = jnp.mean(power, axis=-1, keepdims=True) + 1e-05
    scale = lax.rsqrt(power + 0.1 * level)
    return (values * scale[:, :, None, :]).astype(jnp.bfloat16)


def pair_rows(left_hot, right_hot, panel, cos_ref, sin_ref, target):
    part = cos_ref.shape[0]
    left = left_hot[target]
    right = right_hot[target]

    def rows_of(hot, window, kind):
        col = (window * 2 + kind) * part
        return jnp.dot(hot, panel[:, col:col + part], preferred_element_type=jnp.float32)

    real_sum = None
    imag_sum = None
    for window in range(WINDOWS):
        ra = rows_of(left, window, 0)
        ia = rows_of(left, window, 1)
        rb = rows_of(right, window, 0)
        ib = rows_of(right, window, 1)
        real = (ra * rb + ia * ib).astype(jnp.bfloat16).astype(jnp.float32)
        imag = (ia * rb - ra * ib).astype(jnp.bfloat16).astype(jnp.float32)
        real_sum = real if real_sum is None else real_sum + real
        imag_sum = imag if imag_sum is None else imag_sum + imag
    real_stack = (real_sum / WINDOWS).astype(jnp.bfloat16)
    imag_stack = (imag_sum / WINDOWS).astype(jnp.bfloat16)
    total = jnp.dot(real_stack, cos_ref[...], preferred_element_type=jnp.float32)
    return total + jnp.dot(imag_stack, sin_ref[...], preferred_element_type=jnp.float32)


def pair_exchange_kernel(left_hot, right_hot, panel, cos_ref, sin_ref, out_ref, slots, local_sem, send_sem, recv_sem):
    n = out_ref.shape[0]
    me = lax.axis_index("chan")
    group = lax.axis_index("grp")

    barrier = pltpu.get_barrier_semaphore()
    for step in range(1, n):
        pl.semaphore_signal(barrier, inc=1, device_id=(group, lax.rem(me + step, n)),
                            device_id_type=pl.DeviceIdType.MESH)
    pl.semaphore_wait(barrier, n - 1)

    def fill(target):
        slots[target] = pair_rows(left_hot, right_hot, panel, cos_ref, sin_ref, target).astype(slots.dtype)

    def send(step):
        target = lax.rem(me + step, n)
        return pltpu.make_async_remote_copy(
            src_ref=slots.at[target],
            dst_ref=out_ref.at[me],
            send_sem=send_sem.at[step],
            recv_sem=recv_sem.at[step],
            device_id=(group, target),
            device_id_type=pl.DeviceIdType.MESH,
        )

    def one_step(step, carry):
        fill(lax.rem(me + step, n))

        @pl.when(step > 1)
        def _():
            send(step - 1).start()

        return carry

    lax.fori_loop(1, n, one_step, 0)
    fill(me)
    send(n - 1).start()
    own = pltpu.make_async_copy(slots.at[me], out_ref.at[me], local_sem)
    own.start()
    own.wait()

    def finish(step, carry):
        send(step).wait_send()
        source = lax.rem(me + n - step, n)
        pltpu.make_async_remote_copy(
            src_ref=slots.at[source],
            dst_ref=out_ref.at[source],
            send_sem=send_sem.at[step],
            recv_sem=recv_sem.at[step],
            device_id=(group, source),
            device_id_type=pl.DeviceIdType.MESH,
        ).wait_recv()
        return carry

    lax.fori_loop(1, n, finish, 0)


def pair_exchange(left_hot, right_hot, panel, cos_part, sin_part, chan_count, collective):
    rows = left_hot.shape[0]
    count = rows // chan_count
    left_hot = left_hot.reshape(chan_count, count, -1)
    right_hot = right_hot.reshape(chan_count, count, -1)
    part = cos_part.shape[0]
    vmem = pl.BlockSpec(memory_space=pltpu.VMEM)
    flops = 2 * 2 * rows * panel.shape[0] * panel.shape[1] + 2 * 2 * rows * part * LAGS
    return pl.pallas_call(
        pair_exchange_kernel,
        out_shape=jax.ShapeDtypeStruct((chan_count, count, LAGS), jnp.bfloat16),
        in_specs=[vmem] * 5,
        out_specs=pl.BlockSpec(memory_space=pl.ANY),
        scratch_shapes=[
            pltpu.VMEM((chan_count, count, LAGS), jnp.bfloat16),
            pltpu.SemaphoreType.DMA(()),
            pltpu.SemaphoreType.DMA((chan_count,)),
            pltpu.SemaphoreType.DMA((chan_count,)),
        ],
        compiler_params=pltpu.CompilerParams(
            collective_id=collective, has_side_effects=True, vmem_limit_bytes=56 * 1024 * 1024
        ),
        cost_estimate=pl.CostEstimate(
            flops=flops,
            transcendentals=0,
            bytes_accessed=panel.size * 2 + 4 * part * LAGS + rows * LAGS * 2,
        ),
    )(left_hot, right_hot, panel, cos_part, sin_part)


def exchange_kernel(axis, other_axis, axis_first, stride, x_ref, out_ref, local_sem, send_sem, recv_sem):
    n = x_ref.shape[0]
    index = lax.axis_index(axis)
    me = lax.rem(index // stride, n)
    base = index - me * stride
    other = lax.axis_index(other_axis)

    def device(j):
        coord = base + stride * j
        return (coord, other) if axis_first else (other, coord)

    barrier = pltpu.get_barrier_semaphore()
    for step in range(1, n):
        pl.semaphore_signal(barrier, inc=1, device_id=device(lax.rem(me + step, n)),
                            device_id_type=pl.DeviceIdType.MESH)
    pl.semaphore_wait(barrier, n - 1)

    pieces = x_ref.shape[1]
    own = pltpu.make_async_copy(x_ref.at[me], out_ref.at[me], local_sem)
    own.start()
    copies = []
    for step in range(1, n):
        target = lax.rem(me + step, n)
        for piece in range(pieces):
            copy = pltpu.make_async_remote_copy(
                src_ref=x_ref.at[target, piece],
                dst_ref=out_ref.at[me, piece],
                send_sem=send_sem.at[step, piece],
                recv_sem=recv_sem.at[step, piece],
                device_id=device(target),
                device_id_type=pl.DeviceIdType.MESH,
            )
            copy.start()
            copies.append(copy)
    own.wait()
    for step in range(1, n):
        source = lax.rem(me + n - step, n)
        for piece in range(pieces):
            copies[(step - 1) * pieces + piece].wait_send()
            incoming = pltpu.make_async_remote_copy(
                src_ref=x_ref.at[source, piece],
                dst_ref=out_ref.at[source, piece],
                send_sem=send_sem.at[step, piece],
                recv_sem=recv_sem.at[step, piece],
                device_id=device(source),
                device_id_type=pl.DeviceIdType.MESH,
            )
            incoming.wait_recv()


def exchange(x, axis, other_axis, axis_first, stride, collective):
    n = x.shape[0]
    vmem = pl.BlockSpec(memory_space=pltpu.VMEM)
    return pl.pallas_call(
        functools.partial(exchange_kernel, axis, other_axis, axis_first, stride),
        out_shape=jax.ShapeDtypeStruct(x.shape, x.dtype),
        in_specs=[vmem],
        out_specs=vmem,
        scratch_shapes=[
            pltpu.SemaphoreType.DMA(()),
            pltpu.SemaphoreType.DMA((n, x.shape[1])),
            pltpu.SemaphoreType.DMA((n, x.shape[1])),
        ],
        compiler_params=pltpu.CompilerParams(collective_id=collective, has_side_effects=True),
    )(x)


def spectra_kernel(x_ref, cos_a, sin_a, cos_b, sin_b, weight, out_ref, cos_out, sin_out,
                   local_sem, send_sem, recv_sem):
    n = x_ref.shape[0]
    me = lax.axis_index("chan")
    group = lax.axis_index("grp")

    barrier = pltpu.get_barrier_semaphore()
    for step in range(1, n):
        pl.semaphore_signal(barrier, inc=1, device_id=(group, lax.rem(me + step, n)),
                            device_id_type=pl.DeviceIdType.MESH)
    pl.semaphore_wait(barrier, n - 1)

    def copy(step, target, slot):
        return pltpu.make_async_remote_copy(
            src_ref=x_ref.at[target],
            dst_ref=out_ref.at[slot],
            send_sem=send_sem.at[step],
            recv_sem=recv_sem.at[step],
            device_id=(group, target),
            device_id_type=pl.DeviceIdType.MESH,
        )

    own = pltpu.make_async_copy(x_ref.at[me], out_ref.at[me], local_sem)
    own.start()
    for step in range(1, n):
        copy(step, lax.rem(me + step, n), me).start()

    fill_tables(cos_a, sin_a, cos_b, sin_b, weight, cos_out, sin_out)

    own.wait()
    for step in range(1, n):
        copy(step, lax.rem(me + step, n), me).wait_send()
        source = lax.rem(me + n - step, n)
        copy(step, source, source).wait_recv()


def spectra_exchange(x, factors, collective):
    n = x.shape[0]
    part = factors[4].shape[0]
    anywhere = pl.BlockSpec(memory_space=pl.ANY)
    vmem = pl.BlockSpec(memory_space=pltpu.VMEM)
    return pl.pallas_call(
        spectra_kernel,
        out_shape=(
            jax.ShapeDtypeStruct(x.shape, x.dtype),
            jax.ShapeDtypeStruct((part, LAGS), jnp.bfloat16),
            jax.ShapeDtypeStruct((part, LAGS), jnp.bfloat16),
        ),
        in_specs=[anywhere] + [vmem] * 5,
        out_specs=(anywhere, vmem, vmem),
        scratch_shapes=[
            pltpu.SemaphoreType.DMA(()),
            pltpu.SemaphoreType.DMA((n,)),
            pltpu.SemaphoreType.DMA((n,)),
        ],
        compiler_params=pltpu.CompilerParams(collective_id=collective, has_side_effects=True),
    )(x, *factors)


def local(spectra, pair_blocks, owners):
    groups_count = lax.axis_size("grp")
    chan_count = lax.axis_size("chan")
    slot_count = groups_count * MOST
    pairs = BLK * BLK
    part = F // chan_count
    me = lax.axis_index("chan")

    white = whiten(spectra)
    channels = white.shape[0]
    chunks = white.reshape(channels, WINDOWS, 2, chan_count, part).transpose(3, 0, 1, 2, 4)
    chunks = chunks.reshape(chan_count, channels * WINDOWS * 2, part)
    listed = pair_blocks[0, 0].reshape(-1).astype(jnp.bfloat16)
    extra = jnp.zeros((part,), jnp.bfloat16).at[: listed.shape[0]].set(listed)
    extra = jnp.broadcast_to(extra[None, None, :], (chan_count, 1, part))
    sent = jnp.concatenate([chunks, extra], axis=1)
    got, cos_part, sin_part = spectra_exchange(sent, table_factors(me * part, part), 2)
    rows_per = channels * WINDOWS * 2
    group_channels = chan_count * channels
    panel = got[:, :rows_per].reshape(group_channels, WINDOWS * 2 * part)
    all_blocks = got[:, rows_per, : NB_SRC * 2].astype(jnp.float32).astype(jnp.int32)
    all_blocks = all_blocks.reshape(chan_count * NB_SRC, 1, 2)
    offsets = jnp.arange(BLK, dtype=jnp.int32)
    left_ch = (all_blocks[:, :, 0] * BLK + offsets[None, :])[:, :, None] + jnp.zeros((1, 1, BLK), jnp.int32)
    right_ch = (all_blocks[:, :, 1] * BLK + offsets[None, :])[:, None, :] + jnp.zeros((1, BLK, 1), jnp.int32)
    channel_ids = jnp.arange(group_channels, dtype=jnp.int32)[None, :]
    left_hot = (left_ch.reshape(-1, 1) == channel_ids).astype(jnp.bfloat16)
    right_hot = (right_ch.reshape(-1, 1) == channel_ids).astype(jnp.bfloat16)

    gathered = pair_exchange(left_hot, right_hot, panel, cos_part, sin_part, chan_count, 0)
    corr = jnp.sum(gathered.astype(jnp.float32), axis=0).reshape(NB_SRC, pairs * LAGS)

    owner_list = owners[0, 0, :, 0]
    same = owner_list[:, None] == owner_list[None, :]
    earlier = jnp.arange(NB_SRC)[None, :] < jnp.arange(NB_SRC)[:, None]
    order_rank = jnp.sum(jnp.logical_and(same, earlier), axis=1)
    slot_ids = owner_list * MOST + order_rank
    chooser = slot_ids[None, :] == jnp.arange(slot_count, dtype=jnp.int32)[:, None]
    source = jnp.argmax(chooser, axis=1)
    filled = jnp.any(chooser, axis=1)
    placed = jnp.where(filled[:, None], jnp.take(corr, source, axis=0), 0.0)
    placed = placed.reshape(groups_count, 1, MOST, pairs, LAGS).astype(jnp.bfloat16)
    received = exchange(placed, "grp", "chan", True, 1, 1).astype(jnp.float32)
    return received.reshape(1, 1, slot_count, pairs, LAGS)


def solution(mesh):
    return jax.shard_map(
        local,
        mesh=mesh,
        in_specs=(
            P(("grp", "chan"), None, None, None),
            P("grp", "chan", None, None),
            P("grp", "chan", None, None),
        ),
        out_specs=P("grp", "chan", None, None, None),
        check_vma=False,
    )
```

```python
import functools

import jax
import jax.numpy as jnp
from jax import lax
from jax.experimental import pallas as pl
from jax.experimental.pallas import tpu as pltpu
from jax.sharding import PartitionSpec as P

F = 8192
LAGS = 1024
BLK = 2
NB_SRC = 18
MOST = 3
WINDOWS = 2
FINE = 128


def phase_angle(bins, lag_index):
    phase = bins[:, None] * lag_index[None, :] % (2 * F)
    return phase.astype(jnp.float32) * (jnp.pi / F)


def table_slice(start, count):
    lag_index = jnp.arange(LAGS, dtype=jnp.int32) - LAGS // 2
    coarse = phase_angle(start + FINE * jnp.arange(count // FINE, dtype=jnp.int32), lag_index)
    fine = phase_angle(jnp.arange(FINE, dtype=jnp.int32), lag_index)
    cos_a, sin_a = jnp.cos(coarse)[:, None, :], jnp.sin(coarse)[:, None, :]
    cos_b, sin_b = jnp.cos(fine)[None, :, :], jnp.sin(fine)[None, :, :]
    cos_ab = (cos_a * cos_b - sin_a * sin_b).reshape(count, LAGS)
    sin_ab = (sin_a * cos_b + cos_a * sin_b).reshape(count, LAGS)
    bins = start + jnp.arange(count, dtype=jnp.int32)
    weight = (jnp.where(bins == 0, 1.0, 2.0).astype(jnp.float32) / jnp.sqrt(jnp.float32(F)))[:, None]
    cos_part = (cos_ab * weight).astype(jnp.bfloat16)
    sin_part = (-sin_ab * weight).astype(jnp.bfloat16)
    return cos_part, sin_part


def whiten(spectra):
    values = spectra.astype(jnp.float32)
    power = values[:, :, 0] ** 2 + values[:, :, 1] ** 2
    level = jnp.mean(power, axis=-1, keepdims=True) + 1e-05
    scale = lax.rsqrt(power + 0.1 * level)
    return (values * scale[:, :, None, :]).astype(jnp.bfloat16)


def pair_rows(left_hot, right_hot, panel, cos_ref, sin_ref, target):
    part = cos_ref.shape[0]
    left = left_hot[target]
    right = right_hot[target]

    def rows_of(hot, window, kind):
        col = (window * 2 + kind) * part
        return jnp.dot(hot, panel[:, col:col + part], preferred_element_type=jnp.float32)

    real_sum = None
    imag_sum = None
    for window in range(WINDOWS):
        ra = rows_of(left, window, 0)
        ia = rows_of(left, window, 1)
        rb = rows_of(right, window, 0)
        ib = rows_of(right, window, 1)
        real = (ra * rb + ia * ib).astype(jnp.bfloat16).astype(jnp.float32)
        imag = (ia * rb - ra * ib).astype(jnp.bfloat16).astype(jnp.float32)
        real_sum = real if real_sum is None else real_sum + real
        imag_sum = imag if imag_sum is None else imag_sum + imag
    real_stack = (real_sum / WINDOWS).astype(jnp.bfloat16)
    imag_stack = (imag_sum / WINDOWS).astype(jnp.bfloat16)
    total = jnp.dot(real_stack, cos_ref[...], preferred_element_type=jnp.float32)
    return total + jnp.dot(imag_stack, sin_ref[...], preferred_element_type=jnp.float32)


def pair_exchange_kernel(left_hot, right_hot, panel, cos_ref, sin_ref, out_ref, slots, local_sem, send_sem, recv_sem):
    n = out_ref.shape[0]
    me = lax.axis_index("chan")
    group = lax.axis_index("grp")

    barrier = pltpu.get_barrier_semaphore()
    for step in range(1, n):
        pl.semaphore_signal(barrier, inc=1, device_id=(group, lax.rem(me + step, n)),
                            device_id_type=pl.DeviceIdType.MESH)
    pl.semaphore_wait(barrier, n - 1)

    def fill(target):
        slots[target] = pair_rows(left_hot, right_hot, panel, cos_ref, sin_ref, target).astype(slots.dtype)

    def send(step):
        target = lax.rem(me + step, n)
        return pltpu.make_async_remote_copy(
            src_ref=slots.at[target],
            dst_ref=out_ref.at[me],
            send_sem=send_sem.at[step],
            recv_sem=recv_sem.at[step],
            device_id=(group, target),
            device_id_type=pl.DeviceIdType.MESH,
        )

    def one_step(step, carry):
        fill(lax.rem(me + step, n))

        @pl.when(step > 1)
        def _():
            send(step - 1).start()

        return carry

    lax.fori_loop(1, n, one_step, 0)
    fill(me)
    send(n - 1).start()
    own = pltpu.make_async_copy(slots.at[me], out_ref.at[me], local_sem)
    own.start()
    own.wait()

    def finish(step, carry):
        send(step).wait_send()
        source = lax.rem(me + n - step, n)
        pltpu.make_async_remote_copy(
            src_ref=slots.at[source],
            dst_ref=out_ref.at[source],
            send_sem=send_sem.at[step],
            recv_sem=recv_sem.at[step],
            device_id=(group, source),
            device_id_type=pl.DeviceIdType.MESH,
        ).wait_recv()
        return carry

    lax.fori_loop(1, n, finish, 0)


def pair_exchange(left_hot, right_hot, panel, cos_part, sin_part, chan_count, collective):
    rows = left_hot.shape[0]
    count = rows // chan_count
    left_hot = left_hot.reshape(chan_count, count, -1)
    right_hot = right_hot.reshape(chan_count, count, -1)
    part = cos_part.shape[0]
    vmem = pl.BlockSpec(memory_space=pltpu.VMEM)
    flops = 2 * 2 * rows * panel.shape[0] * panel.shape[1] + 2 * 2 * rows * part * LAGS
    return pl.pallas_call(
        pair_exchange_kernel,
        out_shape=jax.ShapeDtypeStruct((chan_count, count, LAGS), jnp.bfloat16),
        in_specs=[vmem] * 5,
        out_specs=pl.BlockSpec(memory_space=pl.ANY),
        scratch_shapes=[
            pltpu.VMEM((chan_count, count, LAGS), jnp.bfloat16),
            pltpu.SemaphoreType.DMA(()),
            pltpu.SemaphoreType.DMA((chan_count,)),
            pltpu.SemaphoreType.DMA((chan_count,)),
        ],
        compiler_params=pltpu.CompilerParams(
            collective_id=collective, has_side_effects=True, vmem_limit_bytes=56 * 1024 * 1024
        ),
        cost_estimate=pl.CostEstimate(
            flops=flops,
            transcendentals=0,
            bytes_accessed=panel.size * 2 + 4 * part * LAGS + rows * LAGS * 2,
        ),
    )(left_hot, right_hot, panel, cos_part, sin_part)


def exchange_kernel(axis, other_axis, axis_first, stride, x_ref, out_ref, local_sem, send_sem, recv_sem):
    n = x_ref.shape[0]
    index = lax.axis_index(axis)
    me = lax.rem(index // stride, n)
    base = index - me * stride
    other = lax.axis_index(other_axis)

    def device(j):
        coord = base + stride * j
        return (coord, other) if axis_first else (other, coord)

    barrier = pltpu.get_barrier_semaphore()
    for step in range(1, n):
        pl.semaphore_signal(barrier, inc=1, device_id=device(lax.rem(me + step, n)),
                            device_id_type=pl.DeviceIdType.MESH)
    pl.semaphore_wait(barrier, n - 1)

    pieces = x_ref.shape[1]
    own = pltpu.make_async_copy(x_ref.at[me], out_ref.at[me], local_sem)
    own.start()
    copies = []
    for step in range(1, n):
        target = lax.rem(me + step, n)
        for piece in range(pieces):
            copy = pltpu.make_async_remote_copy(
                src_ref=x_ref.at[target, piece],
                dst_ref=out_ref.at[me, piece],
                send_sem=send_sem.at[step, piece],
                recv_sem=recv_sem.at[step, piece],
                device_id=device(target),
                device_id_type=pl.DeviceIdType.MESH,
            )
            copy.start()
            copies.append(copy)
    own.wait()
    for step in range(1, n):
        source = lax.rem(me + n - step, n)
        for piece in range(pieces):
            copies[(step - 1) * pieces + piece].wait_send()
            incoming = pltpu.make_async_remote_copy(
                src_ref=x_ref.at[source, piece],
                dst_ref=out_ref.at[source, piece],
                send_sem=send_sem.at[step, piece],
                recv_sem=recv_sem.at[step, piece],
                device_id=device(source),
                device_id_type=pl.DeviceIdType.MESH,
            )
            incoming.wait_recv()


def exchange(x, axis, other_axis, axis_first, stride, collective):
    n = x.shape[0]
    vmem = pl.BlockSpec(memory_space=pltpu.VMEM)
    return pl.pallas_call(
        functools.partial(exchange_kernel, axis, other_axis, axis_first, stride),
        out_shape=jax.ShapeDtypeStruct(x.shape, x.dtype),
        in_specs=[vmem],
        out_specs=vmem,
        scratch_shapes=[
            pltpu.SemaphoreType.DMA(()),
            pltpu.SemaphoreType.DMA((n, x.shape[1])),
            pltpu.SemaphoreType.DMA((n, x.shape[1])),
        ],
        compiler_params=pltpu.CompilerParams(collective_id=collective, has_side_effects=True),
    )(x)


def local(spectra, pair_blocks, owners):
    groups_count = lax.axis_size("grp")
    chan_count = lax.axis_size("chan")
    slot_count = groups_count * MOST
    pairs = BLK * BLK
    part = F // chan_count
    me = lax.axis_index("chan")

    white = whiten(spectra)
    channels = white.shape[0]
    chunks = white.reshape(channels, WINDOWS, 2, chan_count, part).transpose(3, 0, 1, 2, 4)
    chunks = chunks.reshape(chan_count, channels * WINDOWS * 2, part)
    listed = pair_blocks[0, 0].reshape(-1).astype(jnp.bfloat16)
    extra = jnp.zeros((part,), jnp.bfloat16).at[: listed.shape[0]].set(listed)
    extra = jnp.broadcast_to(extra[None, None, :], (chan_count, 1, part))
    sent = jnp.concatenate([chunks, extra], axis=1)
    got = lax.all_to_all(sent, "chan", split_axis=0, concat_axis=0, tiled=True)
    rows_per = channels * WINDOWS * 2
    group_channels = chan_count * channels
    panel = got[:, :rows_per].reshape(group_channels, WINDOWS * 2 * part)
    all_blocks = got[:, rows_per, : NB_SRC * 2].astype(jnp.float32).astype(jnp.int32)
    all_blocks = all_blocks.reshape(chan_count * NB_SRC, 1, 2)
    offsets = jnp.arange(BLK, dtype=jnp.int32)
    left_ch = (all_blocks[:, :, 0] * BLK + offsets[None, :])[:, :, None] + jnp.zeros((1, 1, BLK), jnp.int32)
    right_ch = (all_blocks[:, :, 1] * BLK + offsets[None, :])[:, None, :] + jnp.zeros((1, BLK, 1), jnp.int32)
    channel_ids = jnp.arange(group_channels, dtype=jnp.int32)[None, :]
    left_hot = (left_ch.reshape(-1, 1) == channel_ids).astype(jnp.bfloat16)
    right_hot = (right_ch.reshape(-1, 1) == channel_ids).astype(jnp.bfloat16)

    cos_part, sin_part = table_slice(me * part, part)
    gathered = pair_exchange(left_hot, right_hot, panel, cos_part, sin_part, chan_count, 0)
    corr = jnp.sum(gathered.astype(jnp.float32), axis=0).reshape(NB_SRC, pairs * LAGS)

    owner_list = owners[0, 0, :, 0]
    same = owner_list[:, None] == owner_list[None, :]
    earlier = jnp.arange(NB_SRC)[None, :] < jnp.arange(NB_SRC)[:, None]
    order_rank = jnp.sum(jnp.logical_and(same, earlier), axis=1)
    slot_ids = owner_list * MOST + order_rank
    chooser = slot_ids[None, :] == jnp.arange(slot_count, dtype=jnp.int32)[:, None]
    source = jnp.argmax(chooser, axis=1)
    filled = jnp.any(chooser, axis=1)
    placed = jnp.where(filled[:, None], jnp.take(corr, source, axis=0), 0.0)
    placed = placed.reshape(groups_count, 1, MOST, pairs, LAGS).astype(jnp.bfloat16)
    received = lax.all_to_all(placed, "grp", split_axis=0, concat_axis=0, tiled=True).astype(jnp.float32)
    return received.reshape(1, 1, slot_count, pairs, LAGS)


def solution(mesh):
    return jax.shard_map(
        local,
        mesh=mesh,
        in_specs=(
            P(("grp", "chan"), None, None, None),
            P("grp", "chan", None, None),
            P("grp", "chan", None, None),
        ),
        out_specs=P("grp", "chan", None, None, None),
        check_vma=False,
    )
```

```python
import functools

import jax
import jax.numpy as jnp
from jax import lax
from jax.experimental import pallas as pl
from jax.experimental.pallas import tpu as pltpu
from jax.sharding import PartitionSpec as P

F = 8192
LAGS = 1024
BLK = 2
NB_SRC = 18
MOST = 3
WINDOWS = 2
FINE = 128


def phase_angle(bins, lag_index):
    phase = bins[:, None] * lag_index[None, :] % (2 * F)
    return phase.astype(jnp.float32) * (jnp.pi / F)


def table_slice(start, count):
    lag_index = jnp.arange(LAGS, dtype=jnp.int32) - LAGS // 2
    coarse = phase_angle(start + FINE * jnp.arange(count // FINE, dtype=jnp.int32), lag_index)
    fine = phase_angle(jnp.arange(FINE, dtype=jnp.int32), lag_index)
    cos_a, sin_a = jnp.cos(coarse)[:, None, :], jnp.sin(coarse)[:, None, :]
    cos_b, sin_b = jnp.cos(fine)[None, :, :], jnp.sin(fine)[None, :, :]
    cos_ab = (cos_a * cos_b - sin_a * sin_b).reshape(count, LAGS)
    sin_ab = (sin_a * cos_b + cos_a * sin_b).reshape(count, LAGS)
    bins = start + jnp.arange(count, dtype=jnp.int32)
    weight = (jnp.where(bins == 0, 1.0, 2.0).astype(jnp.float32) / jnp.sqrt(jnp.float32(F)))[:, None]
    cos_part = (cos_ab * weight).astype(jnp.bfloat16)
    sin_part = (-sin_ab * weight).astype(jnp.bfloat16)
    return cos_part, sin_part


def whiten(spectra):
    values = spectra.astype(jnp.float32)
    power = values[:, :, 0] ** 2 + values[:, :, 1] ** 2
    level = jnp.mean(power, axis=-1, keepdims=True) + 1e-05
    scale = lax.rsqrt(power + 0.1 * level)
    return (values * scale[:, :, None, :]).astype(jnp.bfloat16)


def pair_rows(left_hot, right_hot, panel, cos_ref, sin_ref, target):
    part = cos_ref.shape[0]
    left = left_hot[target]
    right = right_hot[target]

    def rows_of(hot, window, kind):
        col = (window * 2 + kind) * part
        return jnp.dot(hot, panel[:, col:col + part], preferred_element_type=jnp.float32)

    real_sum = None
    imag_sum = None
    for window in range(WINDOWS):
        ra = rows_of(left, window, 0)
        ia = rows_of(left, window, 1)
        rb = rows_of(right, window, 0)
        ib = rows_of(right, window, 1)
        real = (ra * rb + ia * ib).astype(jnp.bfloat16).astype(jnp.float32)
        imag = (ia * rb - ra * ib).astype(jnp.bfloat16).astype(jnp.float32)
        real_sum = real if real_sum is None else real_sum + real
        imag_sum = imag if imag_sum is None else imag_sum + imag
    real_stack = (real_sum / WINDOWS).astype(jnp.bfloat16)
    imag_stack = (imag_sum / WINDOWS).astype(jnp.bfloat16)
    total = jnp.dot(real_stack, cos_ref[...], preferred_element_type=jnp.float32)
    return total + jnp.dot(imag_stack, sin_ref[...], preferred_element_type=jnp.float32)


def pair_exchange_kernel(left_hot, right_hot, panel, cos_ref, sin_ref, out_ref, slots, local_sem, send_sem, recv_sem):
    n = out_ref.shape[0]
    me = lax.axis_index("chan")
    group = lax.axis_index("grp")

    barrier = pltpu.get_barrier_semaphore()
    for step in range(1, n):
        pl.semaphore_signal(barrier, inc=1, device_id=(group, lax.rem(me + step, n)),
                            device_id_type=pl.DeviceIdType.MESH)
    pl.semaphore_wait(barrier, n - 1)

    def fill(target):
        slots[target] = pair_rows(left_hot, right_hot, panel, cos_ref, sin_ref, target).astype(slots.dtype)

    def send(step):
        target = lax.rem(me + step, n)
        return pltpu.make_async_remote_copy(
            src_ref=slots.at[target],
            dst_ref=out_ref.at[me],
            send_sem=send_sem.at[step],
            recv_sem=recv_sem.at[step],
            device_id=(group, target),
            device_id_type=pl.DeviceIdType.MESH,
        )

    def one_step(step, carry):
        fill(lax.rem(me + step, n))

        @pl.when(step > 1)
        def _():
            send(step - 1).start()

        return carry

    lax.fori_loop(1, n, one_step, 0)
    fill(me)
    send(n - 1).start()
    own = pltpu.make_async_copy(slots.at[me], out_ref.at[me], local_sem)
    own.start()
    own.wait()

    def finish(step, carry):
        send(step).wait_send()
        source = lax.rem(me + n - step, n)
        pltpu.make_async_remote_copy(
            src_ref=slots.at[source],
            dst_ref=out_ref.at[source],
            send_sem=send_sem.at[step],
            recv_sem=recv_sem.at[step],
            device_id=(group, source),
            device_id_type=pl.DeviceIdType.MESH,
        ).wait_recv()
        return carry

    lax.fori_loop(1, n, finish, 0)


def pair_exchange(left_hot, right_hot, panel, cos_part, sin_part, chan_count, collective):
    rows = left_hot.shape[0]
    count = rows // chan_count
    left_hot = left_hot.reshape(chan_count, count, -1)
    right_hot = right_hot.reshape(chan_count, count, -1)
    part = cos_part.shape[0]
    vmem = pl.BlockSpec(memory_space=pltpu.VMEM)
    flops = 2 * 2 * rows * panel.shape[0] * panel.shape[1] + 2 * 2 * rows * part * LAGS
    return pl.pallas_call(
        pair_exchange_kernel,
        out_shape=jax.ShapeDtypeStruct((chan_count, count, LAGS), jnp.bfloat16),
        in_specs=[vmem] * 5,
        out_specs=pl.BlockSpec(memory_space=pl.ANY),
        scratch_shapes=[
            pltpu.VMEM((chan_count, count, LAGS), jnp.bfloat16),
            pltpu.SemaphoreType.DMA(()),
            pltpu.SemaphoreType.DMA((chan_count,)),
            pltpu.SemaphoreType.DMA((chan_count,)),
        ],
        compiler_params=pltpu.CompilerParams(
            collective_id=collective, has_side_effects=True, vmem_limit_bytes=56 * 1024 * 1024
        ),
        cost_estimate=pl.CostEstimate(
            flops=flops,
            transcendentals=0,
            bytes_accessed=panel.size * 2 + 4 * part * LAGS + rows * LAGS * 2,
        ),
    )(left_hot, right_hot, panel, cos_part, sin_part)


def exchange_kernel(axis, other_axis, axis_first, stride, x_ref, out_ref, local_sem, send_sem, recv_sem):
    n = x_ref.shape[0]
    index = lax.axis_index(axis)
    me = lax.rem(index // stride, n)
    base = index - me * stride
    other = lax.axis_index(other_axis)

    def device(j):
        coord = base + stride * j
        return (coord, other) if axis_first else (other, coord)

    barrier = pltpu.get_barrier_semaphore()
    for step in range(1, n):
        pl.semaphore_signal(barrier, inc=1, device_id=device(lax.rem(me + step, n)),
                            device_id_type=pl.DeviceIdType.MESH)
    pl.semaphore_wait(barrier, n - 1)

    pieces = x_ref.shape[1]
    own = pltpu.make_async_copy(x_ref.at[me], out_ref.at[me], local_sem)
    own.start()
    copies = []
    for step in range(1, n):
        target = lax.rem(me + step, n)
        for piece in range(pieces):
            copy = pltpu.make_async_remote_copy(
                src_ref=x_ref.at[target, piece],
                dst_ref=out_ref.at[me, piece],
                send_sem=send_sem.at[step, piece],
                recv_sem=recv_sem.at[step, piece],
                device_id=device(target),
                device_id_type=pl.DeviceIdType.MESH,
            )
            copy.start()
            copies.append(copy)
    own.wait()
    for step in range(1, n):
        source = lax.rem(me + n - step, n)
        for piece in range(pieces):
            copies[(step - 1) * pieces + piece].wait_send()
            incoming = pltpu.make_async_remote_copy(
                src_ref=x_ref.at[source, piece],
                dst_ref=out_ref.at[source, piece],
                send_sem=send_sem.at[step, piece],
                recv_sem=recv_sem.at[step, piece],
                device_id=device(source),
                device_id_type=pl.DeviceIdType.MESH,
            )
            incoming.wait_recv()


def exchange(x, axis, other_axis, axis_first, stride, collective):
    n = x.shape[0]
    vmem = pl.BlockSpec(memory_space=pltpu.VMEM)
    return pl.pallas_call(
        functools.partial(exchange_kernel, axis, other_axis, axis_first, stride),
        out_shape=jax.ShapeDtypeStruct(x.shape, x.dtype),
        in_specs=[vmem],
        out_specs=vmem,
        scratch_shapes=[
            pltpu.SemaphoreType.DMA(()),
            pltpu.SemaphoreType.DMA((n, x.shape[1])),
            pltpu.SemaphoreType.DMA((n, x.shape[1])),
        ],
        compiler_params=pltpu.CompilerParams(collective_id=collective, has_side_effects=True),
    )(x)


def local(spectra, pair_blocks, owners):
    groups_count = lax.axis_size("grp")
    chan_count = lax.axis_size("chan")
    slot_count = groups_count * MOST
    pairs = BLK * BLK
    part = F // chan_count
    me = lax.axis_index("chan")

    white = whiten(spectra)
    channels = white.shape[0]
    chunks = white.reshape(channels, WINDOWS, 2, chan_count, part).transpose(3, 0, 1, 2, 4)
    chunks = chunks.reshape(chan_count, channels * WINDOWS * 2, part)
    listed = pair_blocks[0, 0].reshape(-1).astype(jnp.bfloat16)
    extra = jnp.zeros((part,), jnp.bfloat16).at[: listed.shape[0]].set(listed)
    extra = jnp.broadcast_to(extra[None, None, :], (chan_count, 1, part))
    sent = jnp.concatenate([chunks, extra], axis=1)
    got = lax.all_to_all(sent, "chan", split_axis=0, concat_axis=0, tiled=True)
    rows_per = channels * WINDOWS * 2
    group_channels = chan_count * channels
    panel = got[:, :rows_per].reshape(group_channels, WINDOWS * 2 * part)
    all_blocks = got[:, rows_per, : NB_SRC * 2].astype(jnp.float32).astype(jnp.int32)
    all_blocks = all_blocks.reshape(chan_count * NB_SRC, 1, 2)
    offsets = jnp.arange(BLK, dtype=jnp.int32)
    left_ch = (all_blocks[:, :, 0] * BLK + offsets[None, :])[:, :, None] + jnp.zeros((1, 1, BLK), jnp.int32)
    right_ch = (all_blocks[:, :, 1] * BLK + offsets[None, :])[:, None, :] + jnp.zeros((1, BLK, 1), jnp.int32)
    channel_ids = jnp.arange(group_channels, dtype=jnp.int32)[None, :]
    left_hot = (left_ch.reshape(-1, 1) == channel_ids).astype(jnp.bfloat16)
    right_hot = (right_ch.reshape(-1, 1) == channel_ids).astype(jnp.bfloat16)

    cos_part, sin_part = table_slice(me * part, part)
    gathered = pair_exchange(left_hot, right_hot, panel, cos_part, sin_part, chan_count, 0)
    owner_list = owners[0, 0, :, 0]
    same = owner_list[:, None] == owner_list[None, :]
    earlier = jnp.arange(NB_SRC)[None, :] < jnp.arange(NB_SRC)[:, None]
    order_rank = jnp.sum(jnp.logical_and(same, earlier), axis=1)
    slot_ids = owner_list * MOST + order_rank
    chooser = (slot_ids[None, :] == jnp.arange(slot_count, dtype=jnp.int32)[:, None]).astype(jnp.bfloat16)
    chooser = jnp.tile(chooser, (1, chan_count))
    gathered = gathered.reshape(chan_count * NB_SRC, pairs * LAGS)
    placed = jnp.dot(chooser, gathered, preferred_element_type=jnp.float32)
    placed = placed.reshape(groups_count, 1, MOST, pairs, LAGS).astype(jnp.bfloat16)
    received = exchange(placed, "grp", "chan", True, 1, 1).astype(jnp.float32)
    return received.reshape(1, 1, slot_count, pairs, LAGS)


def solution(mesh):
    return jax.shard_map(
        local,
        mesh=mesh,
        in_specs=(
            P(("grp", "chan"), None, None, None),
            P("grp", "chan", None, None),
            P("grp", "chan", None, None),
        ),
        out_specs=P("grp", "chan", None, None, None),
        check_vma=False,
    )
```

```python
import functools

import jax
import jax.numpy as jnp
from jax import lax
from jax.experimental import pallas as pl
from jax.experimental.pallas import tpu as pltpu
from jax.sharding import PartitionSpec as P

F = 8192
LAGS = 1024
BLK = 2
NB_SRC = 18
MOST = 3
WINDOWS = 2
FINE = 128
EXTRA_ROWS = 16


def phase_angle(bins, lag_index):
    phase = bins[:, None] * lag_index[None, :] % (2 * F)
    return phase.astype(jnp.float32) * (jnp.pi / F)


def table_slice(start, count):
    lag_index = jnp.arange(LAGS, dtype=jnp.int32) - LAGS // 2
    coarse = phase_angle(start + FINE * jnp.arange(count // FINE, dtype=jnp.int32), lag_index)
    fine = phase_angle(jnp.arange(FINE, dtype=jnp.int32), lag_index)
    cos_a, sin_a = jnp.cos(coarse)[:, None, :], jnp.sin(coarse)[:, None, :]
    cos_b, sin_b = jnp.cos(fine)[None, :, :], jnp.sin(fine)[None, :, :]
    cos_ab = (cos_a * cos_b - sin_a * sin_b).reshape(count, LAGS)
    sin_ab = (sin_a * cos_b + cos_a * sin_b).reshape(count, LAGS)
    bins = start + jnp.arange(count, dtype=jnp.int32)
    weight = (jnp.where(bins == 0, 1.0, 2.0).astype(jnp.float32) / jnp.sqrt(jnp.float32(F)))[:, None]
    cos_part = (cos_ab * weight).astype(jnp.bfloat16)
    sin_part = (-sin_ab * weight).astype(jnp.bfloat16)
    return cos_part, sin_part


def whiten_kernel(x_ref, extra_ref, out_ref):
    x = x_ref[...].astype(jnp.float32)
    rows = x.shape[0]
    square = x * x
    after = pltpu.roll(square, rows - 1, 0)
    before = pltpu.roll(square, 1, 0)
    odd = lax.broadcasted_iota(jnp.int32, x.shape, 0) % 2 == 1
    power = jnp.where(odd, before + square, square + after)
    level = jnp.mean(power, axis=-1, keepdims=True) + 1e-05
    white = (x * lax.rsqrt(power + 0.1 * level)).astype(out_ref.dtype)
    part = out_ref.shape[2]
    for chunk in range(out_ref.shape[0]):
        out_ref[chunk, :rows, :] = white[:, chunk * part:(chunk + 1) * part]
        out_ref[chunk, rows:, :] = extra_ref[...]


def whiten_chunks(spectra, extra, chan_count):
    channels = spectra.shape[0]
    rows = channels * WINDOWS * 2
    x = spectra.reshape(rows, F)
    vmem = pl.BlockSpec(memory_space=pltpu.VMEM)
    return pl.pallas_call(
        whiten_kernel,
        out_shape=jax.ShapeDtypeStruct((chan_count, rows + extra.shape[0], F // chan_count), jnp.bfloat16),
        in_specs=[vmem, vmem],
        out_specs=vmem,
        compiler_params=pltpu.CompilerParams(vmem_limit_bytes=48 * 1024 * 1024),
        cost_estimate=pl.CostEstimate(flops=8 * rows * F, transcendentals=rows * F, bytes_accessed=4 * rows * F),
    )(x, extra)


def pair_rows(left_hot, right_hot, panel, cos_ref, sin_ref, target):
    part = cos_ref.shape[0]
    left = left_hot[target]
    right = right_hot[target]

    def rows_of(hot, window, kind):
        col = (window * 2 + kind) * part
        return jnp.dot(hot, panel[:, col:col + part], preferred_element_type=jnp.float32)

    real_sum = None
    imag_sum = None
    for window in range(WINDOWS):
        ra = rows_of(left, window, 0)
        ia = rows_of(left, window, 1)
        rb = rows_of(right, window, 0)
        ib = rows_of(right, window, 1)
        real = (ra * rb + ia * ib).astype(jnp.bfloat16).astype(jnp.float32)
        imag = (ia * rb - ra * ib).astype(jnp.bfloat16).astype(jnp.float32)
        real_sum = real if real_sum is None else real_sum + real
        imag_sum = imag if imag_sum is None else imag_sum + imag
    real_stack = (real_sum / WINDOWS).astype(jnp.bfloat16)
    imag_stack = (imag_sum / WINDOWS).astype(jnp.bfloat16)
    total = jnp.dot(real_stack, cos_ref[...], preferred_element_type=jnp.float32)
    return total + jnp.dot(imag_stack, sin_ref[...], preferred_element_type=jnp.float32)


def pair_exchange_kernel(left_hot, right_hot, panel, cos_ref, sin_ref, out_ref, slots, local_sem, send_sem, recv_sem):
    n = out_ref.shape[0]
    me = lax.axis_index("chan")
    group = lax.axis_index("grp")

    barrier = pltpu.get_barrier_semaphore()
    for step in range(1, n):
        pl.semaphore_signal(barrier, inc=1, device_id=(group, lax.rem(me + step, n)),
                            device_id_type=pl.DeviceIdType.MESH)
    pl.semaphore_wait(barrier, n - 1)

    def fill(target):
        slots[target] = pair_rows(left_hot, right_hot, panel, cos_ref, sin_ref, target).astype(slots.dtype)

    def send(step):
        target = lax.rem(me + step, n)
        return pltpu.make_async_remote_copy(
            src_ref=slots.at[target],
            dst_ref=out_ref.at[me],
            send_sem=send_sem.at[step],
            recv_sem=recv_sem.at[step],
            device_id=(group, target),
            device_id_type=pl.DeviceIdType.MESH,
        )

    def one_step(step, carry):
        fill(lax.rem(me + step, n))

        @pl.when(step > 1)
        def _():
            send(step - 1).start()

        return carry

    lax.fori_loop(1, n, one_step, 0)
    fill(me)
    send(n - 1).start()
    own = pltpu.make_async_copy(slots.at[me], out_ref.at[me], local_sem)
    own.start()
    own.wait()

    def finish(step, carry):
        send(step).wait_send()
        source = lax.rem(me + n - step, n)
        pltpu.make_async_remote_copy(
            src_ref=slots.at[source],
            dst_ref=out_ref.at[source],
            send_sem=send_sem.at[step],
            recv_sem=recv_sem.at[step],
            device_id=(group, source),
            device_id_type=pl.DeviceIdType.MESH,
        ).wait_recv()
        return carry

    lax.fori_loop(1, n, finish, 0)


def pair_exchange(left_hot, right_hot, panel, cos_part, sin_part, chan_count, collective):
    rows = left_hot.shape[0]
    count = rows // chan_count
    left_hot = left_hot.reshape(chan_count, count, -1)
    right_hot = right_hot.reshape(chan_count, count, -1)
    part = cos_part.shape[0]
    vmem = pl.BlockSpec(memory_space=pltpu.VMEM)
    flops = 2 * 2 * rows * panel.shape[0] * panel.shape[1] + 2 * 2 * rows * part * LAGS
    return pl.pallas_call(
        pair_exchange_kernel,
        out_shape=jax.ShapeDtypeStruct((chan_count, count, LAGS), jnp.bfloat16),
        in_specs=[vmem] * 5,
        out_specs=pl.BlockSpec(memory_space=pl.ANY),
        scratch_shapes=[
            pltpu.VMEM((chan_count, count, LAGS), jnp.bfloat16),
            pltpu.SemaphoreType.DMA(()),
            pltpu.SemaphoreType.DMA((chan_count,)),
            pltpu.SemaphoreType.DMA((chan_count,)),
        ],
        compiler_params=pltpu.CompilerParams(
            collective_id=collective, has_side_effects=True, vmem_limit_bytes=56 * 1024 * 1024
        ),
        cost_estimate=pl.CostEstimate(
            flops=flops,
            transcendentals=0,
            bytes_accessed=panel.size * 2 + 4 * part * LAGS + rows * LAGS * 2,
        ),
    )(left_hot, right_hot, panel, cos_part, sin_part)


def exchange_kernel(axis, other_axis, axis_first, stride, x_ref, out_ref, local_sem, send_sem, recv_sem):
    n = x_ref.shape[0]
    index = lax.axis_index(axis)
    me = lax.rem(index // stride, n)
    base = index - me * stride
    other = lax.axis_index(other_axis)

    def device(j):
        coord = base + stride * j
        return (coord, other) if axis_first else (other, coord)

    barrier = pltpu.get_barrier_semaphore()
    for step in range(1, n):
        pl.semaphore_signal(barrier, inc=1, device_id=device(lax.rem(me + step, n)),
                            device_id_type=pl.DeviceIdType.MESH)
    pl.semaphore_wait(barrier, n - 1)

    pieces = x_ref.shape[1]
    own = pltpu.make_async_copy(x_ref.at[me], out_ref.at[me], local_sem)
    own.start()
    copies = []
    for step in range(1, n):
        target = lax.rem(me + step, n)
        for piece in range(pieces):
            copy = pltpu.make_async_remote_copy(
                src_ref=x_ref.at[target, piece],
                dst_ref=out_ref.at[me, piece],
                send_sem=send_sem.at[step, piece],
                recv_sem=recv_sem.at[step, piece],
                device_id=device(target),
                device_id_type=pl.DeviceIdType.MESH,
            )
            copy.start()
            copies.append(copy)
    own.wait()
    for step in range(1, n):
        source = lax.rem(me + n - step, n)
        for piece in range(pieces):
            copies[(step - 1) * pieces + piece].wait_send()
            incoming = pltpu.make_async_remote_copy(
                src_ref=x_ref.at[source, piece],
                dst_ref=out_ref.at[source, piece],
                send_sem=send_sem.at[step, piece],
                recv_sem=recv_sem.at[step, piece],
                device_id=device(source),
                device_id_type=pl.DeviceIdType.MESH,
            )
            incoming.wait_recv()


def exchange(x, axis, other_axis, axis_first, stride, collective):
    n = x.shape[0]
    vmem = pl.BlockSpec(memory_space=pltpu.VMEM)
    return pl.pallas_call(
        functools.partial(exchange_kernel, axis, other_axis, axis_first, stride),
        out_shape=jax.ShapeDtypeStruct(x.shape, x.dtype),
        in_specs=[vmem],
        out_specs=vmem,
        scratch_shapes=[
            pltpu.SemaphoreType.DMA(()),
            pltpu.SemaphoreType.DMA((n, x.shape[1])),
            pltpu.SemaphoreType.DMA((n, x.shape[1])),
        ],
        compiler_params=pltpu.CompilerParams(collective_id=collective, has_side_effects=True),
    )(x)


def local(spectra, pair_blocks, owners):
    groups_count = lax.axis_size("grp")
    chan_count = lax.axis_size("chan")
    slot_count = groups_count * MOST
    pairs = BLK * BLK
    part = F // chan_count
    me = lax.axis_index("chan")

    channels = spectra.shape[0]
    listed = pair_blocks[0, 0].reshape(-1).astype(jnp.bfloat16)
    extra = jnp.zeros((EXTRA_ROWS, part), jnp.bfloat16).at[0, : listed.shape[0]].set(listed)
    sent = whiten_chunks(spectra, extra, chan_count)
    got = lax.all_to_all(sent, "chan", split_axis=0, concat_axis=0, tiled=True)
    rows_per = channels * WINDOWS * 2
    group_channels = chan_count * channels
    panel = got[:, :rows_per].reshape(group_channels, WINDOWS * 2 * part)
    all_blocks = got[:, rows_per, : NB_SRC * 2].astype(jnp.float32).astype(jnp.int32)
    all_blocks = all_blocks.reshape(chan_count * NB_SRC, 1, 2)
    offsets = jnp.arange(BLK, dtype=jnp.int32)
    left_ch = (all_blocks[:, :, 0] * BLK + offsets[None, :])[:, :, None] + jnp.zeros((1, 1, BLK), jnp.int32)
    right_ch = (all_blocks[:, :, 1] * BLK + offsets[None, :])[:, None, :] + jnp.zeros((1, BLK, 1), jnp.int32)
    channel_ids = jnp.arange(group_channels, dtype=jnp.int32)[None, :]
    left_hot = (left_ch.reshape(-1, 1) == channel_ids).astype(jnp.bfloat16)
    right_hot = (right_ch.reshape(-1, 1) == channel_ids).astype(jnp.bfloat16)

    cos_part, sin_part = table_slice(me * part, part)
    gathered = pair_exchange(left_hot, right_hot, panel, cos_part, sin_part, chan_count, 0)
    corr = jnp.sum(gathered.astype(jnp.float32), axis=0).reshape(NB_SRC, pairs * LAGS)

    owner_list = owners[0, 0, :, 0]
    same = owner_list[:, None] == owner_list[None, :]
    earlier = jnp.arange(NB_SRC)[None, :] < jnp.arange(NB_SRC)[:, None]
    order_rank = jnp.sum(jnp.logical_and(same, earlier), axis=1)
    slot_ids = owner_list * MOST + order_rank
    chooser = slot_ids[None, :] == jnp.arange(slot_count, dtype=jnp.int32)[:, None]
    source = jnp.argmax(chooser, axis=1)
    filled = jnp.any(chooser, axis=1)
    placed = jnp.where(filled[:, None], jnp.take(corr, source, axis=0), 0.0)
    placed = placed.reshape(groups_count, 1, MOST, pairs, LAGS).astype(jnp.bfloat16)
    received = exchange(placed, "grp", "chan", True, 1, 1).astype(jnp.float32)
    return received.reshape(1, 1, slot_count, pairs, LAGS)


def solution(mesh):
    return jax.shard_map(
        local,
        mesh=mesh,
        in_specs=(
            P(("grp", "chan"), None, None, None),
            P("grp", "chan", None, None),
            P("grp", "chan", None, None),
        ),
        out_specs=P("grp", "chan", None, None, None),
        check_vma=False,
    )
```

```python
import functools

import jax
import jax.numpy as jnp
from jax import lax
from jax.experimental import pallas as pl
from jax.experimental.pallas import tpu as pltpu
from jax.sharding import PartitionSpec as P

F = 8192
LAGS = 1024
BLK = 2
NB_SRC = 18
MOST = 3
WINDOWS = 2
FINE = 128
EXTRA_ROWS = 1


def phase_angle(bins, lag_index):
    phase = bins[:, None] * lag_index[None, :] % (2 * F)
    return phase.astype(jnp.float32) * (jnp.pi / F)


def table_slice(start, count):
    lag_index = jnp.arange(LAGS, dtype=jnp.int32) - LAGS // 2
    coarse = phase_angle(start + FINE * jnp.arange(count // FINE, dtype=jnp.int32), lag_index)
    fine = phase_angle(jnp.arange(FINE, dtype=jnp.int32), lag_index)
    cos_a, sin_a = jnp.cos(coarse)[:, None, :], jnp.sin(coarse)[:, None, :]
    cos_b, sin_b = jnp.cos(fine)[None, :, :], jnp.sin(fine)[None, :, :]
    cos_ab = (cos_a * cos_b - sin_a * sin_b).reshape(count, LAGS)
    sin_ab = (sin_a * cos_b + cos_a * sin_b).reshape(count, LAGS)
    bins = start + jnp.arange(count, dtype=jnp.int32)
    weight = (jnp.where(bins == 0, 1.0, 2.0).astype(jnp.float32) / jnp.sqrt(jnp.float32(F)))[:, None]
    cos_part = (cos_ab * weight).astype(jnp.bfloat16)
    sin_part = (-sin_ab * weight).astype(jnp.bfloat16)
    return cos_part, sin_part


def whiten_kernel(x_ref, extra_ref, out_ref):
    x = x_ref[...].astype(jnp.float32)
    rows = x.shape[0]
    square = x * x
    after = pltpu.roll(square, rows - 1, 0)
    before = pltpu.roll(square, 1, 0)
    odd = lax.broadcasted_iota(jnp.int32, x.shape, 0) % 2 == 1
    power = jnp.where(odd, before + square, square + after)
    level = jnp.mean(power, axis=-1, keepdims=True) + 1e-05
    white = (x * lax.rsqrt(power + 0.1 * level)).astype(out_ref.dtype)
    part = out_ref.shape[2]
    for chunk in range(out_ref.shape[0]):
        out_ref[chunk, :rows, :] = white[:, chunk * part:(chunk + 1) * part]
        out_ref[chunk, rows:, :] = extra_ref[...]


def whiten_chunks(spectra, extra, chan_count):
    channels = spectra.shape[0]
    rows = channels * WINDOWS * 2
    x = spectra.reshape(rows, F)
    vmem = pl.BlockSpec(memory_space=pltpu.VMEM)
    return pl.pallas_call(
        whiten_kernel,
        out_shape=jax.ShapeDtypeStruct((chan_count, rows + extra.shape[0], F // chan_count), jnp.bfloat16),
        in_specs=[vmem, vmem],
        out_specs=vmem,
        compiler_params=pltpu.CompilerParams(vmem_limit_bytes=48 * 1024 * 1024),
        cost_estimate=pl.CostEstimate(flops=8 * rows * F, transcendentals=rows * F, bytes_accessed=4 * rows * F),
    )(x, extra)


def pair_rows(left_hot, right_hot, panel, cos_ref, sin_ref, target):
    part = cos_ref.shape[0]
    left = left_hot[target]
    right = right_hot[target]

    def rows_of(hot, window, kind):
        col = (window * 2 + kind) * part
        return jnp.dot(hot, panel[:, col:col + part], preferred_element_type=jnp.float32)

    real_sum = None
    imag_sum = None
    for window in range(WINDOWS):
        ra = rows_of(left, window, 0)
        ia = rows_of(left, window, 1)
        rb = rows_of(right, window, 0)
        ib = rows_of(right, window, 1)
        real = (ra * rb + ia * ib).astype(jnp.bfloat16).astype(jnp.float32)
        imag = (ia * rb - ra * ib).astype(jnp.bfloat16).astype(jnp.float32)
        real_sum = real if real_sum is None else real_sum + real
        imag_sum = imag if imag_sum is None else imag_sum + imag
    real_stack = (real_sum / WINDOWS).astype(jnp.bfloat16)
    imag_stack = (imag_sum / WINDOWS).astype(jnp.bfloat16)
    total = jnp.dot(real_stack, cos_ref[...], preferred_element_type=jnp.float32)
    return total + jnp.dot(imag_stack, sin_ref[...], preferred_element_type=jnp.float32)


def pair_exchange_kernel(left_hot, right_hot, panel, cos_ref, sin_ref, out_ref, slots, local_sem, send_sem, recv_sem):
    n = out_ref.shape[0]
    me = lax.axis_index("chan")
    group = lax.axis_index("grp")

    barrier = pltpu.get_barrier_semaphore()
    for step in range(1, n):
        pl.semaphore_signal(barrier, inc=1, device_id=(group, lax.rem(me + step, n)),
                            device_id_type=pl.DeviceIdType.MESH)
    pl.semaphore_wait(barrier, n - 1)

    def fill(target):
        slots[target] = pair_rows(left_hot, right_hot, panel, cos_ref, sin_ref, target).astype(slots.dtype)

    def send(step):
        target = lax.rem(me + step, n)
        return pltpu.make_async_remote_copy(
            src_ref=slots.at[target],
            dst_ref=out_ref.at[me],
            send_sem=send_sem.at[step],
            recv_sem=recv_sem.at[step],
            device_id=(group, target),
            device_id_type=pl.DeviceIdType.MESH,
        )

    def one_step(step, carry):
        fill(lax.rem(me + step, n))

        @pl.when(step > 1)
        def _():
            send(step - 1).start()

        return carry

    lax.fori_loop(1, n, one_step, 0)
    fill(me)
    send(n - 1).start()
    own = pltpu.make_async_copy(slots.at[me], out_ref.at[me], local_sem)
    own.start()
    own.wait()

    def finish(step, carry):
        send(step).wait_send()
        source = lax.rem(me + n - step, n)
        pltpu.make_async_remote_copy(
            src_ref=slots.at[source],
            dst_ref=out_ref.at[source],
            send_sem=send_sem.at[step],
            recv_sem=recv_sem.at[step],
            device_id=(group, source),
            device_id_type=pl.DeviceIdType.MESH,
        ).wait_recv()
        return carry

    lax.fori_loop(1, n, finish, 0)


def pair_exchange(left_hot, right_hot, panel, cos_part, sin_part, chan_count, collective):
    rows = left_hot.shape[0]
    count = rows // chan_count
    left_hot = left_hot.reshape(chan_count, count, -1)
    right_hot = right_hot.reshape(chan_count, count, -1)
    part = cos_part.shape[0]
    vmem = pl.BlockSpec(memory_space=pltpu.VMEM)
    flops = 2 * 2 * rows * panel.shape[0] * panel.shape[1] + 2 * 2 * rows * part * LAGS
    return pl.pallas_call(
        pair_exchange_kernel,
        out_shape=jax.ShapeDtypeStruct((chan_count, count, LAGS), jnp.bfloat16),
        in_specs=[vmem] * 5,
        out_specs=pl.BlockSpec(memory_space=pl.ANY),
        scratch_shapes=[
            pltpu.VMEM((chan_count, count, LAGS), jnp.bfloat16),
            pltpu.SemaphoreType.DMA(()),
            pltpu.SemaphoreType.DMA((chan_count,)),
            pltpu.SemaphoreType.DMA((chan_count,)),
        ],
        compiler_params=pltpu.CompilerParams(
            collective_id=collective, has_side_effects=True, vmem_limit_bytes=56 * 1024 * 1024
        ),
        cost_estimate=pl.CostEstimate(
            flops=flops,
            transcendentals=0,
            bytes_accessed=panel.size * 2 + 4 * part * LAGS + rows * LAGS * 2,
        ),
    )(left_hot, right_hot, panel, cos_part, sin_part)


def exchange_kernel(axis, other_axis, axis_first, stride, x_ref, out_ref, local_sem, send_sem, recv_sem):
    n = x_ref.shape[0]
    index = lax.axis_index(axis)
    me = lax.rem(index // stride, n)
    base = index - me * stride
    other = lax.axis_index(other_axis)

    def device(j):
        coord = base + stride * j
        return (coord, other) if axis_first else (other, coord)

    barrier = pltpu.get_barrier_semaphore()
    for step in range(1, n):
        pl.semaphore_signal(barrier, inc=1, device_id=device(lax.rem(me + step, n)),
                            device_id_type=pl.DeviceIdType.MESH)
    pl.semaphore_wait(barrier, n - 1)

    pieces = x_ref.shape[1]
    own = pltpu.make_async_copy(x_ref.at[me], out_ref.at[me], local_sem)
    own.start()
    copies = []
    for step in range(1, n):
        target = lax.rem(me + step, n)
        for piece in range(pieces):
            copy = pltpu.make_async_remote_copy(
                src_ref=x_ref.at[target, piece],
                dst_ref=out_ref.at[me, piece],
                send_sem=send_sem.at[step, piece],
                recv_sem=recv_sem.at[step, piece],
                device_id=device(target),
                device_id_type=pl.DeviceIdType.MESH,
            )
            copy.start()
            copies.append(copy)
    own.wait()
    for step in range(1, n):
        source = lax.rem(me + n - step, n)
        for piece in range(pieces):
            copies[(step - 1) * pieces + piece].wait_send()
            incoming = pltpu.make_async_remote_copy(
                src_ref=x_ref.at[source, piece],
                dst_ref=out_ref.at[source, piece],
                send_sem=send_sem.at[step, piece],
                recv_sem=recv_sem.at[step, piece],
                device_id=device(source),
                device_id_type=pl.DeviceIdType.MESH,
            )
            incoming.wait_recv()


def exchange(x, axis, other_axis, axis_first, stride, collective):
    n = x.shape[0]
    vmem = pl.BlockSpec(memory_space=pltpu.VMEM)
    return pl.pallas_call(
        functools.partial(exchange_kernel, axis, other_axis, axis_first, stride),
        out_shape=jax.ShapeDtypeStruct(x.shape, x.dtype),
        in_specs=[vmem],
        out_specs=vmem,
        scratch_shapes=[
            pltpu.SemaphoreType.DMA(()),
            pltpu.SemaphoreType.DMA((n, x.shape[1])),
            pltpu.SemaphoreType.DMA((n, x.shape[1])),
        ],
        compiler_params=pltpu.CompilerParams(collective_id=collective, has_side_effects=True),
    )(x)


def local(spectra, pair_blocks, owners):
    groups_count = lax.axis_size("grp")
    chan_count = lax.axis_size("chan")
    slot_count = groups_count * MOST
    pairs = BLK * BLK
    part = F // chan_count
    me = lax.axis_index("chan")

    channels = spectra.shape[0]
    listed = pair_blocks[0, 0].reshape(-1).astype(jnp.bfloat16)
    extra = jnp.zeros((EXTRA_ROWS, part), jnp.bfloat16).at[0, : listed.shape[0]].set(listed)
    sent = whiten_chunks(spectra, extra, chan_count)
    got = lax.all_to_all(sent, "chan", split_axis=0, concat_axis=0, tiled=True)
    rows_per = channels * WINDOWS * 2
    group_channels = chan_count * channels
    panel = got[:, :rows_per].reshape(group_channels, WINDOWS * 2 * part)
    all_blocks = got[:, rows_per, : NB_SRC * 2].astype(jnp.float32).astype(jnp.int32)
    all_blocks = all_blocks.reshape(chan_count * NB_SRC, 1, 2)
    offsets = jnp.arange(BLK, dtype=jnp.int32)
    left_ch = (all_blocks[:, :, 0] * BLK + offsets[None, :])[:, :, None] + jnp.zeros((1, 1, BLK), jnp.int32)
    right_ch = (all_blocks[:, :, 1] * BLK + offsets[None, :])[:, None, :] + jnp.zeros((1, BLK, 1), jnp.int32)
    channel_ids = jnp.arange(group_channels, dtype=jnp.int32)[None, :]
    left_hot = (left_ch.reshape(-1, 1) == channel_ids).astype(jnp.bfloat16)
    right_hot = (right_ch.reshape(-1, 1) == channel_ids).astype(jnp.bfloat16)

    cos_part, sin_part = table_slice(me * part, part)
    gathered = pair_exchange(left_hot, right_hot, panel, cos_part, sin_part, chan_count, 0)
    corr = jnp.sum(gathered.astype(jnp.float32), axis=0).reshape(NB_SRC, pairs * LAGS)

    owner_list = owners[0, 0, :, 0]
    same = owner_list[:, None] == owner_list[None, :]
    earlier = jnp.arange(NB_SRC)[None, :] < jnp.arange(NB_SRC)[:, None]
    order_rank = jnp.sum(jnp.logical_and(same, earlier), axis=1)
    slot_ids = owner_list * MOST + order_rank
    chooser = slot_ids[None, :] == jnp.arange(slot_count, dtype=jnp.int32)[:, None]
    source = jnp.argmax(chooser, axis=1)
    filled = jnp.any(chooser, axis=1)
    placed = jnp.where(filled[:, None], jnp.take(corr, source, axis=0), 0.0)
    placed = placed.reshape(groups_count, 1, MOST, pairs, LAGS).astype(jnp.bfloat16)
    received = exchange(placed, "grp", "chan", True, 1, 1).astype(jnp.float32)
    return received.reshape(1, 1, slot_count, pairs, LAGS)


def solution(mesh):
    return jax.shard_map(
        local,
        mesh=mesh,
        in_specs=(
            P(("grp", "chan"), None, None, None),
            P("grp", "chan", None, None),
            P("grp", "chan", None, None),
        ),
        out_specs=P("grp", "chan", None, None, None),
        check_vma=False,
    )
```

```python
import functools

import jax
import jax.numpy as jnp
from jax import lax
from jax.experimental import pallas as pl
from jax.experimental.pallas import tpu as pltpu
from jax.sharding import PartitionSpec as P

F = 8192
LAGS = 1024
BLK = 2
NB_SRC = 18
MOST = 3
WINDOWS = 2
FINE = 128


def phase_angle(bins, lag_index):
    phase = bins[:, None] * lag_index[None, :] % (2 * F)
    return phase.astype(jnp.float32) * (jnp.pi / F)


def table_slice(start, count):
    lag_index = jnp.arange(LAGS, dtype=jnp.int32) - LAGS // 2
    coarse = phase_angle(start + FINE * jnp.arange(count // FINE, dtype=jnp.int32), lag_index)
    fine = phase_angle(jnp.arange(FINE, dtype=jnp.int32), lag_index)
    cos_a, sin_a = jnp.cos(coarse)[:, None, :], jnp.sin(coarse)[:, None, :]
    cos_b, sin_b = jnp.cos(fine)[None, :, :], jnp.sin(fine)[None, :, :]
    cos_ab = (cos_a * cos_b - sin_a * sin_b).reshape(count, LAGS)
    sin_ab = (sin_a * cos_b + cos_a * sin_b).reshape(count, LAGS)
    bins = start + jnp.arange(count, dtype=jnp.int32)
    weight = (jnp.where(bins == 0, 1.0, 2.0).astype(jnp.float32) / jnp.sqrt(jnp.float32(F)))[:, None]
    cos_part = (cos_ab * weight).astype(jnp.bfloat16)
    sin_part = (-sin_ab * weight).astype(jnp.bfloat16)
    return cos_part, sin_part


def whiten_kernel(x_ref, blocks_ref, out_ref):
    x = x_ref[...].astype(jnp.float32)
    rows = x.shape[0]
    square = x * x
    after = pltpu.roll(square, rows - 1, 0)
    before = pltpu.roll(square, 1, 0)
    odd = lax.broadcasted_iota(jnp.int32, x.shape, 0) % 2 == 1
    power = jnp.where(odd, before + square, square + after)
    level = jnp.mean(power, axis=-1, keepdims=True) + 1e-05
    white = (x * lax.rsqrt(power + 0.1 * level)).astype(out_ref.dtype)
    part = out_ref.shape[2]
    lane = lax.broadcasted_iota(jnp.int32, (1, part), 1)
    extra = jnp.zeros((1, part), jnp.float32)
    for pair in range(blocks_ref.shape[2]):
        for side in range(2):
            value = blocks_ref[0, 0, pair, side].astype(jnp.float32)
            extra = jnp.where(lane == pair * 2 + side, value, extra)
    extra = extra.astype(out_ref.dtype)
    for chunk in range(out_ref.shape[0]):
        out_ref[chunk, :rows, :] = white[:, chunk * part:(chunk + 1) * part]
        out_ref[chunk, rows:, :] = extra


def whiten_chunks(spectra, pair_blocks, chan_count):
    channels = spectra.shape[0]
    rows = channels * WINDOWS * 2
    x = spectra.reshape(rows, F)
    vmem = pl.BlockSpec(memory_space=pltpu.VMEM)
    return pl.pallas_call(
        whiten_kernel,
        out_shape=jax.ShapeDtypeStruct((chan_count, rows + 1, F // chan_count), jnp.bfloat16),
        in_specs=[vmem, pl.BlockSpec(memory_space=pltpu.SMEM)],
        out_specs=vmem,
        compiler_params=pltpu.CompilerParams(vmem_limit_bytes=48 * 1024 * 1024),
        cost_estimate=pl.CostEstimate(flops=8 * rows * F, transcendentals=rows * F, bytes_accessed=4 * rows * F),
    )(x, pair_blocks)


def pair_rows(left_hot, right_hot, panel, cos_ref, sin_ref, target):
    part = cos_ref.shape[0]
    left = left_hot[target]
    right = right_hot[target]

    def rows_of(hot, window, kind):
        col = (window * 2 + kind) * part
        return jnp.dot(hot, panel[:, col:col + part], preferred_element_type=jnp.float32)

    real_sum = None
    imag_sum = None
    for window in range(WINDOWS):
        ra = rows_of(left, window, 0)
        ia = rows_of(left, window, 1)
        rb = rows_of(right, window, 0)
        ib = rows_of(right, window, 1)
        real = (ra * rb + ia * ib).astype(jnp.bfloat16).astype(jnp.float32)
        imag = (ia * rb - ra * ib).astype(jnp.bfloat16).astype(jnp.float32)
        real_sum = real if real_sum is None else real_sum + real
        imag_sum = imag if imag_sum is None else imag_sum + imag
    real_stack = (real_sum / WINDOWS).astype(jnp.bfloat16)
    imag_stack = (imag_sum / WINDOWS).astype(jnp.bfloat16)
    total = jnp.dot(real_stack, cos_ref[...], preferred_element_type=jnp.float32)
    return total + jnp.dot(imag_stack, sin_ref[...], preferred_element_type=jnp.float32)


def pair_exchange_kernel(left_hot, right_hot, panel, cos_ref, sin_ref, out_ref, slots, local_sem, send_sem, recv_sem):
    n = out_ref.shape[0]
    me = lax.axis_index("chan")
    group = lax.axis_index("grp")

    barrier = pltpu.get_barrier_semaphore()
    for step in range(1, n):
        pl.semaphore_signal(barrier, inc=1, device_id=(group, lax.rem(me + step, n)),
                            device_id_type=pl.DeviceIdType.MESH)
    pl.semaphore_wait(barrier, n - 1)

    def fill(target):
        slots[target] = pair_rows(left_hot, right_hot, panel, cos_ref, sin_ref, target).astype(slots.dtype)

    def send(step):
        target = lax.rem(me + step, n)
        return pltpu.make_async_remote_copy(
            src_ref=slots.at[target],
            dst_ref=out_ref.at[me],
            send_sem=send_sem.at[step],
            recv_sem=recv_sem.at[step],
            device_id=(group, target),
            device_id_type=pl.DeviceIdType.MESH,
        )

    def one_step(step, carry):
        fill(lax.rem(me + step, n))

        @pl.when(step > 1)
        def _():
            send(step - 1).start()

        return carry

    lax.fori_loop(1, n, one_step, 0)
    fill(me)
    send(n - 1).start()
    own = pltpu.make_async_copy(slots.at[me], out_ref.at[me], local_sem)
    own.start()
    own.wait()

    def finish(step, carry):
        send(step).wait_send()
        source = lax.rem(me + n - step, n)
        pltpu.make_async_remote_copy(
            src_ref=slots.at[source],
            dst_ref=out_ref.at[source],
            send_sem=send_sem.at[step],
            recv_sem=recv_sem.at[step],
            device_id=(group, source),
            device_id_type=pl.DeviceIdType.MESH,
        ).wait_recv()
        return carry

    lax.fori_loop(1, n, finish, 0)


def pair_exchange(left_hot, right_hot, panel, cos_part, sin_part, chan_count, collective):
    rows = left_hot.shape[0]
    count = rows // chan_count
    left_hot = left_hot.reshape(chan_count, count, -1)
    right_hot = right_hot.reshape(chan_count, count, -1)
    part = cos_part.shape[0]
    vmem = pl.BlockSpec(memory_space=pltpu.VMEM)
    flops = 2 * 2 * rows * panel.shape[0] * panel.shape[1] + 2 * 2 * rows * part * LAGS
    return pl.pallas_call(
        pair_exchange_kernel,
        out_shape=jax.ShapeDtypeStruct((chan_count, count, LAGS), jnp.bfloat16),
        in_specs=[vmem] * 5,
        out_specs=pl.BlockSpec(memory_space=pl.ANY),
        scratch_shapes=[
            pltpu.VMEM((chan_count, count, LAGS), jnp.bfloat16),
            pltpu.SemaphoreType.DMA(()),
            pltpu.SemaphoreType.DMA((chan_count,)),
            pltpu.SemaphoreType.DMA((chan_count,)),
        ],
        compiler_params=pltpu.CompilerParams(
            collective_id=collective, has_side_effects=True, vmem_limit_bytes=56 * 1024 * 1024
        ),
        cost_estimate=pl.CostEstimate(
            flops=flops,
            transcendentals=0,
            bytes_accessed=panel.size * 2 + 4 * part * LAGS + rows * LAGS * 2,
        ),
    )(left_hot, right_hot, panel, cos_part, sin_part)


def exchange_kernel(axis, other_axis, axis_first, stride, x_ref, out_ref, local_sem, send_sem, recv_sem):
    n = x_ref.shape[0]
    index = lax.axis_index(axis)
    me = lax.rem(index // stride, n)
    base = index - me * stride
    other = lax.axis_index(other_axis)

    def device(j):
        coord = base + stride * j
        return (coord, other) if axis_first else (other, coord)

    barrier = pltpu.get_barrier_semaphore()
    for step in range(1, n):
        pl.semaphore_signal(barrier, inc=1, device_id=device(lax.rem(me + step, n)),
                            device_id_type=pl.DeviceIdType.MESH)
    pl.semaphore_wait(barrier, n - 1)

    pieces = x_ref.shape[1]
    own = pltpu.make_async_copy(x_ref.at[me], out_ref.at[me], local_sem)
    own.start()
    copies = []
    for step in range(1, n):
        target = lax.rem(me + step, n)
        for piece in range(pieces):
            copy = pltpu.make_async_remote_copy(
                src_ref=x_ref.at[target, piece],
                dst_ref=out_ref.at[me, piece],
                send_sem=send_sem.at[step, piece],
                recv_sem=recv_sem.at[step, piece],
                device_id=device(target),
                device_id_type=pl.DeviceIdType.MESH,
            )
            copy.start()
            copies.append(copy)
    own.wait()
    for step in range(1, n):
        source = lax.rem(me + n - step, n)
        for piece in range(pieces):
            copies[(step - 1) * pieces + piece].wait_send()
            incoming = pltpu.make_async_remote_copy(
                src_ref=x_ref.at[source, piece],
                dst_ref=out_ref.at[source, piece],
                send_sem=send_sem.at[step, piece],
                recv_sem=recv_sem.at[step, piece],
                device_id=device(source),
                device_id_type=pl.DeviceIdType.MESH,
            )
            incoming.wait_recv()


def exchange(x, axis, other_axis, axis_first, stride, collective):
    n = x.shape[0]
    vmem = pl.BlockSpec(memory_space=pltpu.VMEM)
    return pl.pallas_call(
        functools.partial(exchange_kernel, axis, other_axis, axis_first, stride),
        out_shape=jax.ShapeDtypeStruct(x.shape, x.dtype),
        in_specs=[vmem],
        out_specs=vmem,
        scratch_shapes=[
            pltpu.SemaphoreType.DMA(()),
            pltpu.SemaphoreType.DMA((n, x.shape[1])),
            pltpu.SemaphoreType.DMA((n, x.shape[1])),
        ],
        compiler_params=pltpu.CompilerParams(collective_id=collective, has_side_effects=True),
    )(x)


def local(spectra, pair_blocks, owners):
    groups_count = lax.axis_size("grp")
    chan_count = lax.axis_size("chan")
    slot_count = groups_count * MOST
    pairs = BLK * BLK
    part = F // chan_count
    me = lax.axis_index("chan")

    channels = spectra.shape[0]
    sent = whiten_chunks(spectra, pair_blocks, chan_count)
    got = lax.all_to_all(sent, "chan", split_axis=0, concat_axis=0, tiled=True)
    rows_per = channels * WINDOWS * 2
    group_channels = chan_count * channels
    panel = got[:, :rows_per].reshape(group_channels, WINDOWS * 2 * part)
    all_blocks = got[:, rows_per, : NB_SRC * 2].astype(jnp.float32).astype(jnp.int32)
    all_blocks = all_blocks.reshape(chan_count * NB_SRC, 1, 2)
    offsets = jnp.arange(BLK, dtype=jnp.int32)
    left_ch = (all_blocks[:, :, 0] * BLK + offsets[None, :])[:, :, None] + jnp.zeros((1, 1, BLK), jnp.int32)
    right_ch = (all_blocks[:, :, 1] * BLK + offsets[None, :])[:, None, :] + jnp.zeros((1, BLK, 1), jnp.int32)
    channel_ids = jnp.arange(group_channels, dtype=jnp.int32)[None, :]
    left_hot = (left_ch.reshape(-1, 1) == channel_ids).astype(jnp.bfloat16)
    right_hot = (right_ch.reshape(-1, 1) == channel_ids).astype(jnp.bfloat16)

    cos_part, sin_part = table_slice(me * part, part)
    gathered = pair_exchange(left_hot, right_hot, panel, cos_part, sin_part, chan_count, 0)
    corr = jnp.sum(gathered.astype(jnp.float32), axis=0).reshape(NB_SRC, pairs * LAGS)

    owner_list = owners[0, 0, :, 0]
    same = owner_list[:, None] == owner_list[None, :]
    earlier = jnp.arange(NB_SRC)[None, :] < jnp.arange(NB_SRC)[:, None]
    order_rank = jnp.sum(jnp.logical_and(same, earlier), axis=1)
    slot_ids = owner_list * MOST + order_rank
    chooser = slot_ids[None, :] == jnp.arange(slot_count, dtype=jnp.int32)[:, None]
    source = jnp.argmax(chooser, axis=1)
    filled = jnp.any(chooser, axis=1)
    placed = jnp.where(filled[:, None], jnp.take(corr, source, axis=0), 0.0)
    placed = placed.reshape(groups_count, 1, MOST, pairs, LAGS).astype(jnp.bfloat16)
    received = exchange(placed, "grp", "chan", True, 1, 1).astype(jnp.float32)
    return received.reshape(1, 1, slot_count, pairs, LAGS)


def solution(mesh):
    return jax.shard_map(
        local,
        mesh=mesh,
        in_specs=(
            P(("grp", "chan"), None, None, None),
            P("grp", "chan", None, None),
            P("grp", "chan", None, None),
        ),
        out_specs=P("grp", "chan", None, None, None),
        check_vma=False,
    )
```

```python
import functools

import jax
import jax.numpy as jnp
from jax import lax
from jax.experimental import pallas as pl
from jax.experimental.pallas import tpu as pltpu
from jax.sharding import PartitionSpec as P

F = 8192
LAGS = 1024
BLK = 2
NB_SRC = 18
MOST = 3
WINDOWS = 2
FINE = 128


def phase_angle(bins, lag_index):
    phase = bins[:, None] * lag_index[None, :] % (2 * F)
    return phase.astype(jnp.float32) * (jnp.pi / F)


def table_slice(start, count):
    lag_index = jnp.arange(LAGS, dtype=jnp.int32) - LAGS // 2
    coarse = phase_angle(start + FINE * jnp.arange(count // FINE, dtype=jnp.int32), lag_index)
    fine = phase_angle(jnp.arange(FINE, dtype=jnp.int32), lag_index)
    cos_a, sin_a = jnp.cos(coarse)[:, None, :], jnp.sin(coarse)[:, None, :]
    cos_b, sin_b = jnp.cos(fine)[None, :, :], jnp.sin(fine)[None, :, :]
    cos_ab = (cos_a * cos_b - sin_a * sin_b).reshape(count, LAGS)
    sin_ab = (sin_a * cos_b + cos_a * sin_b).reshape(count, LAGS)
    bins = start + jnp.arange(count, dtype=jnp.int32)
    weight = (jnp.where(bins == 0, 1.0, 2.0).astype(jnp.float32) / jnp.sqrt(jnp.float32(F)))[:, None]
    cos_part = (cos_ab * weight).astype(jnp.bfloat16)
    sin_part = (-sin_ab * weight).astype(jnp.bfloat16)
    return cos_part, sin_part


def whiten_kernel(x_ref, blocks_ref, out_ref):
    x = x_ref[...].astype(jnp.float32)
    rows = x.shape[0]
    square = x * x
    after = pltpu.roll(square, rows - 1, 0)
    before = pltpu.roll(square, 1, 0)
    odd = lax.broadcasted_iota(jnp.int32, x.shape, 0) % 2 == 1
    power = jnp.where(odd, before + square, square + after)
    level = jnp.mean(power, axis=-1, keepdims=True) + 1e-05
    white = (x * lax.rsqrt(power + 0.1 * level)).astype(out_ref.dtype)
    channels = rows // (WINDOWS * 2)
    dest = lax.broadcasted_iota(jnp.int32, (rows, rows), 0)
    source = lax.broadcasted_iota(jnp.int32, (rows, rows), 1)
    order = (source == (dest % channels) * (WINDOWS * 2) + dest // channels).astype(white.dtype)
    white = jnp.dot(order, white, preferred_element_type=jnp.float32).astype(out_ref.dtype)
    part = out_ref.shape[2]
    lane = lax.broadcasted_iota(jnp.int32, (1, part), 1)
    extra = jnp.zeros((1, part), jnp.float32)
    for pair in range(blocks_ref.shape[2]):
        for side in range(2):
            value = blocks_ref[0, 0, pair, side].astype(jnp.float32)
            extra = jnp.where(lane == pair * 2 + side, value, extra)
    extra = extra.astype(out_ref.dtype)
    for chunk in range(out_ref.shape[0]):
        out_ref[chunk, :rows, :] = white[:, chunk * part:(chunk + 1) * part]
        out_ref[chunk, rows:, :] = extra


def whiten_chunks(spectra, pair_blocks, chan_count):
    channels = spectra.shape[0]
    rows = channels * WINDOWS * 2
    x = spectra.reshape(rows, F)
    vmem = pl.BlockSpec(memory_space=pltpu.VMEM)
    return pl.pallas_call(
        whiten_kernel,
        out_shape=jax.ShapeDtypeStruct((chan_count, rows + 1, F // chan_count), jnp.bfloat16),
        in_specs=[vmem, pl.BlockSpec(memory_space=pltpu.SMEM)],
        out_specs=vmem,
        compiler_params=pltpu.CompilerParams(vmem_limit_bytes=48 * 1024 * 1024),
        cost_estimate=pl.CostEstimate(flops=8 * rows * F, transcendentals=rows * F, bytes_accessed=4 * rows * F),
    )(x, pair_blocks)


def pair_rows(left_hot, right_hot, panel, cos_ref, sin_ref, target):
    part = cos_ref.shape[0]
    left = left_hot[target]
    right = right_hot[target]

    sources = panel.shape[0]
    channels = (panel.shape[1] - 1) // (WINDOWS * 2)

    def rows_of(hot, window, kind):
        at = (window * 2 + kind) * channels
        cols = panel[:, at:at + channels, :].reshape(sources * channels, part)
        return jnp.dot(hot, cols, preferred_element_type=jnp.float32)

    real_sum = None
    imag_sum = None
    for window in range(WINDOWS):
        ra = rows_of(left, window, 0)
        ia = rows_of(left, window, 1)
        rb = rows_of(right, window, 0)
        ib = rows_of(right, window, 1)
        real = (ra * rb + ia * ib).astype(jnp.bfloat16).astype(jnp.float32)
        imag = (ia * rb - ra * ib).astype(jnp.bfloat16).astype(jnp.float32)
        real_sum = real if real_sum is None else real_sum + real
        imag_sum = imag if imag_sum is None else imag_sum + imag
    real_stack = (real_sum / WINDOWS).astype(jnp.bfloat16)
    imag_stack = (imag_sum / WINDOWS).astype(jnp.bfloat16)
    total = jnp.dot(real_stack, cos_ref[...], preferred_element_type=jnp.float32)
    return total + jnp.dot(imag_stack, sin_ref[...], preferred_element_type=jnp.float32)


def pair_exchange_kernel(left_hot, right_hot, panel, cos_ref, sin_ref, out_ref, slots, local_sem, send_sem, recv_sem):
    n = out_ref.shape[0]
    me = lax.axis_index("chan")
    group = lax.axis_index("grp")

    barrier = pltpu.get_barrier_semaphore()
    for step in range(1, n):
        pl.semaphore_signal(barrier, inc=1, device_id=(group, lax.rem(me + step, n)),
                            device_id_type=pl.DeviceIdType.MESH)
    pl.semaphore_wait(barrier, n - 1)

    def fill(target):
        slots[target] = pair_rows(left_hot, right_hot, panel, cos_ref, sin_ref, target).astype(slots.dtype)

    def send(step):
        target = lax.rem(me + step, n)
        return pltpu.make_async_remote_copy(
            src_ref=slots.at[target],
            dst_ref=out_ref.at[me],
            send_sem=send_sem.at[step],
            recv_sem=recv_sem.at[step],
            device_id=(group, target),
            device_id_type=pl.DeviceIdType.MESH,
        )

    def one_step(step, carry):
        fill(lax.rem(me + step, n))

        @pl.when(step > 1)
        def _():
            send(step - 1).start()

        return carry

    lax.fori_loop(1, n, one_step, 0)
    fill(me)
    send(n - 1).start()
    own = pltpu.make_async_copy(slots.at[me], out_ref.at[me], local_sem)
    own.start()
    own.wait()

    def finish(step, carry):
        send(step).wait_send()
        source = lax.rem(me + n - step, n)
        pltpu.make_async_remote_copy(
            src_ref=slots.at[source],
            dst_ref=out_ref.at[source],
            send_sem=send_sem.at[step],
            recv_sem=recv_sem.at[step],
            device_id=(group, source),
            device_id_type=pl.DeviceIdType.MESH,
        ).wait_recv()
        return carry

    lax.fori_loop(1, n, finish, 0)


def pair_exchange(left_hot, right_hot, panel, cos_part, sin_part, chan_count, collective):
    rows = left_hot.shape[0]
    count = rows // chan_count
    left_hot = left_hot.reshape(chan_count, count, -1)
    right_hot = right_hot.reshape(chan_count, count, -1)
    part = cos_part.shape[0]
    vmem = pl.BlockSpec(memory_space=pltpu.VMEM)
    flops = 2 * 2 * rows * panel.size + 2 * 2 * rows * part * LAGS
    return pl.pallas_call(
        pair_exchange_kernel,
        out_shape=jax.ShapeDtypeStruct((chan_count, count, LAGS), jnp.bfloat16),
        in_specs=[vmem] * 5,
        out_specs=pl.BlockSpec(memory_space=pl.ANY),
        scratch_shapes=[
            pltpu.VMEM((chan_count, count, LAGS), jnp.bfloat16),
            pltpu.SemaphoreType.DMA(()),
            pltpu.SemaphoreType.DMA((chan_count,)),
            pltpu.SemaphoreType.DMA((chan_count,)),
        ],
        compiler_params=pltpu.CompilerParams(
            collective_id=collective, has_side_effects=True, vmem_limit_bytes=56 * 1024 * 1024
        ),
        cost_estimate=pl.CostEstimate(
            flops=flops,
            transcendentals=0,
            bytes_accessed=panel.size * 2 + 4 * part * LAGS + rows * LAGS * 2,
        ),
    )(left_hot, right_hot, panel, cos_part, sin_part)


def exchange_kernel(axis, other_axis, axis_first, stride, x_ref, out_ref, local_sem, send_sem, recv_sem):
    n = x_ref.shape[0]
    index = lax.axis_index(axis)
    me = lax.rem(index // stride, n)
    base = index - me * stride
    other = lax.axis_index(other_axis)

    def device(j):
        coord = base + stride * j
        return (coord, other) if axis_first else (other, coord)

    barrier = pltpu.get_barrier_semaphore()
    for step in range(1, n):
        pl.semaphore_signal(barrier, inc=1, device_id=device(lax.rem(me + step, n)),
                            device_id_type=pl.DeviceIdType.MESH)
    pl.semaphore_wait(barrier, n - 1)

    pieces = x_ref.shape[1]
    own = pltpu.make_async_copy(x_ref.at[me], out_ref.at[me], local_sem)
    own.start()
    copies = []
    for step in range(1, n):
        target = lax.rem(me + step, n)
        for piece in range(pieces):
            copy = pltpu.make_async_remote_copy(
                src_ref=x_ref.at[target, piece],
                dst_ref=out_ref.at[me, piece],
                send_sem=send_sem.at[step, piece],
                recv_sem=recv_sem.at[step, piece],
                device_id=device(target),
                device_id_type=pl.DeviceIdType.MESH,
            )
            copy.start()
            copies.append(copy)
    own.wait()
    for step in range(1, n):
        source = lax.rem(me + n - step, n)
        for piece in range(pieces):
            copies[(step - 1) * pieces + piece].wait_send()
            incoming = pltpu.make_async_remote_copy(
                src_ref=x_ref.at[source, piece],
                dst_ref=out_ref.at[source, piece],
                send_sem=send_sem.at[step, piece],
                recv_sem=recv_sem.at[step, piece],
                device_id=device(source),
                device_id_type=pl.DeviceIdType.MESH,
            )
            incoming.wait_recv()


def exchange(x, axis, other_axis, axis_first, stride, collective):
    n = x.shape[0]
    vmem = pl.BlockSpec(memory_space=pltpu.VMEM)
    return pl.pallas_call(
        functools.partial(exchange_kernel, axis, other_axis, axis_first, stride),
        out_shape=jax.ShapeDtypeStruct(x.shape, x.dtype),
        in_specs=[vmem],
        out_specs=vmem,
        scratch_shapes=[
            pltpu.SemaphoreType.DMA(()),
            pltpu.SemaphoreType.DMA((n, x.shape[1])),
            pltpu.SemaphoreType.DMA((n, x.shape[1])),
        ],
        compiler_params=pltpu.CompilerParams(collective_id=collective, has_side_effects=True),
    )(x)


def local(spectra, pair_blocks, owners):
    groups_count = lax.axis_size("grp")
    chan_count = lax.axis_size("chan")
    slot_count = groups_count * MOST
    pairs = BLK * BLK
    part = F // chan_count
    me = lax.axis_index("chan")

    channels = spectra.shape[0]
    sent = whiten_chunks(spectra, pair_blocks, chan_count)
    got = lax.all_to_all(sent, "chan", split_axis=0, concat_axis=0, tiled=True)
    rows_per = channels * WINDOWS * 2
    group_channels = chan_count * channels
    panel = got
    all_blocks = got[:, rows_per, : NB_SRC * 2].astype(jnp.float32).astype(jnp.int32)
    all_blocks = all_blocks.reshape(chan_count * NB_SRC, 1, 2)
    offsets = jnp.arange(BLK, dtype=jnp.int32)
    left_ch = (all_blocks[:, :, 0] * BLK + offsets[None, :])[:, :, None] + jnp.zeros((1, 1, BLK), jnp.int32)
    right_ch = (all_blocks[:, :, 1] * BLK + offsets[None, :])[:, None, :] + jnp.zeros((1, BLK, 1), jnp.int32)
    channel_ids = jnp.arange(group_channels, dtype=jnp.int32)[None, :]
    left_hot = (left_ch.reshape(-1, 1) == channel_ids).astype(jnp.bfloat16)
    right_hot = (right_ch.reshape(-1, 1) == channel_ids).astype(jnp.bfloat16)

    cos_part, sin_part = table_slice(me * part, part)
    gathered = pair_exchange(left_hot, right_hot, panel, cos_part, sin_part, chan_count, 0)
    corr = jnp.sum(gathered.astype(jnp.float32), axis=0).reshape(NB_SRC, pairs * LAGS)

    owner_list = owners[0, 0, :, 0]
    same = owner_list[:, None] == owner_list[None, :]
    earlier = jnp.arange(NB_SRC)[None, :] < jnp.arange(NB_SRC)[:, None]
    order_rank = jnp.sum(jnp.logical_and(same, earlier), axis=1)
    slot_ids = owner_list * MOST + order_rank
    chooser = slot_ids[None, :] == jnp.arange(slot_count, dtype=jnp.int32)[:, None]
    source = jnp.argmax(chooser, axis=1)
    filled = jnp.any(chooser, axis=1)
    placed = jnp.where(filled[:, None], jnp.take(corr, source, axis=0), 0.0)
    placed = placed.reshape(groups_count, 1, MOST, pairs, LAGS).astype(jnp.bfloat16)
    received = exchange(placed, "grp", "chan", True, 1, 1).astype(jnp.float32)
    return received.reshape(1, 1, slot_count, pairs, LAGS)


def solution(mesh):
    return jax.shard_map(
        local,
        mesh=mesh,
        in_specs=(
            P(("grp", "chan"), None, None, None),
            P("grp", "chan", None, None),
            P("grp", "chan", None, None),
        ),
        out_specs=P("grp", "chan", None, None, None),
        check_vma=False,
    )
```

```python
import functools

import jax
import jax.numpy as jnp
from jax import lax
from jax.experimental import pallas as pl
from jax.experimental.pallas import tpu as pltpu
from jax.sharding import PartitionSpec as P

F = 8192
LAGS = 1024
BLK = 2
NB_SRC = 18
MOST = 3
WINDOWS = 2
FINE = 128


def phase_angle(bins, lag_index):
    phase = bins[:, None] * lag_index[None, :] % (2 * F)
    return phase.astype(jnp.float32) * (jnp.pi / F)


def table_slice(start, count):
    lag_index = jnp.arange(LAGS, dtype=jnp.int32) - LAGS // 2
    coarse = phase_angle(start + FINE * jnp.arange(count // FINE, dtype=jnp.int32), lag_index)
    fine = phase_angle(jnp.arange(FINE, dtype=jnp.int32), lag_index)
    cos_a, sin_a = jnp.cos(coarse)[:, None, :], jnp.sin(coarse)[:, None, :]
    cos_b, sin_b = jnp.cos(fine)[None, :, :], jnp.sin(fine)[None, :, :]
    cos_ab = (cos_a * cos_b - sin_a * sin_b).reshape(count, LAGS)
    sin_ab = (sin_a * cos_b + cos_a * sin_b).reshape(count, LAGS)
    bins = start + jnp.arange(count, dtype=jnp.int32)
    weight = (jnp.where(bins == 0, 1.0, 2.0).astype(jnp.float32) / jnp.sqrt(jnp.float32(F)))[:, None]
    cos_part = (cos_ab * weight).astype(jnp.bfloat16)
    sin_part = (-sin_ab * weight).astype(jnp.bfloat16)
    return cos_part, sin_part


def whiten_kernel(x_ref, blocks_ref, out_ref):
    x = x_ref[...].astype(jnp.float32)
    rows = x.shape[0]
    square = x * x
    after = pltpu.roll(square, rows - 1, 0)
    before = pltpu.roll(square, 1, 0)
    odd = lax.broadcasted_iota(jnp.int32, x.shape, 0) % 2 == 1
    power = jnp.where(odd, before + square, square + after)
    level = jnp.mean(power, axis=-1, keepdims=True) + 1e-05
    white = (x * lax.rsqrt(power + 0.1 * level)).astype(out_ref.dtype)
    channels = rows // (WINDOWS * 2)
    dest = lax.broadcasted_iota(jnp.int32, (rows, rows), 0)
    source = lax.broadcasted_iota(jnp.int32, (rows, rows), 1)
    order = (source == (dest % channels) * (WINDOWS * 2) + dest // channels).astype(white.dtype)
    white = jnp.dot(order, white, preferred_element_type=jnp.float32).astype(out_ref.dtype)
    part = out_ref.shape[2]
    lane = lax.broadcasted_iota(jnp.int32, (1, part), 1)
    extra = jnp.zeros((1, part), jnp.float32)
    for pair in range(blocks_ref.shape[2]):
        for side in range(2):
            value = blocks_ref[0, 0, pair, side].astype(jnp.float32)
            extra = jnp.where(lane == pair * 2 + side, value, extra)
    extra = extra.astype(out_ref.dtype)
    for chunk in range(out_ref.shape[0]):
        out_ref[chunk, :rows, :] = white[:, chunk * part:(chunk + 1) * part]
        out_ref[chunk, rows:, :] = extra


def whiten_chunks(spectra, pair_blocks, chan_count):
    channels = spectra.shape[0]
    rows = channels * WINDOWS * 2
    x = spectra.reshape(rows, F)
    vmem = pl.BlockSpec(memory_space=pltpu.VMEM)
    return pl.pallas_call(
        whiten_kernel,
        out_shape=jax.ShapeDtypeStruct((chan_count, rows + 1, F // chan_count), jnp.bfloat16),
        in_specs=[vmem, pl.BlockSpec(memory_space=pltpu.SMEM)],
        out_specs=vmem,
        compiler_params=pltpu.CompilerParams(vmem_limit_bytes=48 * 1024 * 1024),
        cost_estimate=pl.CostEstimate(flops=8 * rows * F, transcendentals=rows * F, bytes_accessed=4 * rows * F),
    )(x, pair_blocks)


def pair_rows(left_hot, right_hot, panel, cos_ref, sin_ref, target):
    part = cos_ref.shape[0]
    left = left_hot[target]
    right = right_hot[target]

    sources = panel.shape[0]
    channels = (panel.shape[1] - 1) // (WINDOWS * 2)

    def rows_of(hot, window, kind):
        at = (window * 2 + kind) * channels
        cols = panel[:, at:at + channels, :].reshape(sources * channels, part)
        return jnp.dot(hot, cols, preferred_element_type=jnp.float32)

    real_sum = None
    imag_sum = None
    for window in range(WINDOWS):
        ra = rows_of(left, window, 0)
        ia = rows_of(left, window, 1)
        rb = rows_of(right, window, 0)
        ib = rows_of(right, window, 1)
        real = (ra * rb + ia * ib).astype(jnp.bfloat16).astype(jnp.float32)
        imag = (ia * rb - ra * ib).astype(jnp.bfloat16).astype(jnp.float32)
        real_sum = real if real_sum is None else real_sum + real
        imag_sum = imag if imag_sum is None else imag_sum + imag
    real_stack = (real_sum / WINDOWS).astype(jnp.bfloat16)
    imag_stack = (imag_sum / WINDOWS).astype(jnp.bfloat16)
    total = jnp.dot(real_stack, cos_ref[...], preferred_element_type=jnp.float32)
    return total + jnp.dot(imag_stack, sin_ref[...], preferred_element_type=jnp.float32)


def pair_exchange_kernel(left_hot, right_hot, panel, cos_ref, sin_ref, out_ref, slots, received, local_sem,
                         send_sem, recv_sem):
    n = slots.shape[0]
    me = lax.axis_index("chan")
    group = lax.axis_index("grp")

    barrier = pltpu.get_barrier_semaphore()
    for step in range(1, n):
        pl.semaphore_signal(barrier, inc=1, device_id=(group, lax.rem(me + step, n)),
                            device_id_type=pl.DeviceIdType.MESH)
    pl.semaphore_wait(barrier, n - 1)

    def fill(target):
        slots[target] = pair_rows(left_hot, right_hot, panel, cos_ref, sin_ref, target).astype(slots.dtype)

    def send(step):
        target = lax.rem(me + step, n)
        return pltpu.make_async_remote_copy(
            src_ref=slots.at[target],
            dst_ref=received.at[me],
            send_sem=send_sem.at[step],
            recv_sem=recv_sem.at[step],
            device_id=(group, target),
            device_id_type=pl.DeviceIdType.MESH,
        )

    def one_step(step, carry):
        fill(lax.rem(me + step, n))

        @pl.when(step > 1)
        def _():
            send(step - 1).start()

        return carry

    lax.fori_loop(1, n, one_step, 0)
    fill(me)
    send(n - 1).start()
    own = pltpu.make_async_copy(slots.at[me], received.at[me], local_sem)
    own.start()
    own.wait()

    def finish(step, carry):
        send(step).wait_send()
        source = lax.rem(me + n - step, n)
        pltpu.make_async_remote_copy(
            src_ref=slots.at[source],
            dst_ref=received.at[source],
            send_sem=send_sem.at[step],
            recv_sem=recv_sem.at[step],
            device_id=(group, source),
            device_id_type=pl.DeviceIdType.MESH,
        ).wait_recv()
        return carry

    lax.fori_loop(1, n, finish, 0)
    total = received[0].astype(jnp.float32)
    for source in range(1, n):
        total = total + received[source].astype(jnp.float32)
    listed = out_ref.shape[0]
    lags = cos_ref.shape[1]
    for pq in range(total.shape[0] // listed):
        out_ref[:, pq * lags:(pq + 1) * lags] = total[pq * listed:(pq + 1) * listed]


def pair_exchange(left_hot, right_hot, panel, cos_part, sin_part, chan_count, collective):
    rows = left_hot.shape[0]
    count = rows // chan_count
    left_hot = left_hot.reshape(chan_count, count, -1)
    right_hot = right_hot.reshape(chan_count, count, -1)
    part = cos_part.shape[0]
    pairs = BLK * BLK
    vmem = pl.BlockSpec(memory_space=pltpu.VMEM)
    flops = 2 * 2 * rows * panel.size + 2 * 2 * rows * part * LAGS
    return pl.pallas_call(
        pair_exchange_kernel,
        out_shape=jax.ShapeDtypeStruct((count // pairs, pairs * LAGS), jnp.float32),
        in_specs=[vmem] * 5,
        out_specs=vmem,
        scratch_shapes=[
            pltpu.VMEM((chan_count, count, LAGS), jnp.bfloat16),
            pltpu.VMEM((chan_count, count, LAGS), jnp.bfloat16),
            pltpu.SemaphoreType.DMA(()),
            pltpu.SemaphoreType.DMA((chan_count,)),
            pltpu.SemaphoreType.DMA((chan_count,)),
        ],
        compiler_params=pltpu.CompilerParams(
            collective_id=collective, has_side_effects=True, vmem_limit_bytes=56 * 1024 * 1024
        ),
        cost_estimate=pl.CostEstimate(
            flops=flops,
            transcendentals=0,
            bytes_accessed=panel.size * 2 + 4 * part * LAGS + rows * LAGS * 2,
        ),
    )(left_hot, right_hot, panel, cos_part, sin_part)


def exchange_kernel(axis, other_axis, axis_first, stride, x_ref, out_ref, local_sem, send_sem, recv_sem):
    n = x_ref.shape[0]
    index = lax.axis_index(axis)
    me = lax.rem(index // stride, n)
    base = index - me * stride
    other = lax.axis_index(other_axis)

    def device(j):
        coord = base + stride * j
        return (coord, other) if axis_first else (other, coord)

    barrier = pltpu.get_barrier_semaphore()
    for step in range(1, n):
        pl.semaphore_signal(barrier, inc=1, device_id=device(lax.rem(me + step, n)),
                            device_id_type=pl.DeviceIdType.MESH)
    pl.semaphore_wait(barrier, n - 1)

    pieces = x_ref.shape[1]
    own = pltpu.make_async_copy(x_ref.at[me], out_ref.at[me], local_sem)
    own.start()
    copies = []
    for step in range(1, n):
        target = lax.rem(me + step, n)
        for piece in range(pieces):
            copy = pltpu.make_async_remote_copy(
                src_ref=x_ref.at[target, piece],
                dst_ref=out_ref.at[me, piece],
                send_sem=send_sem.at[step, piece],
                recv_sem=recv_sem.at[step, piece],
                device_id=device(target),
                device_id_type=pl.DeviceIdType.MESH,
            )
            copy.start()
            copies.append(copy)
    own.wait()
    for step in range(1, n):
        source = lax.rem(me + n - step, n)
        for piece in range(pieces):
            copies[(step - 1) * pieces + piece].wait_send()
            incoming = pltpu.make_async_remote_copy(
                src_ref=x_ref.at[source, piece],
                dst_ref=out_ref.at[source, piece],
                send_sem=send_sem.at[step, piece],
                recv_sem=recv_sem.at[step, piece],
                device_id=device(source),
                device_id_type=pl.DeviceIdType.MESH,
            )
            incoming.wait_recv()


def exchange(x, axis, other_axis, axis_first, stride, collective):
    n = x.shape[0]
    vmem = pl.BlockSpec(memory_space=pltpu.VMEM)
    return pl.pallas_call(
        functools.partial(exchange_kernel, axis, other_axis, axis_first, stride),
        out_shape=jax.ShapeDtypeStruct(x.shape, x.dtype),
        in_specs=[vmem],
        out_specs=vmem,
        scratch_shapes=[
            pltpu.SemaphoreType.DMA(()),
            pltpu.SemaphoreType.DMA((n, x.shape[1])),
            pltpu.SemaphoreType.DMA((n, x.shape[1])),
        ],
        compiler_params=pltpu.CompilerParams(collective_id=collective, has_side_effects=True),
    )(x)


def local(spectra, pair_blocks, owners):
    groups_count = lax.axis_size("grp")
    chan_count = lax.axis_size("chan")
    slot_count = groups_count * MOST
    pairs = BLK * BLK
    part = F // chan_count
    me = lax.axis_index("chan")

    channels = spectra.shape[0]
    sent = whiten_chunks(spectra, pair_blocks, chan_count)
    got = lax.all_to_all(sent, "chan", split_axis=0, concat_axis=0, tiled=True)
    rows_per = channels * WINDOWS * 2
    group_channels = chan_count * channels
    panel = got
    all_blocks = got[:, rows_per, : NB_SRC * 2].astype(jnp.float32).astype(jnp.int32)
    all_blocks = all_blocks.reshape(chan_count * NB_SRC, 1, 2)
    offsets = jnp.arange(BLK, dtype=jnp.int32)
    left_ch = (all_blocks[:, :, 0] * BLK + offsets[None, :])[:, :, None] + jnp.zeros((1, 1, BLK), jnp.int32)
    right_ch = (all_blocks[:, :, 1] * BLK + offsets[None, :])[:, None, :] + jnp.zeros((1, BLK, 1), jnp.int32)
    channel_ids = jnp.arange(group_channels, dtype=jnp.int32)[None, :]
    left_ch = left_ch.reshape(chan_count, NB_SRC, BLK, BLK).transpose(0, 2, 3, 1)
    right_ch = right_ch.reshape(chan_count, NB_SRC, BLK, BLK).transpose(0, 2, 3, 1)
    left_hot = (left_ch.reshape(-1, 1) == channel_ids).astype(jnp.bfloat16)
    right_hot = (right_ch.reshape(-1, 1) == channel_ids).astype(jnp.bfloat16)

    cos_part, sin_part = table_slice(me * part, part)
    corr = pair_exchange(left_hot, right_hot, panel, cos_part, sin_part, chan_count, 0)

    owner_list = owners[0, 0, :, 0]
    same = owner_list[:, None] == owner_list[None, :]
    earlier = jnp.arange(NB_SRC)[None, :] < jnp.arange(NB_SRC)[:, None]
    order_rank = jnp.sum(jnp.logical_and(same, earlier), axis=1)
    slot_ids = owner_list * MOST + order_rank
    chooser = slot_ids[None, :] == jnp.arange(slot_count, dtype=jnp.int32)[:, None]
    source = jnp.argmax(chooser, axis=1)
    filled = jnp.any(chooser, axis=1)
    placed = jnp.where(filled[:, None], jnp.take(corr, source, axis=0), 0.0)
    placed = placed.reshape(groups_count, 1, MOST, pairs, LAGS).astype(jnp.bfloat16)
    received = exchange(placed, "grp", "chan", True, 1, 1).astype(jnp.float32)
    return received.reshape(1, 1, slot_count, pairs, LAGS)


def solution(mesh):
    return jax.shard_map(
        local,
        mesh=mesh,
        in_specs=(
            P(("grp", "chan"), None, None, None),
            P("grp", "chan", None, None),
            P("grp", "chan", None, None),
        ),
        out_specs=P("grp", "chan", None, None, None),
        check_vma=False,
    )
```

```python
import functools

import jax
import jax.numpy as jnp
from jax import lax
from jax.experimental import pallas as pl
from jax.experimental.pallas import tpu as pltpu
from jax.sharding import PartitionSpec as P

F = 8192
LAGS = 1024
BLK = 2
NB_SRC = 18
MOST = 3
WINDOWS = 2
FINE = 128


def phase_angle(bins, lag_index):
    phase = bins[:, None] * lag_index[None, :] % (2 * F)
    return phase.astype(jnp.float32) * (jnp.pi / F)


def table_slice(start, count):
    lag_index = jnp.arange(LAGS, dtype=jnp.int32) - LAGS // 2
    coarse = phase_angle(start + FINE * jnp.arange(count // FINE, dtype=jnp.int32), lag_index)
    fine = phase_angle(jnp.arange(FINE, dtype=jnp.int32), lag_index)
    cos_a, sin_a = jnp.cos(coarse)[:, None, :], jnp.sin(coarse)[:, None, :]
    cos_b, sin_b = jnp.cos(fine)[None, :, :], jnp.sin(fine)[None, :, :]
    cos_ab = (cos_a * cos_b - sin_a * sin_b).reshape(count, LAGS)
    sin_ab = (sin_a * cos_b + cos_a * sin_b).reshape(count, LAGS)
    bins = start + jnp.arange(count, dtype=jnp.int32)
    weight = (jnp.where(bins == 0, 1.0, 2.0).astype(jnp.float32) / jnp.sqrt(jnp.float32(F)))[:, None]
    cos_part = (cos_ab * weight).astype(jnp.bfloat16)
    sin_part = (-sin_ab * weight).astype(jnp.bfloat16)
    return cos_part, sin_part


def whiten_kernel(x_ref, blocks_ref, out_ref):
    x = x_ref[...].astype(jnp.float32)
    rows = x.shape[0]
    square = x * x
    after = pltpu.roll(square, rows - 1, 0)
    before = pltpu.roll(square, 1, 0)
    odd = lax.broadcasted_iota(jnp.int32, x.shape, 0) % 2 == 1
    power = jnp.where(odd, before + square, square + after)
    level = jnp.mean(power, axis=-1, keepdims=True) + 1e-05
    white = (x * lax.rsqrt(power + 0.1 * level)).astype(out_ref.dtype)
    channels = rows // (WINDOWS * 2)
    dest = lax.broadcasted_iota(jnp.int32, (rows, rows), 0)
    source = lax.broadcasted_iota(jnp.int32, (rows, rows), 1)
    order = (source == (dest % channels) * (WINDOWS * 2) + dest // channels).astype(white.dtype)
    white = jnp.dot(order, white, preferred_element_type=jnp.float32).astype(out_ref.dtype)
    part = out_ref.shape[2]
    lane = lax.broadcasted_iota(jnp.int32, (1, part), 1)
    extra = jnp.zeros((1, part), jnp.float32)
    for pair in range(blocks_ref.shape[2]):
        for side in range(2):
            value = blocks_ref[0, 0, pair, side].astype(jnp.float32)
            extra = jnp.where(lane == pair * 2 + side, value, extra)
    extra = extra.astype(out_ref.dtype)
    for chunk in range(out_ref.shape[0]):
        out_ref[chunk, :rows, :] = white[:, chunk * part:(chunk + 1) * part]
        out_ref[chunk, rows:, :] = extra


def whiten_chunks(spectra, pair_blocks, chan_count):
    channels = spectra.shape[0]
    rows = channels * WINDOWS * 2
    x = spectra.reshape(rows, F)
    vmem = pl.BlockSpec(memory_space=pltpu.VMEM)
    return pl.pallas_call(
        whiten_kernel,
        out_shape=jax.ShapeDtypeStruct((chan_count, rows + 1, F // chan_count), jnp.bfloat16),
        in_specs=[vmem, pl.BlockSpec(memory_space=pltpu.SMEM)],
        out_specs=vmem,
        compiler_params=pltpu.CompilerParams(vmem_limit_bytes=48 * 1024 * 1024),
        cost_estimate=pl.CostEstimate(flops=8 * rows * F, transcendentals=rows * F, bytes_accessed=4 * rows * F),
    )(x, pair_blocks)


def pair_rows(left_hot, right_hot, panel, cos_ref, sin_ref, target):
    part = cos_ref.shape[0]
    left = left_hot[target]
    right = right_hot[target]

    sources = panel.shape[0]
    channels = (panel.shape[1] - 1) // (WINDOWS * 2)

    def rows_of(hot, window, kind):
        at = (window * 2 + kind) * channels
        cols = panel[:, at:at + channels, :].reshape(sources * channels, part)
        return jnp.dot(hot, cols, preferred_element_type=jnp.float32)

    real_sum = None
    imag_sum = None
    for window in range(WINDOWS):
        ra = rows_of(left, window, 0)
        ia = rows_of(left, window, 1)
        rb = rows_of(right, window, 0)
        ib = rows_of(right, window, 1)
        real = (ra * rb + ia * ib).astype(jnp.bfloat16).astype(jnp.float32)
        imag = (ia * rb - ra * ib).astype(jnp.bfloat16).astype(jnp.float32)
        real_sum = real if real_sum is None else real_sum + real
        imag_sum = imag if imag_sum is None else imag_sum + imag
    real_stack = (real_sum / WINDOWS).astype(jnp.bfloat16)
    imag_stack = (imag_sum / WINDOWS).astype(jnp.bfloat16)
    total = jnp.dot(real_stack, cos_ref[...], preferred_element_type=jnp.float32)
    return total + jnp.dot(imag_stack, sin_ref[...], preferred_element_type=jnp.float32)


def pair_exchange_kernel(left_hot, right_hot, panel, cos_ref, sin_ref, out_ref, slots, received, local_sem,
                         send_sem, recv_sem):
    n = slots.shape[0]
    me = lax.axis_index("chan")
    group = lax.axis_index("grp")

    barrier = pltpu.get_barrier_semaphore()
    for step in range(1, n):
        pl.semaphore_signal(barrier, inc=1, device_id=(group, lax.rem(me + step, n)),
                            device_id_type=pl.DeviceIdType.MESH)
    pl.semaphore_wait(barrier, n - 1)

    def fill(target):
        slots[target] = pair_rows(left_hot, right_hot, panel, cos_ref, sin_ref, target).astype(slots.dtype)

    def send(step):
        target = lax.rem(me + step, n)
        return pltpu.make_async_remote_copy(
            src_ref=slots.at[target],
            dst_ref=received.at[me],
            send_sem=send_sem.at[step],
            recv_sem=recv_sem.at[step],
            device_id=(group, target),
            device_id_type=pl.DeviceIdType.MESH,
        )

    def one_step(step, carry):
        fill(lax.rem(me + step, n))

        @pl.when(step > 1)
        def _():
            send(step - 1).start()

        return carry

    lax.fori_loop(1, n, one_step, 0)
    fill(me)
    send(n - 1).start()
    own = pltpu.make_async_copy(slots.at[me], received.at[me], local_sem)
    own.start()
    own.wait()

    def finish(step, carry):
        send(step).wait_send()
        source = lax.rem(me + n - step, n)
        pltpu.make_async_remote_copy(
            src_ref=slots.at[source],
            dst_ref=received.at[source],
            send_sem=send_sem.at[step],
            recv_sem=recv_sem.at[step],
            device_id=(group, source),
            device_id_type=pl.DeviceIdType.MESH,
        ).wait_recv()
        return carry

    lax.fori_loop(1, n, finish, 0)
    total = received[0].astype(jnp.float32)
    for source in range(1, n):
        total = total + received[source].astype(jnp.float32)
    listed = out_ref.shape[0]
    lags = cos_ref.shape[1]
    for pq in range(total.shape[0] // listed):
        out_ref[:, pq * lags:(pq + 1) * lags] = total[pq * listed:(pq + 1) * listed]


def pair_exchange(left_hot, right_hot, panel, cos_part, sin_part, chan_count, collective):
    rows = left_hot.shape[0]
    count = rows // chan_count
    left_hot = left_hot.reshape(chan_count, count, -1)
    right_hot = right_hot.reshape(chan_count, count, -1)
    part = cos_part.shape[0]
    pairs = BLK * BLK
    vmem = pl.BlockSpec(memory_space=pltpu.VMEM)
    flops = 2 * 2 * rows * panel.size + 2 * 2 * rows * part * LAGS
    return pl.pallas_call(
        pair_exchange_kernel,
        out_shape=jax.ShapeDtypeStruct((count // pairs, pairs * LAGS), jnp.float32),
        in_specs=[vmem] * 5,
        out_specs=vmem,
        scratch_shapes=[
            pltpu.VMEM((chan_count, count, LAGS), jnp.bfloat16),
            pltpu.VMEM((chan_count, count, LAGS), jnp.bfloat16),
            pltpu.SemaphoreType.DMA(()),
            pltpu.SemaphoreType.DMA((chan_count,)),
            pltpu.SemaphoreType.DMA((chan_count,)),
        ],
        compiler_params=pltpu.CompilerParams(
            collective_id=collective, has_side_effects=True, vmem_limit_bytes=56 * 1024 * 1024
        ),
        cost_estimate=pl.CostEstimate(
            flops=flops,
            transcendentals=0,
            bytes_accessed=panel.size * 2 + 4 * part * LAGS + rows * LAGS * 2,
        ),
    )(left_hot, right_hot, panel, cos_part, sin_part)


def exchange_kernel(axis, other_axis, axis_first, stride, x_ref, out_ref, local_sem, send_sem, recv_sem):
    n = x_ref.shape[0]
    index = lax.axis_index(axis)
    me = lax.rem(index // stride, n)
    base = index - me * stride
    other = lax.axis_index(other_axis)

    def device(j):
        coord = base + stride * j
        return (coord, other) if axis_first else (other, coord)

    barrier = pltpu.get_barrier_semaphore()
    for step in range(1, n):
        pl.semaphore_signal(barrier, inc=1, device_id=device(lax.rem(me + step, n)),
                            device_id_type=pl.DeviceIdType.MESH)
    pl.semaphore_wait(barrier, n - 1)

    pieces = x_ref.shape[1]
    own = pltpu.make_async_copy(x_ref.at[me], out_ref.at[me], local_sem)
    own.start()
    copies = []
    for step in range(1, n):
        target = lax.rem(me + step, n)
        for piece in range(pieces):
            copy = pltpu.make_async_remote_copy(
                src_ref=x_ref.at[target, piece],
                dst_ref=out_ref.at[me, piece],
                send_sem=send_sem.at[step, piece],
                recv_sem=recv_sem.at[step, piece],
                device_id=device(target),
                device_id_type=pl.DeviceIdType.MESH,
            )
            copy.start()
            copies.append(copy)
    own.wait()
    for step in range(1, n):
        source = lax.rem(me + n - step, n)
        for piece in range(pieces):
            copies[(step - 1) * pieces + piece].wait_send()
            incoming = pltpu.make_async_remote_copy(
                src_ref=x_ref.at[source, piece],
                dst_ref=out_ref.at[source, piece],
                send_sem=send_sem.at[step, piece],
                recv_sem=recv_sem.at[step, piece],
                device_id=device(source),
                device_id_type=pl.DeviceIdType.MESH,
            )
            incoming.wait_recv()


def exchange(x, axis, other_axis, axis_first, stride, collective):
    n = x.shape[0]
    vmem = pl.BlockSpec(memory_space=pltpu.VMEM)
    return pl.pallas_call(
        functools.partial(exchange_kernel, axis, other_axis, axis_first, stride),
        out_shape=jax.ShapeDtypeStruct(x.shape, x.dtype),
        in_specs=[vmem],
        out_specs=vmem,
        scratch_shapes=[
            pltpu.SemaphoreType.DMA(()),
            pltpu.SemaphoreType.DMA((n, x.shape[1])),
            pltpu.SemaphoreType.DMA((n, x.shape[1])),
        ],
        compiler_params=pltpu.CompilerParams(collective_id=collective, has_side_effects=True),
    )(x)


def local(spectra, pair_blocks, owners):
    groups_count = lax.axis_size("grp")
    chan_count = lax.axis_size("chan")
    slot_count = groups_count * MOST
    pairs = BLK * BLK
    part = F // chan_count
    me = lax.axis_index("chan")

    channels = spectra.shape[0]
    sent = whiten_chunks(spectra, pair_blocks, chan_count)
    got = lax.all_to_all(sent, "chan", split_axis=0, concat_axis=0, tiled=True)
    rows_per = channels * WINDOWS * 2
    group_channels = chan_count * channels
    panel = got
    all_blocks = got[:, rows_per, : NB_SRC * 2].astype(jnp.float32).astype(jnp.int32)
    all_blocks = all_blocks.reshape(chan_count * NB_SRC, 1, 2)
    offsets = jnp.arange(BLK, dtype=jnp.int32)
    left_ch = (all_blocks[:, :, 0] * BLK + offsets[None, :])[:, :, None] + jnp.zeros((1, 1, BLK), jnp.int32)
    right_ch = (all_blocks[:, :, 1] * BLK + offsets[None, :])[:, None, :] + jnp.zeros((1, BLK, 1), jnp.int32)
    channel_ids = jnp.arange(group_channels, dtype=jnp.int32)[None, :]
    left_ch = left_ch.reshape(chan_count, NB_SRC, BLK, BLK).transpose(0, 2, 3, 1)
    right_ch = right_ch.reshape(chan_count, NB_SRC, BLK, BLK).transpose(0, 2, 3, 1)
    left_hot = (left_ch.reshape(-1, 1) == channel_ids).astype(jnp.bfloat16)
    right_hot = (right_ch.reshape(-1, 1) == channel_ids).astype(jnp.bfloat16)

    cos_part, sin_part = table_slice(me * part, part)
    corr = pair_exchange(left_hot, right_hot, panel, cos_part, sin_part, chan_count, 0)

    owner_list = owners[0, 0, :, 0]
    same = owner_list[:, None] == owner_list[None, :]
    earlier = jnp.arange(NB_SRC)[None, :] < jnp.arange(NB_SRC)[:, None]
    order_rank = jnp.sum(jnp.logical_and(same, earlier), axis=1)
    slot_ids = owner_list * MOST + order_rank
    chooser = (slot_ids[None, :] == jnp.arange(slot_count, dtype=jnp.int32)[:, None]).astype(jnp.bfloat16)
    placed = jnp.dot(chooser, corr.astype(jnp.bfloat16), preferred_element_type=jnp.float32)
    placed = placed.reshape(groups_count, 1, MOST, pairs, LAGS).astype(jnp.bfloat16)
    received = exchange(placed, "grp", "chan", True, 1, 1).astype(jnp.float32)
    return received.reshape(1, 1, slot_count, pairs, LAGS)


def solution(mesh):
    return jax.shard_map(
        local,
        mesh=mesh,
        in_specs=(
            P(("grp", "chan"), None, None, None),
            P("grp", "chan", None, None),
            P("grp", "chan", None, None),
        ),
        out_specs=P("grp", "chan", None, None, None),
        check_vma=False,
    )
```

```python
import functools

import jax
import jax.numpy as jnp
from jax import lax
from jax.experimental import pallas as pl
from jax.experimental.pallas import tpu as pltpu
from jax.sharding import PartitionSpec as P

F = 8192
LAGS = 1024
BLK = 2
NB_SRC = 18
MOST = 3
WINDOWS = 2
FINE = 128


def phase_angle(bins, lag_index):
    phase = bins[:, None] * lag_index[None, :] % (2 * F)
    return phase.astype(jnp.float32) * (jnp.pi / F)


def table_slice(start, count):
    lag_index = jnp.arange(LAGS, dtype=jnp.int32) - LAGS // 2
    coarse = phase_angle(start + FINE * jnp.arange(count // FINE, dtype=jnp.int32), lag_index)
    fine = phase_angle(jnp.arange(FINE, dtype=jnp.int32), lag_index)
    cos_a, sin_a = jnp.cos(coarse)[:, None, :], jnp.sin(coarse)[:, None, :]
    cos_b, sin_b = jnp.cos(fine)[None, :, :], jnp.sin(fine)[None, :, :]
    cos_ab = (cos_a * cos_b - sin_a * sin_b).reshape(count, LAGS)
    sin_ab = (sin_a * cos_b + cos_a * sin_b).reshape(count, LAGS)
    bins = start + jnp.arange(count, dtype=jnp.int32)
    weight = (jnp.where(bins == 0, 1.0, 2.0).astype(jnp.float32) / jnp.sqrt(jnp.float32(F)))[:, None]
    cos_part = (cos_ab * weight).astype(jnp.bfloat16)
    sin_part = (-sin_ab * weight).astype(jnp.bfloat16)
    return cos_part, sin_part


def whiten_kernel(x_ref, blocks_ref, out_ref):
    x = x_ref[...].astype(jnp.float32)
    rows = x.shape[0]
    square = x * x
    after = pltpu.roll(square, rows - 1, 0)
    before = pltpu.roll(square, 1, 0)
    odd = lax.broadcasted_iota(jnp.int32, x.shape, 0) % 2 == 1
    power = jnp.where(odd, before + square, square + after)
    level = jnp.mean(power, axis=-1, keepdims=True) + 1e-05
    white = (x * lax.rsqrt(power + 0.1 * level)).astype(out_ref.dtype)
    channels = rows // (WINDOWS * 2)
    dest = lax.broadcasted_iota(jnp.int32, (rows, rows), 0)
    source = lax.broadcasted_iota(jnp.int32, (rows, rows), 1)
    order = (source == (dest % channels) * (WINDOWS * 2) + dest // channels).astype(white.dtype)
    white = jnp.dot(order, white, preferred_element_type=jnp.float32).astype(out_ref.dtype)
    part = out_ref.shape[2]
    lane = lax.broadcasted_iota(jnp.int32, (1, part), 1)
    extra = jnp.zeros((1, part), jnp.float32)
    for pair in range(blocks_ref.shape[2]):
        for side in range(2):
            value = blocks_ref[0, 0, pair, side].astype(jnp.float32)
            extra = jnp.where(lane == pair * 2 + side, value, extra)
    extra = extra.astype(out_ref.dtype)
    for chunk in range(out_ref.shape[0]):
        out_ref[chunk, :rows, :] = white[:, chunk * part:(chunk + 1) * part]
        out_ref[chunk, rows:, :] = extra


def whiten_chunks(spectra, pair_blocks, chan_count):
    channels = spectra.shape[0]
    rows = channels * WINDOWS * 2
    x = spectra.reshape(rows, F)
    vmem = pl.BlockSpec(memory_space=pltpu.VMEM)
    return pl.pallas_call(
        whiten_kernel,
        out_shape=jax.ShapeDtypeStruct((chan_count, rows + 1, F // chan_count), jnp.bfloat16),
        in_specs=[vmem, pl.BlockSpec(memory_space=pltpu.SMEM)],
        out_specs=vmem,
        compiler_params=pltpu.CompilerParams(vmem_limit_bytes=48 * 1024 * 1024),
        cost_estimate=pl.CostEstimate(flops=8 * rows * F, transcendentals=rows * F, bytes_accessed=4 * rows * F),
    )(x, pair_blocks)


def pair_rows(left_hot, right_hot, panel, cos_ref, sin_ref, target):
    part = cos_ref.shape[0]
    sources = panel.shape[0]
    channels = (panel.shape[1] - 1) // (WINDOWS * 2)
    ids = lax.broadcasted_iota(jnp.int32, (left_hot.shape[1], sources * channels), 1)
    left = (left_hot[target] == ids).astype(jnp.bfloat16)
    right = (right_hot[target] == ids).astype(jnp.bfloat16)

    def rows_of(hot, window, kind):
        at = (window * 2 + kind) * channels
        cols = panel[:, at:at + channels, :].reshape(sources * channels, part)
        return jnp.dot(hot, cols, preferred_element_type=jnp.float32)

    real_sum = None
    imag_sum = None
    for window in range(WINDOWS):
        ra = rows_of(left, window, 0)
        ia = rows_of(left, window, 1)
        rb = rows_of(right, window, 0)
        ib = rows_of(right, window, 1)
        real = (ra * rb + ia * ib).astype(jnp.bfloat16).astype(jnp.float32)
        imag = (ia * rb - ra * ib).astype(jnp.bfloat16).astype(jnp.float32)
        real_sum = real if real_sum is None else real_sum + real
        imag_sum = imag if imag_sum is None else imag_sum + imag
    real_stack = (real_sum / WINDOWS).astype(jnp.bfloat16)
    imag_stack = (imag_sum / WINDOWS).astype(jnp.bfloat16)
    total = jnp.dot(real_stack, cos_ref[...], preferred_element_type=jnp.float32)
    return total + jnp.dot(imag_stack, sin_ref[...], preferred_element_type=jnp.float32)


def pair_exchange_kernel(left_hot, right_hot, panel, cos_ref, sin_ref, out_ref, slots, received, local_sem,
                         send_sem, recv_sem):
    n = slots.shape[0]
    me = lax.axis_index("chan")
    group = lax.axis_index("grp")

    barrier = pltpu.get_barrier_semaphore()
    for step in range(1, n):
        pl.semaphore_signal(barrier, inc=1, device_id=(group, lax.rem(me + step, n)),
                            device_id_type=pl.DeviceIdType.MESH)
    pl.semaphore_wait(barrier, n - 1)

    def fill(target):
        slots[target] = pair_rows(left_hot, right_hot, panel, cos_ref, sin_ref, target).astype(slots.dtype)

    def send(step):
        target = lax.rem(me + step, n)
        return pltpu.make_async_remote_copy(
            src_ref=slots.at[target],
            dst_ref=received.at[me],
            send_sem=send_sem.at[step],
            recv_sem=recv_sem.at[step],
            device_id=(group, target),
            device_id_type=pl.DeviceIdType.MESH,
        )

    def one_step(step, carry):
        fill(lax.rem(me + step, n))

        @pl.when(step > 1)
        def _():
            send(step - 1).start()

        return carry

    lax.fori_loop(1, n, one_step, 0)
    fill(me)
    send(n - 1).start()
    own = pltpu.make_async_copy(slots.at[me], received.at[me], local_sem)
    own.start()
    own.wait()

    def finish(step, carry):
        send(step).wait_send()
        source = lax.rem(me + n - step, n)
        pltpu.make_async_remote_copy(
            src_ref=slots.at[source],
            dst_ref=received.at[source],
            send_sem=send_sem.at[step],
            recv_sem=recv_sem.at[step],
            device_id=(group, source),
            device_id_type=pl.DeviceIdType.MESH,
        ).wait_recv()
        return carry

    lax.fori_loop(1, n, finish, 0)
    total = received[0].astype(jnp.float32)
    for source in range(1, n):
        total = total + received[source].astype(jnp.float32)
    listed = out_ref.shape[0]
    lags = cos_ref.shape[1]
    for pq in range(total.shape[0] // listed):
        out_ref[:, pq * lags:(pq + 1) * lags] = total[pq * listed:(pq + 1) * listed]


def pair_exchange(left_hot, right_hot, panel, cos_part, sin_part, chan_count, collective):
    rows = left_hot.shape[0]
    count = rows // chan_count
    left_hot = left_hot.reshape(chan_count, count, -1)
    right_hot = right_hot.reshape(chan_count, count, -1)
    part = cos_part.shape[0]
    pairs = BLK * BLK
    vmem = pl.BlockSpec(memory_space=pltpu.VMEM)
    flops = 2 * 2 * rows * panel.size + 2 * 2 * rows * part * LAGS
    return pl.pallas_call(
        pair_exchange_kernel,
        out_shape=jax.ShapeDtypeStruct((count // pairs, pairs * LAGS), jnp.float32),
        in_specs=[vmem] * 5,
        out_specs=vmem,
        scratch_shapes=[
            pltpu.VMEM((chan_count, count, LAGS), jnp.bfloat16),
            pltpu.VMEM((chan_count, count, LAGS), jnp.bfloat16),
            pltpu.SemaphoreType.DMA(()),
            pltpu.SemaphoreType.DMA((chan_count,)),
            pltpu.SemaphoreType.DMA((chan_count,)),
        ],
        compiler_params=pltpu.CompilerParams(
            collective_id=collective, has_side_effects=True, vmem_limit_bytes=56 * 1024 * 1024
        ),
        cost_estimate=pl.CostEstimate(
            flops=flops,
            transcendentals=0,
            bytes_accessed=panel.size * 2 + 4 * part * LAGS + rows * LAGS * 2,
        ),
    )(left_hot, right_hot, panel, cos_part, sin_part)


def exchange_kernel(axis, other_axis, axis_first, stride, x_ref, out_ref, local_sem, send_sem, recv_sem):
    n = x_ref.shape[0]
    index = lax.axis_index(axis)
    me = lax.rem(index // stride, n)
    base = index - me * stride
    other = lax.axis_index(other_axis)

    def device(j):
        coord = base + stride * j
        return (coord, other) if axis_first else (other, coord)

    barrier = pltpu.get_barrier_semaphore()
    for step in range(1, n):
        pl.semaphore_signal(barrier, inc=1, device_id=device(lax.rem(me + step, n)),
                            device_id_type=pl.DeviceIdType.MESH)
    pl.semaphore_wait(barrier, n - 1)

    pieces = x_ref.shape[1]
    own = pltpu.make_async_copy(x_ref.at[me], out_ref.at[me], local_sem)
    own.start()
    copies = []
    for step in range(1, n):
        target = lax.rem(me + step, n)
        for piece in range(pieces):
            copy = pltpu.make_async_remote_copy(
                src_ref=x_ref.at[target, piece],
                dst_ref=out_ref.at[me, piece],
                send_sem=send_sem.at[step, piece],
                recv_sem=recv_sem.at[step, piece],
                device_id=device(target),
                device_id_type=pl.DeviceIdType.MESH,
            )
            copy.start()
            copies.append(copy)
    own.wait()
    for step in range(1, n):
        source = lax.rem(me + n - step, n)
        for piece in range(pieces):
            copies[(step - 1) * pieces + piece].wait_send()
            incoming = pltpu.make_async_remote_copy(
                src_ref=x_ref.at[source, piece],
                dst_ref=out_ref.at[source, piece],
                send_sem=send_sem.at[step, piece],
                recv_sem=recv_sem.at[step, piece],
                device_id=device(source),
                device_id_type=pl.DeviceIdType.MESH,
            )
            incoming.wait_recv()


def exchange(x, axis, other_axis, axis_first, stride, collective):
    n = x.shape[0]
    vmem = pl.BlockSpec(memory_space=pltpu.VMEM)
    return pl.pallas_call(
        functools.partial(exchange_kernel, axis, other_axis, axis_first, stride),
        out_shape=jax.ShapeDtypeStruct(x.shape, x.dtype),
        in_specs=[vmem],
        out_specs=vmem,
        scratch_shapes=[
            pltpu.SemaphoreType.DMA(()),
            pltpu.SemaphoreType.DMA((n, x.shape[1])),
            pltpu.SemaphoreType.DMA((n, x.shape[1])),
        ],
        compiler_params=pltpu.CompilerParams(collective_id=collective, has_side_effects=True),
    )(x)


def local(spectra, pair_blocks, owners):
    groups_count = lax.axis_size("grp")
    chan_count = lax.axis_size("chan")
    slot_count = groups_count * MOST
    pairs = BLK * BLK
    part = F // chan_count
    me = lax.axis_index("chan")

    channels = spectra.shape[0]
    sent = whiten_chunks(spectra, pair_blocks, chan_count)
    got = lax.all_to_all(sent, "chan", split_axis=0, concat_axis=0, tiled=True)
    rows_per = channels * WINDOWS * 2
    group_channels = chan_count * channels
    panel = got
    all_blocks = got[:, rows_per, : NB_SRC * 2].astype(jnp.float32).astype(jnp.int32)
    all_blocks = all_blocks.reshape(chan_count * NB_SRC, 1, 2)
    offsets = jnp.arange(BLK, dtype=jnp.int32)
    left_ch = (all_blocks[:, :, 0] * BLK + offsets[None, :])[:, :, None] + jnp.zeros((1, 1, BLK), jnp.int32)
    right_ch = (all_blocks[:, :, 1] * BLK + offsets[None, :])[:, None, :] + jnp.zeros((1, BLK, 1), jnp.int32)
    channel_ids = jnp.arange(group_channels, dtype=jnp.int32)[None, :]
    left_ch = left_ch.reshape(chan_count, NB_SRC, BLK, BLK).transpose(0, 2, 3, 1)
    right_ch = right_ch.reshape(chan_count, NB_SRC, BLK, BLK).transpose(0, 2, 3, 1)
    left_hot = left_ch.reshape(-1, 1)
    right_hot = right_ch.reshape(-1, 1)

    cos_part, sin_part = table_slice(me * part, part)
    corr = pair_exchange(left_hot, right_hot, panel, cos_part, sin_part, chan_count, 0)

    owner_list = owners[0, 0, :, 0]
    same = owner_list[:, None] == owner_list[None, :]
    earlier = jnp.arange(NB_SRC)[None, :] < jnp.arange(NB_SRC)[:, None]
    order_rank = jnp.sum(jnp.logical_and(same, earlier), axis=1)
    slot_ids = owner_list * MOST + order_rank
    chooser = (slot_ids[None, :] == jnp.arange(slot_count, dtype=jnp.int32)[:, None]).astype(jnp.bfloat16)
    placed = jnp.dot(chooser, corr.astype(jnp.bfloat16), preferred_element_type=jnp.float32)
    placed = placed.reshape(groups_count, 1, MOST, pairs, LAGS).astype(jnp.bfloat16)
    received = exchange(placed, "grp", "chan", True, 1, 1).astype(jnp.float32)
    return received.reshape(1, 1, slot_count, pairs, LAGS)


def solution(mesh):
    return jax.shard_map(
        local,
        mesh=mesh,
        in_specs=(
            P(("grp", "chan"), None, None, None),
            P("grp", "chan", None, None),
            P("grp", "chan", None, None),
        ),
        out_specs=P("grp", "chan", None, None, None),
        check_vma=False,
    )
```

```python
import functools

import jax
import jax.numpy as jnp
from jax import lax
from jax.experimental import pallas as pl
from jax.experimental.pallas import tpu as pltpu
from jax.sharding import PartitionSpec as P

F = 8192
LAGS = 1024
BLK = 2
NB_SRC = 18
MOST = 3
WINDOWS = 2
FINE = 128


def phase_angle(bins, lag_index):
    phase = bins[:, None] * lag_index[None, :] % (2 * F)
    return phase.astype(jnp.float32) * (jnp.pi / F)


def table_slice(start, count):
    lag_index = jnp.arange(LAGS, dtype=jnp.int32) - LAGS // 2
    coarse = phase_angle(start + FINE * jnp.arange(count // FINE, dtype=jnp.int32), lag_index)
    fine = phase_angle(jnp.arange(FINE, dtype=jnp.int32), lag_index)
    cos_a, sin_a = jnp.cos(coarse)[:, None, :], jnp.sin(coarse)[:, None, :]
    cos_b, sin_b = jnp.cos(fine)[None, :, :], jnp.sin(fine)[None, :, :]
    cos_ab = (cos_a * cos_b - sin_a * sin_b).reshape(count, LAGS)
    sin_ab = (sin_a * cos_b + cos_a * sin_b).reshape(count, LAGS)
    bins = start + jnp.arange(count, dtype=jnp.int32)
    weight = (jnp.where(bins == 0, 1.0, 2.0).astype(jnp.float32) / jnp.sqrt(jnp.float32(F)))[:, None]
    cos_part = (cos_ab * weight).astype(jnp.bfloat16)
    sin_part = (-sin_ab * weight).astype(jnp.bfloat16)
    return cos_part, sin_part


def whiten_kernel(x_ref, blocks_ref, out_ref):
    x = x_ref[...].astype(jnp.float32)
    rows = x.shape[0]
    square = x * x
    after = pltpu.roll(square, rows - 1, 0)
    before = pltpu.roll(square, 1, 0)
    odd = lax.broadcasted_iota(jnp.int32, x.shape, 0) % 2 == 1
    power = jnp.where(odd, before + square, square + after)
    level = jnp.mean(power, axis=-1, keepdims=True) + 1e-05
    white = (x * lax.rsqrt(power + 0.1 * level)).astype(out_ref.dtype)
    channels = rows // (WINDOWS * 2)
    dest = lax.broadcasted_iota(jnp.int32, (rows, rows), 0)
    source = lax.broadcasted_iota(jnp.int32, (rows, rows), 1)
    order = (source == (dest % channels) * (WINDOWS * 2) + dest // channels).astype(white.dtype)
    white = jnp.dot(order, white, preferred_element_type=jnp.float32).astype(out_ref.dtype)
    part = out_ref.shape[2]
    lane = lax.broadcasted_iota(jnp.int32, (1, part), 1)
    extra = jnp.zeros((1, part), jnp.float32)
    for pair in range(blocks_ref.shape[2]):
        for side in range(2):
            value = blocks_ref[0, 0, pair, side].astype(jnp.float32)
            extra = jnp.where(lane == pair * 2 + side, value, extra)
    extra = extra.astype(out_ref.dtype)
    for chunk in range(out_ref.shape[0]):
        out_ref[chunk, :rows, :] = white[:, chunk * part:(chunk + 1) * part]
        out_ref[chunk, rows:, :] = extra


def whiten_chunks(spectra, pair_blocks, chan_count):
    channels = spectra.shape[0]
    rows = channels * WINDOWS * 2
    x = spectra.reshape(rows, F)
    vmem = pl.BlockSpec(memory_space=pltpu.VMEM)
    return pl.pallas_call(
        whiten_kernel,
        out_shape=jax.ShapeDtypeStruct((chan_count, rows + 1, F // chan_count), jnp.bfloat16),
        in_specs=[vmem, pl.BlockSpec(memory_space=pltpu.SMEM)],
        out_specs=vmem,
        compiler_params=pltpu.CompilerParams(vmem_limit_bytes=48 * 1024 * 1024),
        cost_estimate=pl.CostEstimate(flops=8 * rows * F, transcendentals=rows * F, bytes_accessed=4 * rows * F),
    )(x, pair_blocks)


def pair_rows(left_hot, right_hot, panel, cos_ref, sin_ref, target):
    part = cos_ref.shape[0]
    left = left_hot[target]
    right = right_hot[target]

    sources = panel.shape[0]
    channels = (panel.shape[1] - 1) // (WINDOWS * 2)

    def rows_of(hot, window, kind):
        at = (window * 2 + kind) * channels
        cols = panel[:, at:at + channels, :].reshape(sources * channels, part)
        return jnp.dot(hot, cols, preferred_element_type=jnp.float32)

    real_sum = None
    imag_sum = None
    for window in range(WINDOWS):
        ra = rows_of(left, window, 0)
        ia = rows_of(left, window, 1)
        rb = rows_of(right, window, 0)
        ib = rows_of(right, window, 1)
        real = (ra * rb + ia * ib).astype(jnp.bfloat16).astype(jnp.float32)
        imag = (ia * rb - ra * ib).astype(jnp.bfloat16).astype(jnp.float32)
        real_sum = real if real_sum is None else real_sum + real
        imag_sum = imag if imag_sum is None else imag_sum + imag
    real_stack = (real_sum / WINDOWS).astype(jnp.bfloat16)
    imag_stack = (imag_sum / WINDOWS).astype(jnp.bfloat16)
    total = jnp.dot(real_stack, cos_ref[...], preferred_element_type=jnp.float32)
    return total + jnp.dot(imag_stack, sin_ref[...], preferred_element_type=jnp.float32)


def flip(x, step, n):
    out = 0
    bit = 1
    while bit < n:
        out = out + ((x // bit + step // bit) % 2) * bit
        bit = bit * 2
    return out


def pair_exchange_kernel(left_hot, right_hot, panel, cos_ref, sin_ref, out_ref, slots, received, local_sem,
                         send_sem, recv_sem):
    n = slots.shape[0]
    me = lax.axis_index("chan")
    group = lax.axis_index("grp")

    barrier = pltpu.get_barrier_semaphore()
    for step in range(1, n):
        pl.semaphore_signal(barrier, inc=1, device_id=(group, lax.rem(me + step, n)),
                            device_id_type=pl.DeviceIdType.MESH)
    pl.semaphore_wait(barrier, n - 1)

    def fill(target):
        slots[target] = pair_rows(left_hot, right_hot, panel, cos_ref, sin_ref, target).astype(slots.dtype)

    def send(step):
        target = flip(me, step, n)
        return pltpu.make_async_remote_copy(
            src_ref=slots.at[target],
            dst_ref=received.at[me],
            send_sem=send_sem.at[step],
            recv_sem=recv_sem.at[step],
            device_id=(group, target),
            device_id_type=pl.DeviceIdType.MESH,
        )

    def one_step(step, carry):
        fill(flip(me, step, n))

        @pl.when(step > 1)
        def _():
            send(step - 1).start()

        return carry

    lax.fori_loop(1, n, one_step, 0)
    fill(me)
    send(n - 1).start()
    own = pltpu.make_async_copy(slots.at[me], received.at[me], local_sem)
    own.start()
    own.wait()

    def finish(step, carry):
        send(step).wait_send()
        source = flip(me, step, n)
        pltpu.make_async_remote_copy(
            src_ref=slots.at[source],
            dst_ref=received.at[source],
            send_sem=send_sem.at[step],
            recv_sem=recv_sem.at[step],
            device_id=(group, source),
            device_id_type=pl.DeviceIdType.MESH,
        ).wait_recv()
        return carry

    lax.fori_loop(1, n, finish, 0)
    total = received[0].astype(jnp.float32)
    for source in range(1, n):
        total = total + received[source].astype(jnp.float32)
    listed = out_ref.shape[0]
    lags = cos_ref.shape[1]
    for pq in range(total.shape[0] // listed):
        out_ref[:, pq * lags:(pq + 1) * lags] = total[pq * listed:(pq + 1) * listed]


def pair_exchange(left_hot, right_hot, panel, cos_part, sin_part, chan_count, collective):
    rows = left_hot.shape[0]
    count = rows // chan_count
    left_hot = left_hot.reshape(chan_count, count, -1)
    right_hot = right_hot.reshape(chan_count, count, -1)
    part = cos_part.shape[0]
    pairs = BLK * BLK
    vmem = pl.BlockSpec(memory_space=pltpu.VMEM)
    flops = 2 * 2 * rows * panel.size + 2 * 2 * rows * part * LAGS
    return pl.pallas_call(
        pair_exchange_kernel,
        out_shape=jax.ShapeDtypeStruct((count // pairs, pairs * LAGS), jnp.float32),
        in_specs=[vmem] * 5,
        out_specs=vmem,
        scratch_shapes=[
            pltpu.VMEM((chan_count, count, LAGS), jnp.bfloat16),
            pltpu.VMEM((chan_count, count, LAGS), jnp.bfloat16),
            pltpu.SemaphoreType.DMA(()),
            pltpu.SemaphoreType.DMA((chan_count,)),
            pltpu.SemaphoreType.DMA((chan_count,)),
        ],
        compiler_params=pltpu.CompilerParams(
            collective_id=collective, has_side_effects=True, vmem_limit_bytes=56 * 1024 * 1024
        ),
        cost_estimate=pl.CostEstimate(
            flops=flops,
            transcendentals=0,
            bytes_accessed=panel.size * 2 + 4 * part * LAGS + rows * LAGS * 2,
        ),
    )(left_hot, right_hot, panel, cos_part, sin_part)


def exchange_kernel(axis, other_axis, axis_first, stride, x_ref, out_ref, local_sem, send_sem, recv_sem):
    n = x_ref.shape[0]
    index = lax.axis_index(axis)
    me = lax.rem(index // stride, n)
    base = index - me * stride
    other = lax.axis_index(other_axis)

    def device(j):
        coord = base + stride * j
        return (coord, other) if axis_first else (other, coord)

    barrier = pltpu.get_barrier_semaphore()
    for step in range(1, n):
        pl.semaphore_signal(barrier, inc=1, device_id=device(lax.rem(me + step, n)),
                            device_id_type=pl.DeviceIdType.MESH)
    pl.semaphore_wait(barrier, n - 1)

    pieces = x_ref.shape[1]
    own = pltpu.make_async_copy(x_ref.at[me], out_ref.at[me], local_sem)
    own.start()
    copies = []
    for step in range(1, n):
        target = lax.rem(me + step, n)
        for piece in range(pieces):
            copy = pltpu.make_async_remote_copy(
                src_ref=x_ref.at[target, piece],
                dst_ref=out_ref.at[me, piece],
                send_sem=send_sem.at[step, piece],
                recv_sem=recv_sem.at[step, piece],
                device_id=device(target),
                device_id_type=pl.DeviceIdType.MESH,
            )
            copy.start()
            copies.append(copy)
    own.wait()
    for step in range(1, n):
        source = lax.rem(me + n - step, n)
        for piece in range(pieces):
            copies[(step - 1) * pieces + piece].wait_send()
            incoming = pltpu.make_async_remote_copy(
                src_ref=x_ref.at[source, piece],
                dst_ref=out_ref.at[source, piece],
                send_sem=send_sem.at[step, piece],
                recv_sem=recv_sem.at[step, piece],
                device_id=device(source),
                device_id_type=pl.DeviceIdType.MESH,
            )
            incoming.wait_recv()


def exchange(x, axis, other_axis, axis_first, stride, collective):
    n = x.shape[0]
    vmem = pl.BlockSpec(memory_space=pltpu.VMEM)
    return pl.pallas_call(
        functools.partial(exchange_kernel, axis, other_axis, axis_first, stride),
        out_shape=jax.ShapeDtypeStruct(x.shape, x.dtype),
        in_specs=[vmem],
        out_specs=vmem,
        scratch_shapes=[
            pltpu.SemaphoreType.DMA(()),
            pltpu.SemaphoreType.DMA((n, x.shape[1])),
            pltpu.SemaphoreType.DMA((n, x.shape[1])),
        ],
        compiler_params=pltpu.CompilerParams(collective_id=collective, has_side_effects=True),
    )(x)


def local(spectra, pair_blocks, owners):
    groups_count = lax.axis_size("grp")
    chan_count = lax.axis_size("chan")
    slot_count = groups_count * MOST
    pairs = BLK * BLK
    part = F // chan_count
    me = lax.axis_index("chan")

    channels = spectra.shape[0]
    sent = whiten_chunks(spectra, pair_blocks, chan_count)
    got = lax.all_to_all(sent, "chan", split_axis=0, concat_axis=0, tiled=True)
    rows_per = channels * WINDOWS * 2
    group_channels = chan_count * channels
    panel = got
    all_blocks = got[:, rows_per, : NB_SRC * 2].astype(jnp.float32).astype(jnp.int32)
    all_blocks = all_blocks.reshape(chan_count * NB_SRC, 1, 2)
    offsets = jnp.arange(BLK, dtype=jnp.int32)
    left_ch = (all_blocks[:, :, 0] * BLK + offsets[None, :])[:, :, None] + jnp.zeros((1, 1, BLK), jnp.int32)
    right_ch = (all_blocks[:, :, 1] * BLK + offsets[None, :])[:, None, :] + jnp.zeros((1, BLK, 1), jnp.int32)
    channel_ids = jnp.arange(group_channels, dtype=jnp.int32)[None, :]
    left_ch = left_ch.reshape(chan_count, NB_SRC, BLK, BLK).transpose(0, 2, 3, 1)
    right_ch = right_ch.reshape(chan_count, NB_SRC, BLK, BLK).transpose(0, 2, 3, 1)
    left_hot = (left_ch.reshape(-1, 1) == channel_ids).astype(jnp.bfloat16)
    right_hot = (right_ch.reshape(-1, 1) == channel_ids).astype(jnp.bfloat16)

    cos_part, sin_part = table_slice(me * part, part)
    corr = pair_exchange(left_hot, right_hot, panel, cos_part, sin_part, chan_count, 0)

    owner_list = owners[0, 0, :, 0]
    same = owner_list[:, None] == owner_list[None, :]
    earlier = jnp.arange(NB_SRC)[None, :] < jnp.arange(NB_SRC)[:, None]
    order_rank = jnp.sum(jnp.logical_and(same, earlier), axis=1)
    slot_ids = owner_list * MOST + order_rank
    chooser = (slot_ids[None, :] == jnp.arange(slot_count, dtype=jnp.int32)[:, None]).astype(jnp.bfloat16)
    placed = jnp.dot(chooser, corr.astype(jnp.bfloat16), preferred_element_type=jnp.float32)
    placed = placed.reshape(groups_count, 1, MOST, pairs, LAGS).astype(jnp.bfloat16)
    received = exchange(placed, "grp", "chan", True, 1, 1).astype(jnp.float32)
    return received.reshape(1, 1, slot_count, pairs, LAGS)


def solution(mesh):
    return jax.shard_map(
        local,
        mesh=mesh,
        in_specs=(
            P(("grp", "chan"), None, None, None),
            P("grp", "chan", None, None),
            P("grp", "chan", None, None),
        ),
        out_specs=P("grp", "chan", None, None, None),
        check_vma=False,
    )
```

```python
import functools

import jax
import jax.numpy as jnp
from jax import lax
from jax.experimental import pallas as pl
from jax.experimental.pallas import tpu as pltpu
from jax.sharding import PartitionSpec as P

F = 8192
LAGS = 1024
BLK = 2
NB_SRC = 18
MOST = 3
WINDOWS = 2
FINE = 128


def phase_angle(bins, lag_index):
    phase = bins[:, None] * lag_index[None, :] % (2 * F)
    return phase.astype(jnp.float32) * (jnp.pi / F)


def table_slice(start, count):
    lag_index = jnp.arange(LAGS, dtype=jnp.int32) - LAGS // 2
    coarse = phase_angle(start + FINE * jnp.arange(count // FINE, dtype=jnp.int32), lag_index)
    fine = phase_angle(jnp.arange(FINE, dtype=jnp.int32), lag_index)
    cos_a, sin_a = jnp.cos(coarse)[:, None, :], jnp.sin(coarse)[:, None, :]
    cos_b, sin_b = jnp.cos(fine)[None, :, :], jnp.sin(fine)[None, :, :]
    cos_ab = (cos_a * cos_b - sin_a * sin_b).reshape(count, LAGS)
    sin_ab = (sin_a * cos_b + cos_a * sin_b).reshape(count, LAGS)
    bins = start + jnp.arange(count, dtype=jnp.int32)
    weight = (jnp.where(bins == 0, 1.0, 2.0).astype(jnp.float32) / jnp.sqrt(jnp.float32(F)))[:, None]
    cos_part = (cos_ab * weight).astype(jnp.bfloat16)
    sin_part = (-sin_ab * weight).astype(jnp.bfloat16)
    return cos_part, sin_part


def whiten_kernel(x_ref, blocks_ref, out_ref):
    x = x_ref[...].astype(jnp.float32)
    rows = x.shape[0]
    square = x * x
    after = pltpu.roll(square, rows - 1, 0)
    before = pltpu.roll(square, 1, 0)
    odd = lax.broadcasted_iota(jnp.int32, x.shape, 0) % 2 == 1
    power = jnp.where(odd, before + square, square + after)
    level = jnp.mean(power, axis=-1, keepdims=True) + 1e-05
    white = (x * lax.rsqrt(power + 0.1 * level)).astype(out_ref.dtype)
    channels = rows // (WINDOWS * 2)
    dest = lax.broadcasted_iota(jnp.int32, (rows, rows), 0)
    source = lax.broadcasted_iota(jnp.int32, (rows, rows), 1)
    order = (source == (dest % channels) * (WINDOWS * 2) + dest // channels).astype(white.dtype)
    white = jnp.dot(order, white, preferred_element_type=jnp.float32).astype(out_ref.dtype)
    part = out_ref.shape[2]
    lane = lax.broadcasted_iota(jnp.int32, (1, part), 1)
    extra = jnp.zeros((1, part), jnp.float32)
    for pair in range(blocks_ref.shape[2]):
        for side in range(2):
            value = blocks_ref[0, 0, pair, side].astype(jnp.float32)
            extra = jnp.where(lane == pair * 2 + side, value, extra)
    extra = extra.astype(out_ref.dtype)
    for chunk in range(out_ref.shape[0]):
        out_ref[chunk, :rows, :] = white[:, chunk * part:(chunk + 1) * part]
        out_ref[chunk, rows:, :] = extra


def whiten_chunks(spectra, pair_blocks, chan_count):
    channels = spectra.shape[0]
    rows = channels * WINDOWS * 2
    x = spectra.reshape(rows, F)
    vmem = pl.BlockSpec(memory_space=pltpu.VMEM)
    return pl.pallas_call(
        whiten_kernel,
        out_shape=jax.ShapeDtypeStruct((chan_count, rows + 1, F // chan_count), jnp.bfloat16),
        in_specs=[vmem, pl.BlockSpec(memory_space=pltpu.SMEM)],
        out_specs=vmem,
        compiler_params=pltpu.CompilerParams(vmem_limit_bytes=48 * 1024 * 1024),
        cost_estimate=pl.CostEstimate(flops=8 * rows * F, transcendentals=rows * F, bytes_accessed=4 * rows * F),
    )(x, pair_blocks)


def pair_rows(left_hot, right_hot, panel, cos_ref, sin_ref, target):
    part = cos_ref.shape[0]
    left = left_hot[target]
    right = right_hot[target]

    sources = panel.shape[0]
    channels = (panel.shape[1] - 1) // (WINDOWS * 2)

    def rows_of(hot, window, kind):
        at = (window * 2 + kind) * channels
        cols = panel[:, at:at + channels, :].reshape(sources * channels, part)
        return jnp.dot(hot, cols, preferred_element_type=jnp.float32)

    real_sum = None
    imag_sum = None
    for window in range(WINDOWS):
        ra = rows_of(left, window, 0)
        ia = rows_of(left, window, 1)
        rb = rows_of(right, window, 0)
        ib = rows_of(right, window, 1)
        real = (ra * rb + ia * ib).astype(jnp.bfloat16).astype(jnp.float32)
        imag = (ia * rb - ra * ib).astype(jnp.bfloat16).astype(jnp.float32)
        real_sum = real if real_sum is None else real_sum + real
        imag_sum = imag if imag_sum is None else imag_sum + imag
    real_stack = (real_sum / WINDOWS).astype(jnp.bfloat16)
    imag_stack = (imag_sum / WINDOWS).astype(jnp.bfloat16)
    total = jnp.dot(real_stack, cos_ref[...], preferred_element_type=jnp.float32)
    return total + jnp.dot(imag_stack, sin_ref[...], preferred_element_type=jnp.float32)


def pair_exchange_kernel(left_hot, right_hot, panel, cos_ref, sin_ref, out_ref, slots, received, local_sem,
                         send_sem, recv_sem):
    n = slots.shape[0]
    me = lax.axis_index("chan")
    group = lax.axis_index("grp")

    barrier = pltpu.get_barrier_semaphore()
    for step in range(1, n):
        pl.semaphore_signal(barrier, inc=1, device_id=(group, lax.rem(me + step, n)),
                            device_id_type=pl.DeviceIdType.MESH)
    pl.semaphore_wait(barrier, n - 1)

    parity = me % 2

    def offset(step):
        return step + parity * ((step + n - 3) % (n - 1) + 1 - step)

    def fill(target):
        slots[target] = pair_rows(left_hot, right_hot, panel, cos_ref, sin_ref, target).astype(slots.dtype)

    def send(step):
        target = lax.rem(me + offset(step), n)
        return pltpu.make_async_remote_copy(
            src_ref=slots.at[target],
            dst_ref=received.at[me],
            send_sem=send_sem.at[step],
            recv_sem=recv_sem.at[offset(step)],
            device_id=(group, target),
            device_id_type=pl.DeviceIdType.MESH,
        )

    def one_step(step, carry):
        fill(lax.rem(me + offset(step), n))

        @pl.when(step > 1)
        def _():
            send(step - 1).start()

        return carry

    lax.fori_loop(1, n, one_step, 0)
    fill(me)
    send(n - 1).start()
    own = pltpu.make_async_copy(slots.at[me], received.at[me], local_sem)
    own.start()
    own.wait()

    def finish(step, carry):
        send(step).wait_send()
        distance = step
        source = lax.rem(me + n - distance, n)
        pltpu.make_async_remote_copy(
            src_ref=slots.at[source],
            dst_ref=received.at[source],
            send_sem=send_sem.at[step],
            recv_sem=recv_sem.at[distance],
            device_id=(group, source),
            device_id_type=pl.DeviceIdType.MESH,
        ).wait_recv()
        return carry

    lax.fori_loop(1, n, finish, 0)
    total = received[0].astype(jnp.float32)
    for source in range(1, n):
        total = total + received[source].astype(jnp.float32)
    listed = out_ref.shape[0]
    lags = cos_ref.shape[1]
    for pq in range(total.shape[0] // listed):
        out_ref[:, pq * lags:(pq + 1) * lags] = total[pq * listed:(pq + 1) * listed]


def pair_exchange(left_hot, right_hot, panel, cos_part, sin_part, chan_count, collective):
    rows = left_hot.shape[0]
    count = rows // chan_count
    left_hot = left_hot.reshape(chan_count, count, -1)
    right_hot = right_hot.reshape(chan_count, count, -1)
    part = cos_part.shape[0]
    pairs = BLK * BLK
    vmem = pl.BlockSpec(memory_space=pltpu.VMEM)
    flops = 2 * 2 * rows * panel.size + 2 * 2 * rows * part * LAGS
    return pl.pallas_call(
        pair_exchange_kernel,
        out_shape=jax.ShapeDtypeStruct((count // pairs, pairs * LAGS), jnp.float32),
        in_specs=[vmem] * 5,
        out_specs=vmem,
        scratch_shapes=[
            pltpu.VMEM((chan_count, count, LAGS), jnp.bfloat16),
            pltpu.VMEM((chan_count, count, LAGS), jnp.bfloat16),
            pltpu.SemaphoreType.DMA(()),
            pltpu.SemaphoreType.DMA((chan_count,)),
            pltpu.SemaphoreType.DMA((chan_count,)),
        ],
        compiler_params=pltpu.CompilerParams(
            collective_id=collective, has_side_effects=True, vmem_limit_bytes=56 * 1024 * 1024
        ),
        cost_estimate=pl.CostEstimate(
            flops=flops,
            transcendentals=0,
            bytes_accessed=panel.size * 2 + 4 * part * LAGS + rows * LAGS * 2,
        ),
    )(left_hot, right_hot, panel, cos_part, sin_part)


def exchange_kernel(axis, other_axis, axis_first, stride, x_ref, out_ref, local_sem, send_sem, recv_sem):
    n = x_ref.shape[0]
    index = lax.axis_index(axis)
    me = lax.rem(index // stride, n)
    base = index - me * stride
    other = lax.axis_index(other_axis)

    def device(j):
        coord = base + stride * j
        return (coord, other) if axis_first else (other, coord)

    barrier = pltpu.get_barrier_semaphore()
    for step in range(1, n):
        pl.semaphore_signal(barrier, inc=1, device_id=device(lax.rem(me + step, n)),
                            device_id_type=pl.DeviceIdType.MESH)
    pl.semaphore_wait(barrier, n - 1)

    pieces = x_ref.shape[1]
    own = pltpu.make_async_copy(x_ref.at[me], out_ref.at[me], local_sem)
    own.start()
    copies = []
    for step in range(1, n):
        target = lax.rem(me + step, n)
        for piece in range(pieces):
            copy = pltpu.make_async_remote_copy(
                src_ref=x_ref.at[target, piece],
                dst_ref=out_ref.at[me, piece],
                send_sem=send_sem.at[step, piece],
                recv_sem=recv_sem.at[step, piece],
                device_id=device(target),
                device_id_type=pl.DeviceIdType.MESH,
            )
            copy.start()
            copies.append(copy)
    own.wait()
    for step in range(1, n):
        source = lax.rem(me + n - step, n)
        for piece in range(pieces):
            copies[(step - 1) * pieces + piece].wait_send()
            incoming = pltpu.make_async_remote_copy(
                src_ref=x_ref.at[source, piece],
                dst_ref=out_ref.at[source, piece],
                send_sem=send_sem.at[step, piece],
                recv_sem=recv_sem.at[step, piece],
                device_id=device(source),
                device_id_type=pl.DeviceIdType.MESH,
            )
            incoming.wait_recv()


def exchange(x, axis, other_axis, axis_first, stride, collective):
    n = x.shape[0]
    vmem = pl.BlockSpec(memory_space=pltpu.VMEM)
    return pl.pallas_call(
        functools.partial(exchange_kernel, axis, other_axis, axis_first, stride),
        out_shape=jax.ShapeDtypeStruct(x.shape, x.dtype),
        in_specs=[vmem],
        out_specs=vmem,
        scratch_shapes=[
            pltpu.SemaphoreType.DMA(()),
            pltpu.SemaphoreType.DMA((n, x.shape[1])),
            pltpu.SemaphoreType.DMA((n, x.shape[1])),
        ],
        compiler_params=pltpu.CompilerParams(collective_id=collective, has_side_effects=True),
    )(x)


def local(spectra, pair_blocks, owners):
    groups_count = lax.axis_size("grp")
    chan_count = lax.axis_size("chan")
    slot_count = groups_count * MOST
    pairs = BLK * BLK
    part = F // chan_count
    me = lax.axis_index("chan")

    channels = spectra.shape[0]
    sent = whiten_chunks(spectra, pair_blocks, chan_count)
    got = lax.all_to_all(sent, "chan", split_axis=0, concat_axis=0, tiled=True)
    rows_per = channels * WINDOWS * 2
    group_channels = chan_count * channels
    panel = got
    all_blocks = got[:, rows_per, : NB_SRC * 2].astype(jnp.float32).astype(jnp.int32)
    all_blocks = all_blocks.reshape(chan_count * NB_SRC, 1, 2)
    offsets = jnp.arange(BLK, dtype=jnp.int32)
    left_ch = (all_blocks[:, :, 0] * BLK + offsets[None, :])[:, :, None] + jnp.zeros((1, 1, BLK), jnp.int32)
    right_ch = (all_blocks[:, :, 1] * BLK + offsets[None, :])[:, None, :] + jnp.zeros((1, BLK, 1), jnp.int32)
    channel_ids = jnp.arange(group_channels, dtype=jnp.int32)[None, :]
    left_ch = left_ch.reshape(chan_count, NB_SRC, BLK, BLK).transpose(0, 2, 3, 1)
    right_ch = right_ch.reshape(chan_count, NB_SRC, BLK, BLK).transpose(0, 2, 3, 1)
    left_hot = (left_ch.reshape(-1, 1) == channel_ids).astype(jnp.bfloat16)
    right_hot = (right_ch.reshape(-1, 1) == channel_ids).astype(jnp.bfloat16)

    cos_part, sin_part = table_slice(me * part, part)
    corr = pair_exchange(left_hot, right_hot, panel, cos_part, sin_part, chan_count, 0)

    owner_list = owners[0, 0, :, 0]
    same = owner_list[:, None] == owner_list[None, :]
    earlier = jnp.arange(NB_SRC)[None, :] < jnp.arange(NB_SRC)[:, None]
    order_rank = jnp.sum(jnp.logical_and(same, earlier), axis=1)
    slot_ids = owner_list * MOST + order_rank
    chooser = (slot_ids[None, :] == jnp.arange(slot_count, dtype=jnp.int32)[:, None]).astype(jnp.bfloat16)
    placed = jnp.dot(chooser, corr.astype(jnp.bfloat16), preferred_element_type=jnp.float32)
    placed = placed.reshape(groups_count, 1, MOST, pairs, LAGS).astype(jnp.bfloat16)
    received = exchange(placed, "grp", "chan", True, 1, 1).astype(jnp.float32)
    return received.reshape(1, 1, slot_count, pairs, LAGS)


def solution(mesh):
    return jax.shard_map(
        local,
        mesh=mesh,
        in_specs=(
            P(("grp", "chan"), None, None, None),
            P("grp", "chan", None, None),
            P("grp", "chan", None, None),
        ),
        out_specs=P("grp", "chan", None, None, None),
        check_vma=False,
    )
```

```python
import functools

import jax
import jax.numpy as jnp
from jax import lax
from jax.experimental import pallas as pl
from jax.experimental.pallas import tpu as pltpu
from jax.sharding import PartitionSpec as P

F = 8192
LAGS = 1024
BLK = 2
NB_SRC = 18
MOST = 3
WINDOWS = 2
FINE = 128


def phase_angle(bins, lag_index):
    phase = bins[:, None] * lag_index[None, :] % (2 * F)
    return phase.astype(jnp.float32) * (jnp.pi / F)


def table_slice(start, count):
    lag_index = jnp.arange(LAGS, dtype=jnp.int32) - LAGS // 2
    coarse = phase_angle(start + FINE * jnp.arange(count // FINE, dtype=jnp.int32), lag_index)
    fine = phase_angle(jnp.arange(FINE, dtype=jnp.int32), lag_index)
    cos_a, sin_a = jnp.cos(coarse)[:, None, :], jnp.sin(coarse)[:, None, :]
    cos_b, sin_b = jnp.cos(fine)[None, :, :], jnp.sin(fine)[None, :, :]
    cos_ab = (cos_a * cos_b - sin_a * sin_b).reshape(count, LAGS)
    sin_ab = (sin_a * cos_b + cos_a * sin_b).reshape(count, LAGS)
    bins = start + jnp.arange(count, dtype=jnp.int32)
    weight = (jnp.where(bins == 0, 1.0, 2.0).astype(jnp.float32) / jnp.sqrt(jnp.float32(F)))[:, None]
    cos_part = (cos_ab * weight).astype(jnp.bfloat16)
    sin_part = (-sin_ab * weight).astype(jnp.bfloat16)
    return cos_part, sin_part


def whiten_kernel(x_ref, blocks_ref, out_ref):
    x = x_ref[...].astype(jnp.float32)
    rows = x.shape[0]
    square = x * x
    after = pltpu.roll(square, rows - 1, 0)
    before = pltpu.roll(square, 1, 0)
    odd = lax.broadcasted_iota(jnp.int32, x.shape, 0) % 2 == 1
    power = jnp.where(odd, before + square, square + after)
    level = jnp.mean(power, axis=-1, keepdims=True) + 1e-05
    white = (x * lax.rsqrt(power + 0.1 * level)).astype(out_ref.dtype)
    channels = rows // (WINDOWS * 2)
    dest = lax.broadcasted_iota(jnp.int32, (rows, rows), 0)
    source = lax.broadcasted_iota(jnp.int32, (rows, rows), 1)
    order = (source == (dest % channels) * (WINDOWS * 2) + dest // channels).astype(white.dtype)
    white = jnp.dot(order, white, preferred_element_type=jnp.float32).astype(out_ref.dtype)
    part = out_ref.shape[2]
    lane = lax.broadcasted_iota(jnp.int32, (1, part), 1)
    extra = jnp.zeros((1, part), jnp.float32)
    for pair in range(blocks_ref.shape[2]):
        for side in range(2):
            value = blocks_ref[0, 0, pair, side].astype(jnp.float32)
            extra = jnp.where(lane == pair * 2 + side, value, extra)
    extra = extra.astype(out_ref.dtype)
    for chunk in range(out_ref.shape[0]):
        out_ref[chunk, :rows, :] = white[:, chunk * part:(chunk + 1) * part]
        out_ref[chunk, rows:, :] = extra


def whiten_chunks(spectra, pair_blocks, chan_count):
    channels = spectra.shape[0]
    rows = channels * WINDOWS * 2
    x = spectra.reshape(rows, F)
    vmem = pl.BlockSpec(memory_space=pltpu.VMEM)
    return pl.pallas_call(
        whiten_kernel,
        out_shape=jax.ShapeDtypeStruct((chan_count, rows + 1, F // chan_count), jnp.bfloat16),
        in_specs=[vmem, pl.BlockSpec(memory_space=pltpu.SMEM)],
        out_specs=vmem,
        compiler_params=pltpu.CompilerParams(vmem_limit_bytes=48 * 1024 * 1024),
        cost_estimate=pl.CostEstimate(flops=8 * rows * F, transcendentals=rows * F, bytes_accessed=4 * rows * F),
    )(x, pair_blocks)


def pair_rows(left_hot, right_hot, panel, cos_ref, sin_ref, target):
    part = cos_ref.shape[0]
    left = left_hot[target]
    right = right_hot[target]

    sources = panel.shape[0]
    channels = (panel.shape[1] - 1) // (WINDOWS * 2)

    def rows_of(hot, window, kind):
        at = (window * 2 + kind) * channels
        cols = panel[:, at:at + channels, :].reshape(sources * channels, part)
        return jnp.dot(hot, cols, preferred_element_type=jnp.float32)

    real_sum = None
    imag_sum = None
    for window in range(WINDOWS):
        ra = rows_of(left, window, 0)
        ia = rows_of(left, window, 1)
        rb = rows_of(right, window, 0)
        ib = rows_of(right, window, 1)
        real = (ra * rb + ia * ib).astype(jnp.bfloat16).astype(jnp.float32)
        imag = (ia * rb - ra * ib).astype(jnp.bfloat16).astype(jnp.float32)
        real_sum = real if real_sum is None else real_sum + real
        imag_sum = imag if imag_sum is None else imag_sum + imag
    real_stack = (real_sum / WINDOWS).astype(jnp.bfloat16)
    imag_stack = (imag_sum / WINDOWS).astype(jnp.bfloat16)
    total = jnp.dot(real_stack, cos_ref[...], preferred_element_type=jnp.float32)
    return total + jnp.dot(imag_stack, sin_ref[...], preferred_element_type=jnp.float32)


def pair_exchange_kernel(left_hot, right_hot, panel, cos_ref, sin_ref, out_ref, slots, received, local_sem,
                         send_sem, recv_sem):
    n = slots.shape[0]
    me = lax.axis_index("chan")
    group = lax.axis_index("grp")

    def fill(target):
        slots[target] = pair_rows(left_hot, right_hot, panel, cos_ref, sin_ref, target).astype(slots.dtype)

    def send(step):
        target = lax.rem(me + step, n)
        return pltpu.make_async_remote_copy(
            src_ref=slots.at[target],
            dst_ref=received.at[me],
            send_sem=send_sem.at[step],
            recv_sem=recv_sem.at[step],
            device_id=(group, target),
            device_id_type=pl.DeviceIdType.MESH,
        )

    def one_step(step, carry):
        fill(lax.rem(me + step, n))
        send(step - 1).start()

        return carry

    fill(lax.rem(me + 1, n))
    barrier = pltpu.get_barrier_semaphore()
    for step in range(1, n):
        pl.semaphore_signal(barrier, inc=1, device_id=(group, lax.rem(me + step, n)),
                            device_id_type=pl.DeviceIdType.MESH)
    pl.semaphore_wait(barrier, n - 1)
    lax.fori_loop(2, n, one_step, 0)
    fill(me)
    send(n - 1).start()
    own = pltpu.make_async_copy(slots.at[me], received.at[me], local_sem)
    own.start()
    own.wait()

    def finish(step, carry):
        send(step).wait_send()
        source = lax.rem(me + n - step, n)
        pltpu.make_async_remote_copy(
            src_ref=slots.at[source],
            dst_ref=received.at[source],
            send_sem=send_sem.at[step],
            recv_sem=recv_sem.at[step],
            device_id=(group, source),
            device_id_type=pl.DeviceIdType.MESH,
        ).wait_recv()
        return carry

    lax.fori_loop(1, n, finish, 0)
    total = received[0].astype(jnp.float32)
    for source in range(1, n):
        total = total + received[source].astype(jnp.float32)
    listed = out_ref.shape[0]
    lags = cos_ref.shape[1]
    for pq in range(total.shape[0] // listed):
        out_ref[:, pq * lags:(pq + 1) * lags] = total[pq * listed:(pq + 1) * listed]


def pair_exchange(left_hot, right_hot, panel, cos_part, sin_part, chan_count, collective):
    rows = left_hot.shape[0]
    count = rows // chan_count
    left_hot = left_hot.reshape(chan_count, count, -1)
    right_hot = right_hot.reshape(chan_count, count, -1)
    part = cos_part.shape[0]
    pairs = BLK * BLK
    vmem = pl.BlockSpec(memory_space=pltpu.VMEM)
    flops = 2 * 2 * rows * panel.size + 2 * 2 * rows * part * LAGS
    return pl.pallas_call(
        pair_exchange_kernel,
        out_shape=jax.ShapeDtypeStruct((count // pairs, pairs * LAGS), jnp.float32),
        in_specs=[vmem] * 5,
        out_specs=vmem,
        scratch_shapes=[
            pltpu.VMEM((chan_count, count, LAGS), jnp.bfloat16),
            pltpu.VMEM((chan_count, count, LAGS), jnp.bfloat16),
            pltpu.SemaphoreType.DMA(()),
            pltpu.SemaphoreType.DMA((chan_count,)),
            pltpu.SemaphoreType.DMA((chan_count,)),
        ],
        compiler_params=pltpu.CompilerParams(
            collective_id=collective, has_side_effects=True, vmem_limit_bytes=56 * 1024 * 1024
        ),
        cost_estimate=pl.CostEstimate(
            flops=flops,
            transcendentals=0,
            bytes_accessed=panel.size * 2 + 4 * part * LAGS + rows * LAGS * 2,
        ),
    )(left_hot, right_hot, panel, cos_part, sin_part)


def exchange_kernel(axis, other_axis, axis_first, stride, x_ref, out_ref, local_sem, send_sem, recv_sem):
    n = x_ref.shape[0]
    index = lax.axis_index(axis)
    me = lax.rem(index // stride, n)
    base = index - me * stride
    other = lax.axis_index(other_axis)

    def device(j):
        coord = base + stride * j
        return (coord, other) if axis_first else (other, coord)

    barrier = pltpu.get_barrier_semaphore()
    for step in range(1, n):
        pl.semaphore_signal(barrier, inc=1, device_id=device(lax.rem(me + step, n)),
                            device_id_type=pl.DeviceIdType.MESH)
    pl.semaphore_wait(barrier, n - 1)

    pieces = x_ref.shape[1]
    own = pltpu.make_async_copy(x_ref.at[me], out_ref.at[me], local_sem)
    own.start()
    copies = []
    for step in range(1, n):
        target = lax.rem(me + step, n)
        for piece in range(pieces):
            copy = pltpu.make_async_remote_copy(
                src_ref=x_ref.at[target, piece],
                dst_ref=out_ref.at[me, piece],
                send_sem=send_sem.at[step, piece],
                recv_sem=recv_sem.at[step, piece],
                device_id=device(target),
                device_id_type=pl.DeviceIdType.MESH,
            )
            copy.start()
            copies.append(copy)
    own.wait()
    for step in range(1, n):
        source = lax.rem(me + n - step, n)
        for piece in range(pieces):
            copies[(step - 1) * pieces + piece].wait_send()
            incoming = pltpu.make_async_remote_copy(
                src_ref=x_ref.at[source, piece],
                dst_ref=out_ref.at[source, piece],
                send_sem=send_sem.at[step, piece],
                recv_sem=recv_sem.at[step, piece],
                device_id=device(source),
                device_id_type=pl.DeviceIdType.MESH,
            )
            incoming.wait_recv()


def exchange(x, axis, other_axis, axis_first, stride, collective):
    n = x.shape[0]
    vmem = pl.BlockSpec(memory_space=pltpu.VMEM)
    return pl.pallas_call(
        functools.partial(exchange_kernel, axis, other_axis, axis_first, stride),
        out_shape=jax.ShapeDtypeStruct(x.shape, x.dtype),
        in_specs=[vmem],
        out_specs=vmem,
        scratch_shapes=[
            pltpu.SemaphoreType.DMA(()),
            pltpu.SemaphoreType.DMA((n, x.shape[1])),
            pltpu.SemaphoreType.DMA((n, x.shape[1])),
        ],
        compiler_params=pltpu.CompilerParams(collective_id=collective, has_side_effects=True),
    )(x)


def local(spectra, pair_blocks, owners):
    groups_count = lax.axis_size("grp")
    chan_count = lax.axis_size("chan")
    slot_count = groups_count * MOST
    pairs = BLK * BLK
    part = F // chan_count
    me = lax.axis_index("chan")

    channels = spectra.shape[0]
    sent = whiten_chunks(spectra, pair_blocks, chan_count)
    got = lax.all_to_all(sent, "chan", split_axis=0, concat_axis=0, tiled=True)
    rows_per = channels * WINDOWS * 2
    group_channels = chan_count * channels
    panel = got
    all_blocks = got[:, rows_per, : NB_SRC * 2].astype(jnp.float32).astype(jnp.int32)
    all_blocks = all_blocks.reshape(chan_count * NB_SRC, 1, 2)
    offsets = jnp.arange(BLK, dtype=jnp.int32)
    left_ch = (all_blocks[:, :, 0] * BLK + offsets[None, :])[:, :, None] + jnp.zeros((1, 1, BLK), jnp.int32)
    right_ch = (all_blocks[:, :, 1] * BLK + offsets[None, :])[:, None, :] + jnp.zeros((1, BLK, 1), jnp.int32)
    channel_ids = jnp.arange(group_channels, dtype=jnp.int32)[None, :]
    left_ch = left_ch.reshape(chan_count, NB_SRC, BLK, BLK).transpose(0, 2, 3, 1)
    right_ch = right_ch.reshape(chan_count, NB_SRC, BLK, BLK).transpose(0, 2, 3, 1)
    left_hot = (left_ch.reshape(-1, 1) == channel_ids).astype(jnp.bfloat16)
    right_hot = (right_ch.reshape(-1, 1) == channel_ids).astype(jnp.bfloat16)

    cos_part, sin_part = table_slice(me * part, part)
    corr = pair_exchange(left_hot, right_hot, panel, cos_part, sin_part, chan_count, 0)

    owner_list = owners[0, 0, :, 0]
    same = owner_list[:, None] == owner_list[None, :]
    earlier = jnp.arange(NB_SRC)[None, :] < jnp.arange(NB_SRC)[:, None]
    order_rank = jnp.sum(jnp.logical_and(same, earlier), axis=1)
    slot_ids = owner_list * MOST + order_rank
    chooser = (slot_ids[None, :] == jnp.arange(slot_count, dtype=jnp.int32)[:, None]).astype(jnp.bfloat16)
    placed = jnp.dot(chooser, corr.astype(jnp.bfloat16), preferred_element_type=jnp.float32)
    placed = placed.reshape(groups_count, 1, MOST, pairs, LAGS).astype(jnp.bfloat16)
    received = exchange(placed, "grp", "chan", True, 1, 1).astype(jnp.float32)
    return received.reshape(1, 1, slot_count, pairs, LAGS)


def solution(mesh):
    return jax.shard_map(
        local,
        mesh=mesh,
        in_specs=(
            P(("grp", "chan"), None, None, None),
            P("grp", "chan", None, None),
            P("grp", "chan", None, None),
        ),
        out_specs=P("grp", "chan", None, None, None),
        check_vma=False,
    )
```

```python
import functools

import jax
import jax.numpy as jnp
from jax import lax
from jax.experimental import pallas as pl
from jax.experimental.pallas import tpu as pltpu
from jax.sharding import PartitionSpec as P

F = 8192
LAGS = 1024
BLK = 2
NB_SRC = 18
MOST = 3
WINDOWS = 2
FINE = 128


def phase_angle(bins, lag_index):
    phase = bins[:, None] * lag_index[None, :] % (2 * F)
    return phase.astype(jnp.float32) * (jnp.pi / F)


def table_slice(start, count):
    lag_index = jnp.arange(LAGS, dtype=jnp.int32) - LAGS // 2
    coarse = phase_angle(start + FINE * jnp.arange(count // FINE, dtype=jnp.int32), lag_index)
    fine = phase_angle(jnp.arange(FINE, dtype=jnp.int32), lag_index)
    cos_a, sin_a = jnp.cos(coarse)[:, None, :], jnp.sin(coarse)[:, None, :]
    cos_b, sin_b = jnp.cos(fine)[None, :, :], jnp.sin(fine)[None, :, :]
    cos_ab = (cos_a * cos_b - sin_a * sin_b).reshape(count, LAGS)
    sin_ab = (sin_a * cos_b + cos_a * sin_b).reshape(count, LAGS)
    bins = start + jnp.arange(count, dtype=jnp.int32)
    weight = (jnp.where(bins == 0, 1.0, 2.0).astype(jnp.float32) / jnp.sqrt(jnp.float32(F)))[:, None]
    cos_part = (cos_ab * weight).astype(jnp.bfloat16)
    sin_part = (-sin_ab * weight).astype(jnp.bfloat16)
    return cos_part, sin_part


def whiten_kernel(x_ref, blocks_ref, out_ref):
    x = x_ref[...].astype(jnp.float32)
    rows = x.shape[0]
    square = x * x
    after = pltpu.roll(square, rows - 1, 0)
    before = pltpu.roll(square, 1, 0)
    odd = lax.broadcasted_iota(jnp.int32, x.shape, 0) % 2 == 1
    power = jnp.where(odd, before + square, square + after)
    level = jnp.mean(power, axis=-1, keepdims=True) + 1e-05
    white = (x * lax.rsqrt(power + 0.1 * level)).astype(out_ref.dtype)
    channels = rows // (WINDOWS * 2)
    dest = lax.broadcasted_iota(jnp.int32, (rows, rows), 0)
    source = lax.broadcasted_iota(jnp.int32, (rows, rows), 1)
    order = (source == (dest % channels) * (WINDOWS * 2) + dest // channels).astype(white.dtype)
    white = jnp.dot(order, white, preferred_element_type=jnp.float32).astype(out_ref.dtype)
    part = out_ref.shape[2]
    lane = lax.broadcasted_iota(jnp.int32, (1, part), 1)
    extra = jnp.zeros((1, part), jnp.float32)
    for pair in range(blocks_ref.shape[2]):
        for side in range(2):
            value = blocks_ref[0, 0, pair, side].astype(jnp.float32)
            extra = jnp.where(lane == pair * 2 + side, value, extra)
    extra = extra.astype(out_ref.dtype)
    for chunk in range(out_ref.shape[0]):
        out_ref[chunk, :rows, :] = white[:, chunk * part:(chunk + 1) * part]
        out_ref[chunk, rows:, :] = extra


def whiten_chunks(spectra, pair_blocks, chan_count):
    channels = spectra.shape[0]
    rows = channels * WINDOWS * 2
    x = spectra.reshape(rows, F)
    vmem = pl.BlockSpec(memory_space=pltpu.VMEM)
    return pl.pallas_call(
        whiten_kernel,
        out_shape=jax.ShapeDtypeStruct((chan_count, rows + 1, F // chan_count), jnp.bfloat16),
        in_specs=[vmem, pl.BlockSpec(memory_space=pltpu.SMEM)],
        out_specs=vmem,
        compiler_params=pltpu.CompilerParams(vmem_limit_bytes=48 * 1024 * 1024),
        cost_estimate=pl.CostEstimate(flops=8 * rows * F, transcendentals=rows * F, bytes_accessed=4 * rows * F),
    )(x, pair_blocks)


def pair_rows(left_hot, right_hot, panel, cos_ref, sin_ref, target):
    part = cos_ref.shape[0]
    left = left_hot[0, target]
    right = left_hot[1, target]

    sources = panel.shape[0]
    channels = (panel.shape[1] - 1) // (WINDOWS * 2)

    def rows_of(hot, window, kind):
        at = (window * 2 + kind) * channels
        cols = panel[:, at:at + channels, :].reshape(sources * channels, part)
        return jnp.dot(hot, cols, preferred_element_type=jnp.float32)

    real_sum = None
    imag_sum = None
    for window in range(WINDOWS):
        ra = rows_of(left, window, 0)
        ia = rows_of(left, window, 1)
        rb = rows_of(right, window, 0)
        ib = rows_of(right, window, 1)
        real = (ra * rb + ia * ib).astype(jnp.bfloat16).astype(jnp.float32)
        imag = (ia * rb - ra * ib).astype(jnp.bfloat16).astype(jnp.float32)
        real_sum = real if real_sum is None else real_sum + real
        imag_sum = imag if imag_sum is None else imag_sum + imag
    real_stack = (real_sum / WINDOWS).astype(jnp.bfloat16)
    imag_stack = (imag_sum / WINDOWS).astype(jnp.bfloat16)
    total = jnp.dot(real_stack, cos_ref[...], preferred_element_type=jnp.float32)
    return total + jnp.dot(imag_stack, sin_ref[...], preferred_element_type=jnp.float32)


def pair_exchange_kernel(left_hot, panel, cos_ref, sin_ref, out_ref, slots, received, local_sem,
                         send_sem, recv_sem):
    n = slots.shape[0]
    me = lax.axis_index("chan")
    group = lax.axis_index("grp")

    barrier = pltpu.get_barrier_semaphore()
    for step in range(1, n):
        pl.semaphore_signal(barrier, inc=1, device_id=(group, lax.rem(me + step, n)),
                            device_id_type=pl.DeviceIdType.MESH)
    pl.semaphore_wait(barrier, n - 1)

    def fill(target):
        slots[target] = pair_rows(left_hot, None, panel, cos_ref, sin_ref, target).astype(slots.dtype)

    def send(step):
        target = lax.rem(me + step, n)
        return pltpu.make_async_remote_copy(
            src_ref=slots.at[target],
            dst_ref=received.at[me],
            send_sem=send_sem.at[step],
            recv_sem=recv_sem.at[step],
            device_id=(group, target),
            device_id_type=pl.DeviceIdType.MESH,
        )

    def one_step(step, carry):
        fill(lax.rem(me + step, n))

        @pl.when(step > 1)
        def _():
            send(step - 1).start()

        return carry

    lax.fori_loop(1, n, one_step, 0)
    fill(me)
    send(n - 1).start()
    own = pltpu.make_async_copy(slots.at[me], received.at[me], local_sem)
    own.start()
    own.wait()

    def finish(step, carry):
        send(step).wait_send()
        source = lax.rem(me + n - step, n)
        pltpu.make_async_remote_copy(
            src_ref=slots.at[source],
            dst_ref=received.at[source],
            send_sem=send_sem.at[step],
            recv_sem=recv_sem.at[step],
            device_id=(group, source),
            device_id_type=pl.DeviceIdType.MESH,
        ).wait_recv()
        return carry

    lax.fori_loop(1, n, finish, 0)
    total = received[0].astype(jnp.float32)
    for source in range(1, n):
        total = total + received[source].astype(jnp.float32)
    listed = out_ref.shape[0]
    lags = cos_ref.shape[1]
    for pq in range(total.shape[0] // listed):
        out_ref[:, pq * lags:(pq + 1) * lags] = total[pq * listed:(pq + 1) * listed]


def pair_exchange(left_hot, right_hot, panel, cos_part, sin_part, chan_count, collective):
    rows = left_hot.shape[0]
    count = rows // chan_count
    hots = jnp.stack([left_hot, right_hot]).reshape(2, chan_count, count, -1)
    part = cos_part.shape[0]
    pairs = BLK * BLK
    vmem = pl.BlockSpec(memory_space=pltpu.VMEM)
    flops = 2 * 2 * rows * panel.size + 2 * 2 * rows * part * LAGS
    return pl.pallas_call(
        pair_exchange_kernel,
        out_shape=jax.ShapeDtypeStruct((count // pairs, pairs * LAGS), jnp.float32),
        in_specs=[vmem] * 4,
        out_specs=vmem,
        scratch_shapes=[
            pltpu.VMEM((chan_count, count, LAGS), jnp.bfloat16),
            pltpu.VMEM((chan_count, count, LAGS), jnp.bfloat16),
            pltpu.SemaphoreType.DMA(()),
            pltpu.SemaphoreType.DMA((chan_count,)),
            pltpu.SemaphoreType.DMA((chan_count,)),
        ],
        compiler_params=pltpu.CompilerParams(
            collective_id=collective, has_side_effects=True, vmem_limit_bytes=56 * 1024 * 1024
        ),
        cost_estimate=pl.CostEstimate(
            flops=flops,
            transcendentals=0,
            bytes_accessed=panel.size * 2 + 4 * part * LAGS + rows * LAGS * 2,
        ),
    )(hots, panel, cos_part, sin_part)


def exchange_kernel(axis, other_axis, axis_first, stride, x_ref, out_ref, local_sem, send_sem, recv_sem):
    n = x_ref.shape[0]
    index = lax.axis_index(axis)
    me = lax.rem(index // stride, n)
    base = index - me * stride
    other = lax.axis_index(other_axis)

    def device(j):
        coord = base + stride * j
        return (coord, other) if axis_first else (other, coord)

    barrier = pltpu.get_barrier_semaphore()
    for step in range(1, n):
        pl.semaphore_signal(barrier, inc=1, device_id=device(lax.rem(me + step, n)),
                            device_id_type=pl.DeviceIdType.MESH)
    pl.semaphore_wait(barrier, n - 1)

    pieces = x_ref.shape[1]
    own = pltpu.make_async_copy(x_ref.at[me], out_ref.at[me], local_sem)
    own.start()
    copies = []
    for step in range(1, n):
        target = lax.rem(me + step, n)
        for piece in range(pieces):
            copy = pltpu.make_async_remote_copy(
                src_ref=x_ref.at[target, piece],
                dst_ref=out_ref.at[me, piece],
                send_sem=send_sem.at[step, piece],
                recv_sem=recv_sem.at[step, piece],
                device_id=device(target),
                device_id_type=pl.DeviceIdType.MESH,
            )
            copy.start()
            copies.append(copy)
    own.wait()
    for step in range(1, n):
        source = lax.rem(me + n - step, n)
        for piece in range(pieces):
            copies[(step - 1) * pieces + piece].wait_send()
            incoming = pltpu.make_async_remote_copy(
                src_ref=x_ref.at[source, piece],
                dst_ref=out_ref.at[source, piece],
                send_sem=send_sem.at[step, piece],
                recv_sem=recv_sem.at[step, piece],
                device_id=device(source),
                device_id_type=pl.DeviceIdType.MESH,
            )
            incoming.wait_recv()


def exchange(x, axis, other_axis, axis_first, stride, collective):
    n = x.shape[0]
    vmem = pl.BlockSpec(memory_space=pltpu.VMEM)
    return pl.pallas_call(
        functools.partial(exchange_kernel, axis, other_axis, axis_first, stride),
        out_shape=jax.ShapeDtypeStruct(x.shape, x.dtype),
        in_specs=[vmem],
        out_specs=vmem,
        scratch_shapes=[
            pltpu.SemaphoreType.DMA(()),
            pltpu.SemaphoreType.DMA((n, x.shape[1])),
            pltpu.SemaphoreType.DMA((n, x.shape[1])),
        ],
        compiler_params=pltpu.CompilerParams(collective_id=collective, has_side_effects=True),
    )(x)


def local(spectra, pair_blocks, owners):
    groups_count = lax.axis_size("grp")
    chan_count = lax.axis_size("chan")
    slot_count = groups_count * MOST
    pairs = BLK * BLK
    part = F // chan_count
    me = lax.axis_index("chan")

    channels = spectra.shape[0]
    sent = whiten_chunks(spectra, pair_blocks, chan_count)
    got = lax.all_to_all(sent, "chan", split_axis=0, concat_axis=0, tiled=True)
    rows_per = channels * WINDOWS * 2
    group_channels = chan_count * channels
    panel = got
    all_blocks = got[:, rows_per, : NB_SRC * 2].astype(jnp.float32).astype(jnp.int32)
    all_blocks = all_blocks.reshape(chan_count * NB_SRC, 1, 2)
    offsets = jnp.arange(BLK, dtype=jnp.int32)
    left_ch = (all_blocks[:, :, 0] * BLK + offsets[None, :])[:, :, None] + jnp.zeros((1, 1, BLK), jnp.int32)
    right_ch = (all_blocks[:, :, 1] * BLK + offsets[None, :])[:, None, :] + jnp.zeros((1, BLK, 1), jnp.int32)
    channel_ids = jnp.arange(group_channels, dtype=jnp.int32)[None, :]
    left_ch = left_ch.reshape(chan_count, NB_SRC, BLK, BLK).transpose(0, 2, 3, 1)
    right_ch = right_ch.reshape(chan_count, NB_SRC, BLK, BLK).transpose(0, 2, 3, 1)
    both = jnp.stack([left_ch.reshape(-1), right_ch.reshape(-1)])[:, :, None] == channel_ids[None]
    both = both.astype(jnp.bfloat16)
    left_hot, right_hot = both[0], both[1]

    cos_part, sin_part = table_slice(me * part, part)
    corr = pair_exchange(left_hot, right_hot, panel, cos_part, sin_part, chan_count, 0)

    owner_list = owners[0, 0, :, 0]
    same = owner_list[:, None] == owner_list[None, :]
    earlier = jnp.arange(NB_SRC)[None, :] < jnp.arange(NB_SRC)[:, None]
    order_rank = jnp.sum(jnp.logical_and(same, earlier), axis=1)
    slot_ids = owner_list * MOST + order_rank
    chooser = (slot_ids[None, :] == jnp.arange(slot_count, dtype=jnp.int32)[:, None]).astype(jnp.bfloat16)
    placed = jnp.dot(chooser, corr.astype(jnp.bfloat16), preferred_element_type=jnp.float32)
    placed = placed.reshape(groups_count, 1, MOST, pairs, LAGS).astype(jnp.bfloat16)
    received = exchange(placed, "grp", "chan", True, 1, 1).astype(jnp.float32)
    return received.reshape(1, 1, slot_count, pairs, LAGS)


def solution(mesh):
    return jax.shard_map(
        local,
        mesh=mesh,
        in_specs=(
            P(("grp", "chan"), None, None, None),
            P("grp", "chan", None, None),
            P("grp", "chan", None, None),
        ),
        out_specs=P("grp", "chan", None, None, None),
        check_vma=False,
    )
```

```python
import functools

import jax
import jax.numpy as jnp
from jax import lax
from jax.experimental import pallas as pl
from jax.experimental.pallas import tpu as pltpu
from jax.sharding import PartitionSpec as P

F = 8192
LAGS = 1024
BLK = 2
NB_SRC = 18
MOST = 3
WINDOWS = 2
FINE = 128


def phase_angle(bins, lag_index):
    phase = bins[:, None] * lag_index[None, :] % (2 * F)
    return phase.astype(jnp.float32) * (jnp.pi / F)


def table_slice(start, count):
    lag_index = jnp.arange(LAGS, dtype=jnp.int32) - LAGS // 2
    coarse = phase_angle(start + FINE * jnp.arange(count // FINE, dtype=jnp.int32), lag_index)
    fine = phase_angle(jnp.arange(FINE, dtype=jnp.int32), lag_index)
    cos_a, sin_a = jnp.cos(coarse)[:, None, :], jnp.sin(coarse)[:, None, :]
    cos_b, sin_b = jnp.cos(fine)[None, :, :], jnp.sin(fine)[None, :, :]
    cos_ab = (cos_a * cos_b - sin_a * sin_b).reshape(count, LAGS)
    sin_ab = (sin_a * cos_b + cos_a * sin_b).reshape(count, LAGS)
    bins = start + jnp.arange(count, dtype=jnp.int32)
    weight = (jnp.where(bins == 0, 1.0, 2.0).astype(jnp.float32) / jnp.sqrt(jnp.float32(F)))[:, None]
    cos_part = (cos_ab * weight).astype(jnp.bfloat16)
    sin_part = (-sin_ab * weight).astype(jnp.bfloat16)
    return cos_part, sin_part


def whiten_kernel(x_ref, blocks_ref, out_ref):
    x = x_ref[...].astype(jnp.float32)
    rows = x.shape[0]
    square = x * x
    after = pltpu.roll(square, rows - 1, 0)
    before = pltpu.roll(square, 1, 0)
    odd = lax.broadcasted_iota(jnp.int32, x.shape, 0) % 2 == 1
    power = jnp.where(odd, before + square, square + after)
    level = jnp.mean(power, axis=-1, keepdims=True) + 1e-05
    white = (x * lax.rsqrt(power + 0.1 * level)).astype(out_ref.dtype)
    channels = rows // (WINDOWS * 2)
    dest = lax.broadcasted_iota(jnp.int32, (rows, rows), 0)
    source = lax.broadcasted_iota(jnp.int32, (rows, rows), 1)
    order = (source == (dest % channels) * (WINDOWS * 2) + dest // channels).astype(white.dtype)
    white = jnp.dot(order, white, preferred_element_type=jnp.float32).astype(out_ref.dtype)
    part = out_ref.shape[2]
    lane = lax.broadcasted_iota(jnp.int32, (1, part), 1)
    extra = jnp.zeros((1, part), jnp.float32)
    for pair in range(blocks_ref.shape[2]):
        for side in range(2):
            value = blocks_ref[0, 0, pair, side].astype(jnp.float32)
            extra = jnp.where(lane == pair * 2 + side, value, extra)
    extra = extra.astype(out_ref.dtype)
    for chunk in range(out_ref.shape[0]):
        out_ref[chunk, :rows, :] = white[:, chunk * part:(chunk + 1) * part]
        out_ref[chunk, rows:, :] = extra


def whiten_chunks(spectra, pair_blocks, chan_count):
    channels = spectra.shape[0]
    rows = channels * WINDOWS * 2
    x = spectra.reshape(rows, F)
    vmem = pl.BlockSpec(memory_space=pltpu.VMEM)
    return pl.pallas_call(
        whiten_kernel,
        out_shape=jax.ShapeDtypeStruct((chan_count, rows + 1, F // chan_count), jnp.bfloat16),
        in_specs=[vmem, pl.BlockSpec(memory_space=pltpu.SMEM)],
        out_specs=vmem,
        compiler_params=pltpu.CompilerParams(vmem_limit_bytes=48 * 1024 * 1024),
        cost_estimate=pl.CostEstimate(flops=8 * rows * F, transcendentals=rows * F, bytes_accessed=4 * rows * F),
    )(x, pair_blocks)


def pair_rows(left_hot, right_hot, panel, cos_ref, sin_ref, target):
    part = cos_ref.shape[0]
    left = left_hot[target]
    right = right_hot[target]

    sources = panel.shape[0]
    channels = (panel.shape[1] - 1) // (WINDOWS * 2)

    def rows_of(hot, window, kind):
        at = (window * 2 + kind) * channels
        cols = panel[:, at:at + channels, :].reshape(sources * channels, part)
        return jnp.dot(hot, cols, preferred_element_type=jnp.float32)

    real_sum = None
    imag_sum = None
    for window in range(WINDOWS):
        ra = rows_of(left, window, 0)
        ia = rows_of(left, window, 1)
        rb = rows_of(right, window, 0)
        ib = rows_of(right, window, 1)
        real = (ra * rb + ia * ib).astype(jnp.bfloat16).astype(jnp.float32)
        imag = (ia * rb - ra * ib).astype(jnp.bfloat16).astype(jnp.float32)
        real_sum = real if real_sum is None else real_sum + real
        imag_sum = imag if imag_sum is None else imag_sum + imag
    real_stack = (real_sum / WINDOWS).astype(jnp.bfloat16)
    imag_stack = (imag_sum / WINDOWS).astype(jnp.bfloat16)
    total = jnp.dot(real_stack, cos_ref[...], preferred_element_type=jnp.float32)
    return total + jnp.dot(imag_stack, sin_ref[...], preferred_element_type=jnp.float32)


def pair_exchange_kernel(left_hot, right_hot, panel, cos_ref, sin_ref, out_ref, slots, received, local_sem,
                         send_sem, recv_sem):
    n = slots.shape[0]
    me = lax.axis_index("chan")
    group = lax.axis_index("grp")

    barrier = pltpu.get_barrier_semaphore()
    for step in range(1, n):
        pl.semaphore_signal(barrier, inc=1, device_id=(group, lax.rem(me + step, n)),
                            device_id_type=pl.DeviceIdType.MESH)
    pl.semaphore_wait(barrier, n - 1)

    def fill(target):
        slots[target] = pair_rows(left_hot, right_hot, panel, cos_ref, sin_ref, target).astype(slots.dtype)

    def send(step):
        target = lax.rem(me + step, n)
        return pltpu.make_async_remote_copy(
            src_ref=slots.at[target],
            dst_ref=received.at[me],
            send_sem=send_sem.at[step],
            recv_sem=recv_sem.at[step],
            device_id=(group, target),
            device_id_type=pl.DeviceIdType.MESH,
        )

    def one_step(step, carry):
        fill(lax.rem(me + step, n))

        @pl.when(step > 1)
        def _():
            send(step - 1).start()

        return carry

    lax.fori_loop(1, n, one_step, 0)
    fill(me)
    send(n - 1).start()
    own = pltpu.make_async_copy(slots.at[me], received.at[me], local_sem)
    own.start()
    own.wait()

    def finish(step, carry):
        send(step).wait_send()
        source = lax.rem(me + n - step, n)
        pltpu.make_async_remote_copy(
            src_ref=slots.at[source],
            dst_ref=received.at[source],
            send_sem=send_sem.at[step],
            recv_sem=recv_sem.at[step],
            device_id=(group, source),
            device_id_type=pl.DeviceIdType.MESH,
        ).wait_recv()
        return carry

    lax.fori_loop(1, n, finish, 0)
    total = received[0].astype(jnp.float32)
    for source in range(1, n):
        total = total + received[source].astype(jnp.float32)
    listed = out_ref.shape[0]
    lags = cos_ref.shape[1]
    for pq in range(total.shape[0] // listed):
        out_ref[:, pq * lags:(pq + 1) * lags] = total[pq * listed:(pq + 1) * listed]


def pair_exchange(left_hot, right_hot, panel, cos_part, sin_part, chan_count, collective):
    rows = left_hot.shape[0]
    count = rows // chan_count
    left_hot = left_hot.reshape(chan_count, count, -1)
    right_hot = right_hot.reshape(chan_count, count, -1)
    part = cos_part.shape[0]
    pairs = BLK * BLK
    vmem = pl.BlockSpec(memory_space=pltpu.VMEM)
    flops = 2 * 2 * rows * panel.size + 2 * 2 * rows * part * LAGS
    return pl.pallas_call(
        pair_exchange_kernel,
        out_shape=jax.ShapeDtypeStruct((count // pairs, pairs * LAGS), jnp.float32),
        in_specs=[vmem] * 5,
        out_specs=vmem,
        scratch_shapes=[
            pltpu.VMEM((chan_count, count, LAGS), jnp.bfloat16),
            pltpu.VMEM((chan_count, count, LAGS), jnp.bfloat16),
            pltpu.SemaphoreType.DMA(()),
            pltpu.SemaphoreType.DMA((chan_count,)),
            pltpu.SemaphoreType.DMA((chan_count,)),
        ],
        compiler_params=pltpu.CompilerParams(
            collective_id=collective, has_side_effects=True, vmem_limit_bytes=56 * 1024 * 1024
        ),
        cost_estimate=pl.CostEstimate(
            flops=flops,
            transcendentals=0,
            bytes_accessed=panel.size * 2 + 4 * part * LAGS + rows * LAGS * 2,
        ),
    )(left_hot, right_hot, panel, cos_part, sin_part)


def exchange_kernel(axis, other_axis, axis_first, stride, x_ref, out_ref, local_sem, send_sem, recv_sem):
    n = x_ref.shape[0]
    index = lax.axis_index(axis)
    me = lax.rem(index // stride, n)
    base = index - me * stride
    other = lax.axis_index(other_axis)

    def device(j):
        coord = base + stride * j
        return (coord, other) if axis_first else (other, coord)

    barrier = pltpu.get_barrier_semaphore()
    for step in range(1, n):
        pl.semaphore_signal(barrier, inc=1, device_id=device(lax.rem(me + step, n)),
                            device_id_type=pl.DeviceIdType.MESH)
    pl.semaphore_wait(barrier, n - 1)

    pieces = x_ref.shape[1]
    own = pltpu.make_async_copy(x_ref.at[me], out_ref.at[me], local_sem)
    own.start()
    copies = []
    for step in range(1, n):
        target = lax.rem(me + step, n)
        for piece in range(pieces):
            copy = pltpu.make_async_remote_copy(
                src_ref=x_ref.at[target, piece],
                dst_ref=out_ref.at[me, piece],
                send_sem=send_sem.at[step, piece],
                recv_sem=recv_sem.at[step, piece],
                device_id=device(target),
                device_id_type=pl.DeviceIdType.MESH,
            )
            copy.start()
            copies.append(copy)
    own.wait()
    for step in range(1, n):
        source = lax.rem(me + n - step, n)
        for piece in range(pieces):
            copies[(step - 1) * pieces + piece].wait_send()
            incoming = pltpu.make_async_remote_copy(
                src_ref=x_ref.at[source, piece],
                dst_ref=out_ref.at[source, piece],
                send_sem=send_sem.at[step, piece],
                recv_sem=recv_sem.at[step, piece],
                device_id=device(source),
                device_id_type=pl.DeviceIdType.MESH,
            )
            incoming.wait_recv()


def exchange(x, axis, other_axis, axis_first, stride, collective):
    n = x.shape[0]
    anywhere = pl.BlockSpec(memory_space=pl.ANY)
    return pl.pallas_call(
        functools.partial(exchange_kernel, axis, other_axis, axis_first, stride),
        out_shape=jax.ShapeDtypeStruct(x.shape, x.dtype),
        in_specs=[anywhere],
        out_specs=anywhere,
        scratch_shapes=[
            pltpu.SemaphoreType.DMA(()),
            pltpu.SemaphoreType.DMA((n, x.shape[1])),
            pltpu.SemaphoreType.DMA((n, x.shape[1])),
        ],
        compiler_params=pltpu.CompilerParams(collective_id=collective, has_side_effects=True),
    )(x)


def local(spectra, pair_blocks, owners):
    groups_count = lax.axis_size("grp")
    chan_count = lax.axis_size("chan")
    slot_count = groups_count * MOST
    pairs = BLK * BLK
    part = F // chan_count
    me = lax.axis_index("chan")

    channels = spectra.shape[0]
    sent = whiten_chunks(spectra, pair_blocks, chan_count)
    got = lax.all_to_all(sent, "chan", split_axis=0, concat_axis=0, tiled=True)
    rows_per = channels * WINDOWS * 2
    group_channels = chan_count * channels
    panel = got
    all_blocks = got[:, rows_per, : NB_SRC * 2].astype(jnp.float32).astype(jnp.int32)
    all_blocks = all_blocks.reshape(chan_count * NB_SRC, 1, 2)
    offsets = jnp.arange(BLK, dtype=jnp.int32)
    left_ch = (all_blocks[:, :, 0] * BLK + offsets[None, :])[:, :, None] + jnp.zeros((1, 1, BLK), jnp.int32)
    right_ch = (all_blocks[:, :, 1] * BLK + offsets[None, :])[:, None, :] + jnp.zeros((1, BLK, 1), jnp.int32)
    channel_ids = jnp.arange(group_channels, dtype=jnp.int32)[None, :]
    left_ch = left_ch.reshape(chan_count, NB_SRC, BLK, BLK).transpose(0, 2, 3, 1)
    right_ch = right_ch.reshape(chan_count, NB_SRC, BLK, BLK).transpose(0, 2, 3, 1)
    left_hot = (left_ch.reshape(-1, 1) == channel_ids).astype(jnp.bfloat16)
    right_hot = (right_ch.reshape(-1, 1) == channel_ids).astype(jnp.bfloat16)

    cos_part, sin_part = table_slice(me * part, part)
    corr = pair_exchange(left_hot, right_hot, panel, cos_part, sin_part, chan_count, 0)

    owner_list = owners[0, 0, :, 0]
    same = owner_list[:, None] == owner_list[None, :]
    earlier = jnp.arange(NB_SRC)[None, :] < jnp.arange(NB_SRC)[:, None]
    order_rank = jnp.sum(jnp.logical_and(same, earlier), axis=1)
    slot_ids = owner_list * MOST + order_rank
    chooser = (slot_ids[None, :] == jnp.arange(slot_count, dtype=jnp.int32)[:, None]).astype(jnp.bfloat16)
    placed = jnp.dot(chooser, corr.astype(jnp.bfloat16), preferred_element_type=jnp.float32)
    placed = placed.reshape(groups_count, 1, MOST, pairs, LAGS).astype(jnp.bfloat16)
    received = exchange(placed, "grp", "chan", True, 1, 1).astype(jnp.float32)
    return received.reshape(1, 1, slot_count, pairs, LAGS)


def solution(mesh):
    return jax.shard_map(
        local,
        mesh=mesh,
        in_specs=(
            P(("grp", "chan"), None, None, None),
            P("grp", "chan", None, None),
            P("grp", "chan", None, None),
        ),
        out_specs=P("grp", "chan", None, None, None),
        check_vma=False,
    )
```
